128 devices in a mesh: rows: 8 (over x, z_lo), cols: 16 (over y, z_hi, core).
Axes of the slice: x: 4, y: 4, z: 4 (z_hi: 2, z_lo: 2; z = z_hi * 2 + z_lo), core: 2. Of those that a mesh axis runs over, the one named last changes fastest.
Arguments:
- object_tiles: float32 [2, 2, 6144, 12288], P(None, None, 'rows', 'cols'), may hold values from -6 to 6
- probe: float32 [2, 512, 512], replicated, may hold values from -6 to 6
- prop_phase: float32 [512, 512], replicated, may hold values from -3.140625 to 3.140625
- amplitudes: bfloat16 [8, 16, 1, 512, 512], P('rows', 'cols'), may hold values from 0 to 2
- offsets: int32 [8, 16, 1, 2], P('rows', 'cols'), may hold values from 0 to 512
- counts: int32 [8, 16], P('rows', 'cols'), may hold values from 0 to 1
- step_size: float32 [2], replicated, may hold values from 0.3 to 1
Outputs:
- updated: float32 [2, 2, 6144, 12288], P(None, None, 'rows', 'cols')
The draws below stay inside these ranges and needn't reach their ends.
Inputs may be any that keep to these rules, and one draw needn't show every extreme that they name: `offsets`: row and column of a window's first cell in the device's tile extended by 128 cells on every side. `counts`: slots at or past a tile's count are ignored; a tile may have no probe position.
All inputs are finite; a program needn't handle non-finite values.
Results may differ from the reference program's by a relative error of at most 0.013.
The reference program's roundings to bfloat16 on the way count: a program that leaves them out, or rounds other values in their place, can miss the bound.
Values sent between devices are 32-bit elements; how exact they have to be, the bound alone decides.
No kernel may reach another device: no remote copies, remote signals or barrier semaphores. Data moves between devices by JAX's collectives and lax.ppermute only.
A program may use at most 192 MiB of HBM per device.

```python
import math
import jax
import jax.numpy as jnp
from jax import lax

P_SIZE = 512
H = 128
TILE = 768
MAXP = 1
TROWS = 8
TCOLS = 16
NR = 6144
NC = 12288


def with_ends(entries, own_key, smallest, largest):
    extent = entries.shape
    place = [jax.random.randint(jax.random.fold_in(own_key, axis), (), 0, extent[axis]) for axis in range(len(extent))]
    entries = entries.at[tuple(place)].set(smallest)
    longest = extent.index(max(extent))
    place[longest] = (place[longest] + 1) % extent[longest]
    return entries.at[tuple(place)].set(largest)


def block_scale(stream_key, shape, cuts, least, top_value):
    loudness, own = 1.0, jax.random.fold_in(stream_key, 6)
    for dim, shards_of in cuts:
        draws = jnp.exp(jax.random.uniform(jax.random.fold_in(own, dim), (shards_of,), jnp.float32, least / len(cuts), top_value / len(cuts)))
        loudness = loudness * jnp.repeat(draws, shape[dim] // shards_of).reshape([-1 if axis == dim else 1 for axis in range(len(shape))])
    return loudness


def scatter_about(stream_key, dims, spread, reach, shards=(), kind=jnp.bfloat16):
    loudness = block_scale(stream_key, dims, shards, -0.22, 0.18) if shards else 1.0
    entries = jax.random.normal(stream_key, dims, jnp.float32) * spread * loudness
    return jnp.minimum(jnp.maximum(entries, -reach), reach).astype(kind)


def setup_inputs(seed: int = 0) -> dict:
    streams_of = jax.random.split(jax.random.key(seed), 8)
    object_tiles = scatter_about(streams_of[0], (2, 2, NR, NC), 1.0, 6.0, ((2, 8), (3, 16)), jnp.float32)
    probe = scatter_about(streams_of[1], (2, P_SIZE, P_SIZE), 1.0, 6.0, (), jnp.float32)
    prop_phase = jnp.clip(jax.random.uniform(streams_of[2], (P_SIZE, P_SIZE), jnp.float32, -3.140625, 3.140625), -3.140625, 3.140625)
    amplitudes = jnp.clip(2.0 * jax.random.uniform(streams_of[3], (TROWS, TCOLS, MAXP, P_SIZE, P_SIZE), jnp.float32) ** block_scale(streams_of[3], (TROWS, TCOLS, MAXP, P_SIZE, P_SIZE), ((0, 8), (1, 16)), -0.2, 0.2), 0.0, 2.0).astype(jnp.bfloat16)
    offsets = with_ends(jax.random.randint(streams_of[4], (TROWS, TCOLS, MAXP, 2), 0, TILE + 2 * H - P_SIZE + 1), jax.random.fold_in(streams_of[4], 1), 0, TILE + 2 * H - P_SIZE).astype(jnp.int32)
    counts = with_ends(jax.random.randint(streams_of[5], (TROWS, TCOLS), 0, MAXP + 1), jax.random.fold_in(streams_of[5], 1), 0, MAXP).astype(jnp.int32)
    step_size = jnp.clip(jnp.exp(jax.random.uniform(streams_of[6], (2,), jnp.float32, math.log(0.3), math.log(1.0))), 0.3, 1.0)
    return {"object_tiles": object_tiles, "probe": probe, "prop_phase": prop_phase, "amplitudes": amplitudes, "offsets": offsets, "counts": counts, "step_size": step_size}


def dft_tables(length, inverse):
    index = jnp.arange(length, dtype=jnp.int32)
    product = index[:, None] * index[None, :] % length
    angles = product.astype(jnp.float32) * (2.0 * math.pi / length)
    scaling = 1.0 / math.sqrt(length)
    direction = 1.0 if inverse else -1.0
    return ((jnp.cos(angles) * scaling).astype(jnp.bfloat16), (direction * jnp.sin(angles) * scaling).astype(jnp.bfloat16))

def transform(real_part, imag_part, tables):
    table_re, table_im = tables
    left_re = real_part.astype(jnp.bfloat16)
    left_im = imag_part.astype(jnp.bfloat16)
    mid_re = jnp.dot(table_re, left_re, preferred_element_type=jnp.float32) - jnp.dot(table_im, left_im, preferred_element_type=jnp.float32)
    mid_im = jnp.dot(table_re, left_im, preferred_element_type=jnp.float32) + jnp.dot(table_im, left_re, preferred_element_type=jnp.float32)
    mid_re = mid_re.astype(jnp.bfloat16)
    mid_im = mid_im.astype(jnp.bfloat16)
    out_re = jnp.dot(mid_re, table_re, preferred_element_type=jnp.float32) - jnp.dot(mid_im, table_im, preferred_element_type=jnp.float32)
    out_im = jnp.dot(mid_re, table_im, preferred_element_type=jnp.float32) + jnp.dot(mid_im, table_re, preferred_element_type=jnp.float32)
    return (out_re, out_im)

def probe_gradient(window, probe, kernel_re, kernel_im, measured, forward, backward):
    first_re, first_im = (window[0, 0], window[0, 1])
    second_re, second_im = (window[1, 0], window[1, 1])
    probe_re, probe_im = (probe[0], probe[1])
    wave_re = probe_re * first_re - probe_im * first_im
    wave_im = probe_re * first_im + probe_im * first_re
    spec_re, spec_im = transform(wave_re, wave_im, forward)
    prop_re = spec_re * kernel_re - spec_im * kernel_im
    prop_im = spec_re * kernel_im + spec_im * kernel_re
    psi1_re, psi1_im = transform(prop_re, prop_im, backward)
    exit_re = psi1_re * second_re - psi1_im * second_im
    exit_im = psi1_re * second_im + psi1_im * second_re
    far_re, far_im = transform(exit_re, exit_im, forward)
    magnitude = jnp.sqrt(far_re * far_re + far_im * far_im + 1.0)
    factor = 1.0 - measured.astype(jnp.float32) / magnitude
    chi2_re, chi2_im = transform(far_re * factor, far_im * factor, backward)
    grad2_re = psi1_re * chi2_re + psi1_im * chi2_im
    grad2_im = psi1_re * chi2_im - psi1_im * chi2_re
    back_re = second_re * chi2_re + second_im * chi2_im
    back_im = second_re * chi2_im - second_im * chi2_re
    bspec_re, bspec_im = transform(back_re, back_im, forward)
    bprop_re = bspec_re * kernel_re + bspec_im * kernel_im
    bprop_im = bspec_im * kernel_re - bspec_re * kernel_im
    dwave_re, dwave_im = transform(bprop_re, bprop_im, backward)
    grad1_re = probe_re * dwave_re + probe_im * dwave_im
    grad1_im = probe_re * dwave_im - probe_im * dwave_re
    return jnp.stack([jnp.stack([grad1_re, grad1_im]), jnp.stack([grad2_re, grad2_im])])

def reference(object_tiles, probe, prop_phase, amplitudes, offsets, counts, step_size):
    padded = jnp.pad(object_tiles, ((0, 0), (0, 0), (H, H), (H, H)))
    forward = dft_tables(P_SIZE, False)
    backward = dft_tables(P_SIZE, True)
    kernel_re = jnp.cos(prop_phase)
    kernel_im = jnp.sin(prop_phase)
    zero = jnp.int32(0)
    total = TROWS * TCOLS * MAXP

    def visit(grad, index):
        tile_row = (index // (TCOLS * MAXP)).astype(jnp.int32)
        tile_col = (index // MAXP % TCOLS).astype(jnp.int32)
        slot = (index % MAXP).astype(jnp.int32)
        start_row = (tile_row * TILE + offsets[tile_row, tile_col, slot, 0]).astype(jnp.int32)
        start_col = (tile_col * TILE + offsets[tile_row, tile_col, slot, 1]).astype(jnp.int32)
        corner = (zero, zero, start_row, start_col)

        def compute(unused):
            window = lax.dynamic_slice(padded, corner, (2, 2, P_SIZE, P_SIZE))
            return probe_gradient(window, probe, kernel_re, kernel_im, amplitudes[tile_row, tile_col, slot], forward, backward)

        def nothing(unused):
            return jnp.zeros((2, 2, P_SIZE, P_SIZE), jnp.float32)
        contribution = lax.cond(slot < counts[tile_row, tile_col], compute, nothing, 0)
        current = lax.dynamic_slice(grad, corner, (2, 2, P_SIZE, P_SIZE))
        return (lax.dynamic_update_slice(grad, current + contribution, corner), None)
    grad, unused = lax.scan(visit, jnp.zeros(padded.shape, jnp.float32), jnp.arange(total, dtype=jnp.int32))
    grad = grad[:, :, H:H + NR, H:H + NC]
    return object_tiles - step_size[:, None, None, None] * grad
```

```python
import math

import jax
import jax.numpy as jnp
from jax import lax
from jax.experimental import pallas as pl
from jax.experimental.pallas import tpu as pltpu
from jax.sharding import PartitionSpec as P

H = 128
W = 512
T = 768
B = 128
HALF = W // 2
LAST = T // H - 1
R0, C0, PR0, PC0, FR0, FC0, LIVE, ODD = range(8)

F32, BF16 = jnp.float32, jnp.bfloat16


def rows_below(shape, first, limit):
    return lax.broadcasted_iota(jnp.int32, shape, 0) + first < limit


def cols_below(shape, first, limit):
    return lax.broadcasted_iota(jnp.int32, shape, 1) + first < limit


def params(limit_mib=None):
    if limit_mib is None:
        return pltpu.CompilerParams(dimension_semantics=("arbitrary",))
    return pltpu.CompilerParams(vmem_limit_bytes=limit_mib << 20)


def vmem():
    return pl.BlockSpec(memory_space=pltpu.VMEM)


def smem():
    return pl.BlockSpec(memory_space=pltpu.SMEM)


def prep_kernel(meta, probe, la, lai, rb, rbi, q):
    def table(rows, first_row, row_shift, col_shift):
        p = (lax.broadcasted_iota(jnp.int32, (rows, W), 0) + (first_row - row_shift)) & (W - 1)
        k = (lax.broadcasted_iota(jnp.int32, (rows, W), 1) - col_shift) & (W - 1)
        m = (p * k) & (W - 1)
        quadrant = (m + W // 8) >> 7
        x = (m - quadrant * (W // 4)).astype(F32) * (2.0 * math.pi / W)
        y = x * x
        s = x * (1.0 + y * (-1.0 / 6 + y * (1.0 / 120 + y * (-1.0 / 5040 + y * (1.0 / 362880)))))
        c = 1.0 + y * (-0.5 + y * (1.0 / 24 + y * (-1.0 / 720 + y * (1.0 / 40320 - y * (1.0 / 3628800)))))
        swap = (quadrant & 1) == 1
        cos = jnp.where(swap, s, c)
        sin = jnp.where(swap, c, s)
        cos = jnp.where(((quadrant + 1) & 2) == 2, -cos, cos)
        sin = jnp.where((quadrant & 2) == 2, -sin, sin)
        scaling = 1.0 / math.sqrt(W)
        return (cos * scaling).astype(BF16), (-sin * scaling).astype(BF16)

    r0, c0 = meta[R0], meta[C0]
    for first in range(0, W, B):
        rows = pl.ds(first, B)
        later = pl.ds(W + first, B)
        la[rows, :W], la[rows, W:] = table(B, first, 0, r0)
        lai[rows, :W], lai[rows, W:] = table(B, first, r0, 0)
        rb[rows, :], rb[later, :] = table(B, first, c0, 0)
        rbi[rows, :], rbi[later, :] = table(B, first, 0, c0)
    for part in range(2):
        q[part] = pltpu.roll(pltpu.roll(probe[part], r0 & (W - 1), 0), c0 & (W - 1), 1)


def prepare(meta, probe):
    return pl.pallas_call(
        prep_kernel,
        out_shape=[
            jax.ShapeDtypeStruct((W, 2 * W), BF16),
            jax.ShapeDtypeStruct((W, 2 * W), BF16),
            jax.ShapeDtypeStruct((2 * W, W), BF16),
            jax.ShapeDtypeStruct((2 * W, W), BF16),
            jax.ShapeDtypeStruct((2, W, W), F32),
        ],
        in_specs=[smem(), vmem()],
        out_specs=[vmem()] * 5,
        compiler_params=params(32),
        name="prepare",
    )(meta, probe)


def pack(tile, left, right, c0):
    shape = (tile.shape[0], H)
    middle = (tile.shape[0], W - 2 * H)
    a = jnp.where(cols_below(shape, 0, c0), tile[:, W - H : W], left)
    b = jnp.where(cols_below(middle, H, c0), tile[:, W:], tile[:, : W - 2 * H])
    c = jnp.where(cols_below(shape, W - H, c0), right, tile[:, W - 2 * H : W - H])
    return a, b, c


def put(out, rows, pieces):
    a, b, c = pieces
    out[rows, :H] = a
    out[rows, H : W - H] = b
    out[rows, W - H :] = c


def use_own(meta):
    upper = (meta[PR0] < HALF).astype(jnp.int32)
    return upper + meta[ODD] == 1


def far_kernel(meta, tile, left, right, out):
    put(out, slice(None), pack(tile[...], left[...], right[...], meta[FC0]))


def mate_kernel(meta, tile, left, right, passing, out):
    own = use_own(meta)

    @pl.when(own)
    def _():
        put(out, slice(None), pack(tile[...], left[...], right[...], meta[PC0]))

    @pl.when(jnp.logical_not(own))
    def _():
        out[...] = passing[...]


def far_strip(s, meta, obj, left, right):
    edge = lambda i, m: (i, m[ODD] * LAST, 0)
    return pl.pallas_call(
        far_kernel,
        out_shape=jax.ShapeDtypeStruct((2, H, W), F32),
        grid_spec=pltpu.PrefetchScalarGridSpec(
            num_scalar_prefetch=1,
            grid=(2,),
            in_specs=[
                pl.BlockSpec((None, None, H, T), lambda i, m: (s, i, m[ODD] * LAST, 0)),
                pl.BlockSpec((None, H, H), edge),
                pl.BlockSpec((None, H, H), edge),
            ],
            out_specs=pl.BlockSpec((None, H, W), lambda i, m: (i, 0, 0)),
        ),
        compiler_params=params(),
        name="far_strip",
    )(meta, obj, left, right)


def mate_strip(s, meta, obj, left, right, passing):
    edge = lambda i, m: (i, (1 - m[ODD]) * LAST, 0)
    return pl.pallas_call(
        mate_kernel,
        out_shape=jax.ShapeDtypeStruct((2, H, W), F32),
        grid_spec=pltpu.PrefetchScalarGridSpec(
            num_scalar_prefetch=1,
            grid=(2,),
            in_specs=[
                pl.BlockSpec((None, None, H, T), lambda i, m: (s, i, (1 - m[ODD]) * LAST, 0)),
                pl.BlockSpec((None, H, H), edge),
                pl.BlockSpec((None, H, H), edge),
                pl.BlockSpec((None, H, W), lambda i, m: (i, 0, 0)),
            ],
            out_specs=pl.BlockSpec((None, H, W), lambda i, m: (i, 0, 0)),
        ),
        compiler_params=params(),
        name="mate_strip",
    )(meta, obj, left, right, passing)


def local_kernel(meta, tile, left, right, out):
    r0, c0 = meta[R0], meta[C0]

    def packed(first):
        rows = pl.ds(first, B)
        return pack(tile[rows, :], left[rows, :], right[rows, :], c0)

    put(out, pl.ds(0, B), packed(W - H))
    for first in range(B, W - B, B):
        low, high = packed(first - H), packed(first + W - H)
        put(
            out,
            pl.ds(first, B),
            [jnp.where(rows_below(x.shape, first, r0), y, x) for x, y in zip(low, high)],
        )
    put(out, pl.ds(W - B, B), packed(W - B - H))


def local_window(s, meta, obj, left, right):
    return pl.pallas_call(
        local_kernel,
        out_shape=jax.ShapeDtypeStruct((2, W, W), F32),
        grid_spec=pltpu.PrefetchScalarGridSpec(
            num_scalar_prefetch=1,
            grid=(2,),
            in_specs=[
                pl.BlockSpec((None, None, T, T), lambda i, m: (s, i, 0, 0)),
                pl.BlockSpec((None, T, H), lambda i, m: (i, 0, 0)),
                pl.BlockSpec((None, T, H), lambda i, m: (i, 0, 0)),
            ],
            out_specs=pl.BlockSpec((None, W, W), lambda i, m: (i, 0, 0)),
        ),
        compiler_params=params(),
        name="local_window",
    )(meta, obj, left, right)


def window_rows(meta, local, strip, part, first):
    x = local[part, pl.ds(first, B), :]
    if first == 0:
        x = jnp.where(rows_below(x.shape, first, meta[R0]), x, strip[part])
    if first == W - B:
        x = jnp.where(rows_below(x.shape, first, meta[R0]), strip[part], x)
    return x


def put_left(v4, first, re, im, inverse):
    re, im = re.astype(BF16), im.astype(BF16)
    rows, later = pl.ds(first, B), pl.ds(W + first, B)
    v4[rows, :W] = re
    v4[rows, W:] = im
    v4[later, :W] = im if inverse else -im
    v4[later, W:] = -re if inverse else re


def left_product(table, v4, m4, inverse):
    for first in range(0, W, B):
        rows, later = pl.ds(first, B), pl.ds(W + first, B)
        mid = jnp.dot(table[rows, :], v4[...], preferred_element_type=F32).astype(BF16)
        re, im = mid[:, :W], mid[:, W:]
        m4[rows, :W] = re
        m4[rows, W:] = im if inverse else -im
        m4[later, :W] = im
        m4[later, W:] = -re if inverse else re


def right_product(m4, table, first):
    re = jnp.dot(m4[pl.ds(first, B), :], table[...], preferred_element_type=F32)
    im = jnp.dot(m4[pl.ds(W + first, B), :], table[...], preferred_element_type=F32)
    return re, im


def first_kernel(meta, local, strip, q, kern, la, lai, rb, rbi, psi, v4, m4):
    for first in range(0, W, B):
        rows = pl.ds(first, B)
        o_re = window_rows(meta, local, strip, 0, first)
        o_im = window_rows(meta, local, strip, 1, first)
        q_re, q_im = q[0, rows, :], q[1, rows, :]
        put_left(v4, first, q_re * o_re - q_im * o_im, q_re * o_im + q_im * o_re, False)
    left_product(la, v4, m4, False)
    for first in range(0, W, B):
        rows = pl.ds(first, B)
        re, im = right_product(m4, rb, first)
        k_re, k_im = kern[0, rows, :], kern[1, rows, :]
        put_left(v4, first, re * k_re - im * k_im, re * k_im + im * k_re, True)
    left_product(lai, v4, m4, True)
    for first in range(0, W, B):
        rows = pl.ds(first, B)
        psi[0, rows, :], psi[1, rows, :] = right_product(m4, rbi, first)


def edge_rows(meta, g, zg):
    keep_first = meta[R0] < HALF
    live = meta[LIVE] > 0

    @pl.when(keep_first)
    def _():
        for part in range(2):
            x = g[part, :H, :]
            hide = rows_below(x.shape, 0, meta[R0])
            zg[part] = jnp.where(jnp.logical_and(live, jnp.logical_not(hide)), x, 0.0)

    @pl.when(jnp.logical_not(keep_first))
    def _():
        for part in range(2):
            x = g[part, W - H :, :]
            show = rows_below(x.shape, W - H, meta[R0])
            zg[part] = jnp.where(jnp.logical_and(live, show), x, 0.0)


def second_kernel(meta, local, strip, psi, amp, la, lai, rb, rbi, g2, back, zg, v4, m4):
    for first in range(0, W, B):
        rows = pl.ds(first, B)
        o_re = window_rows(meta, local, strip, 0, first)
        o_im = window_rows(meta, local, strip, 1, first)
        p_re, p_im = psi[0, rows, :], psi[1, rows, :]
        put_left(v4, first, p_re * o_re - p_im * o_im, p_re * o_im + p_im * o_re, False)
    left_product(la, v4, m4, False)
    for first in range(0, W, B):
        rows = pl.ds(first, B)
        re, im = right_product(m4, rb, first)
        factor = 1.0 - amp[rows, :].astype(F32) / jnp.sqrt(re * re + im * im + 1.0)
        put_left(v4, first, re * factor, im * factor, True)
    left_product(lai, v4, m4, True)
    for first in range(0, W, B):
        rows = pl.ds(first, B)
        re, im = right_product(m4, rbi, first)
        p_re, p_im = psi[0, rows, :], psi[1, rows, :]
        g2[0, rows, :] = p_re * re + p_im * im
        g2[1, rows, :] = p_re * im - p_im * re
        o_re = window_rows(meta, local, strip, 0, first)
        o_im = window_rows(meta, local, strip, 1, first)
        back[0, rows, :] = (o_re * re + o_im * im).astype(BF16)
        back[1, rows, :] = (o_re * im - o_im * re).astype(BF16)
    edge_rows(meta, g2, zg)


def third_kernel(meta, back, q, kern, la, lai, rb, rbi, g1, zg, v4, m4):
    for first in range(0, W, B):
        rows = pl.ds(first, B)
        put_left(v4, first, back[0, rows, :], back[1, rows, :], False)
    left_product(la, v4, m4, False)
    for first in range(0, W, B):
        rows = pl.ds(first, B)
        re, im = right_product(m4, rb, first)
        k_re, k_im = kern[0, rows, :], kern[1, rows, :]
        put_left(v4, first, re * k_re + im * k_im, im * k_re - re * k_im, True)
    left_product(lai, v4, m4, True)
    for first in range(0, W, B):
        rows = pl.ds(first, B)
        re, im = right_product(m4, rbi, first)
        q_re, q_im = q[0, rows, :], q[1, rows, :]
        g1[0, rows, :] = q_re * re + q_im * im
        g1[1, rows, :] = q_re * im - q_im * re
    edge_rows(meta, g1, zg)


WINDOW = jax.ShapeDtypeStruct((2, W, W), F32)
STRIP = jax.ShapeDtypeStruct((2, H, W), F32)


def transforms(kernel, name, out_shape, meta, *operands):
    return pl.pallas_call(
        kernel,
        out_shape=out_shape,
        in_specs=[smem()] + [vmem()] * len(operands),
        out_specs=[vmem()] * len(out_shape),
        scratch_shapes=[pltpu.VMEM((2 * W, 2 * W), BF16), pltpu.VMEM((2 * W, 2 * W), BF16)],
        compiler_params=params(44),
        name=name,
    )(meta, *operands)


def shares(meta, own, mate, far):
    odd = meta[ODD] > 0
    take = use_own(meta)
    mate = jnp.where(take, mate, 0.0)
    top = jnp.where(odd, mate, far)
    bottom = jnp.where(odd, far, mate)
    c_top = jnp.where(odd, meta[PC0], meta[FC0])
    c_bottom = jnp.where(odd, meta[FC0], meta[PC0])
    return (top, c_top), (bottom, c_bottom)


def left_part(x, c0):
    x = x[:, :H]
    return jnp.where(cols_below(x.shape, 0, c0), 0.0, x)


def right_part(x, c0):
    x = x[:, W - H :]
    return jnp.where(cols_below(x.shape, W - H, c0), x, 0.0)


def inner_parts(x, c0):
    low, high = x[:, H:], x[:, : W - H]
    low = jnp.where(cols_below(low.shape, H, c0), 0.0, low)
    high = jnp.where(cols_below(high.shape, 0, c0), high, 0.0)
    return low, high


def tile_rows(meta, g, first):
    live = meta[LIVE] > 0
    if first < W - H:
        x = g[pl.ds(first + H, B), :]
        hide = rows_below(x.shape, first + H, meta[R0])
        return jnp.where(jnp.logical_and(live, jnp.logical_not(hide)), x, 0.0)
    x = g[pl.ds(first - (W - H), B), :]
    show = rows_below(x.shape, first - (W - H), meta[R0])
    return jnp.where(jnp.logical_and(live, show), x, 0.0)


def sides_kernel(meta, g, mate, far, to_left, to_right):
    top, bottom = shares(meta, g, mate[...], far[...])
    for first in range(0, T, B):
        x = tile_rows(meta, g, first)
        a, b = left_part(x, meta[C0]), right_part(x, meta[C0])
        if first == 0:
            a, b = a + left_part(*top), b + right_part(*top)
        if first == T - B:
            a, b = a + left_part(*bottom), b + right_part(*bottom)
        to_left[pl.ds(first, B), :] = a
        to_right[pl.ds(first, B), :] = b


def sides(meta, g, mate, far):
    whole = lambda i, m: (i, 0, 0)
    return pl.pallas_call(
        sides_kernel,
        out_shape=[jax.ShapeDtypeStruct((2, T, H), F32)] * 2,
        grid_spec=pltpu.PrefetchScalarGridSpec(
            num_scalar_prefetch=1,
            grid=(2,),
            in_specs=[
                pl.BlockSpec((None, W, W), whole),
                pl.BlockSpec((None, H, W), whole),
                pl.BlockSpec((None, H, W), whole),
            ],
            out_specs=[pl.BlockSpec((None, T, H), whole)] * 2,
        ),
        compiler_params=params(),
        name="sides",
    )(meta, g, mate, far)


def inner_kernel(s, meta, step, obj, g, mate, far, *rest):
    out = rest[-1]
    top, bottom = shares(meta, g, mate[...], far[...])
    size = step[s]
    for first in range(0, T, B):
        rows = pl.ds(first, B)
        low, high = inner_parts(tile_rows(meta, g, first), meta[C0])
        if first in (0, T - B):
            more = inner_parts(*(top if first == 0 else bottom))
            low, high = low + more[0], high + more[1]
        out[rows, : W - H] = obj[rows, : W - H] - size * low
        out[rows, W - H :] = obj[rows, W - H :] - size * high


def inner(s, meta, step, obj, g, mate, far, before):
    whole = lambda i, m, z: (i, 0, 0)
    tile = pl.BlockSpec((None, None, T, T), lambda i, m, z: (s, i, 0, 0))
    return pl.pallas_call(
        lambda *refs: inner_kernel(s, *refs),
        out_shape=jax.ShapeDtypeStruct(obj.shape, F32),
        grid_spec=pltpu.PrefetchScalarGridSpec(
            num_scalar_prefetch=2,
            grid=(2,),
            in_specs=[
                tile,
                pl.BlockSpec((None, W, W), whole),
                pl.BlockSpec((None, H, W), whole),
                pl.BlockSpec((None, H, W), whole),
            ]
            + [pl.BlockSpec(memory_space=pl.ANY)] * len(before),
            out_specs=tile,
        ),
        input_output_aliases={6: 0} if before else {},
        compiler_params=params(),
        name="inner",
    )(meta, step, obj, g, mate, far, *before)


def border_kernel(s, step, edges, received, out):
    out[...] = edges[...] - step[s] * received[...]


def border(s, side, step, received, out):
    edge = pl.BlockSpec((None, None, T, H), lambda i, z: (s, i, 0, side * LAST))
    return pl.pallas_call(
        lambda *refs: border_kernel(s, *refs),
        out_shape=jax.ShapeDtypeStruct(out.shape, F32),
        grid_spec=pltpu.PrefetchScalarGridSpec(
            num_scalar_prefetch=1,
            grid=(2,),
            in_specs=[edge, pl.BlockSpec((None, T, H), lambda i, z: (i, 0, 0))],
            out_specs=edge,
        ),
        input_output_aliases={1: 0},
        compiler_params=params(),
        name="border",
    )(step, out, received)


def per_device(object_tiles, probe, prop_phase, amplitudes, offsets, counts, step_size):
    n_rows, n_cols = lax.axis_size("rows"), lax.axis_size("cols")
    rightward = [(i, i + 1) for i in range(n_cols - 1)]
    leftward = [(i + 1, i) for i in range(n_cols - 1)]
    mates = [(i, i ^ 1) for i in range(n_rows) if i ^ 1 < n_rows]
    fars = [(i, i + 1) for i in range(1, n_rows - 1, 2)]
    fars = fars + [(j, i) for i, j in fars]
    inward = [(i, i - 2) for i in range(2, n_rows, 2)] + [(i, i + 2) for i in range(1, n_rows - 2, 2)]
    outward = [(j, i) for i, j in inward]

    own = offsets.reshape(2)
    odd = lax.axis_index("rows").astype(jnp.int32).reshape(1) & 1
    left, right = [], []
    for s in range(2):
        left.append(lax.ppermute(object_tiles[s, :, :, T - H :], "cols", rightward))
        right.append(lax.ppermute(object_tiles[s, :, :, :H], "cols", leftward))
    meta = jnp.concatenate(
        [
            own,
            lax.ppermute(own, "rows", mates),
            lax.ppermute(own, "rows", fars),
            counts.reshape(1),
            odd,
        ]
    )
    la, lai, rb, rbi, q = prepare(meta, probe)
    kern = jnp.stack([jnp.cos(prop_phase), jnp.sin(prop_phase)])
    tables = (la, lai, rb, rbi)

    local, strip = [], []
    for s in range(2):
        args = (s, meta, object_tiles, left[s], right[s])
        passing = lax.ppermute(far_strip(*args), "rows", inward)
        strip.append(lax.ppermute(mate_strip(*args, passing), "rows", mates))
        local.append(local_window(*args))

    (psi,) = transforms(first_kernel, "first", [WINDOW], meta, local[0], strip[0], q, kern, *tables)
    g2, back, z2 = transforms(
        second_kernel,
        "second",
        [WINDOW, jax.ShapeDtypeStruct((2, W, W), BF16), STRIP],
        meta,
        local[1],
        strip[1],
        psi,
        amplitudes[0, 0, 0],
        *tables,
    )
    g1, z1 = transforms(third_kernel, "third", [WINDOW, STRIP], meta, back, q, kern, *tables)

    upper = (meta[PR0] < HALF).astype(jnp.int32)
    keep = upper + meta[ODD] == 1
    out = ()
    received = [None, None]
    for s, g, z in ((1, g2, z2), (0, g1, z1)):
        mate = lax.ppermute(z, "rows", mates)
        far = lax.ppermute(jnp.where(keep, 0.0, mate), "rows", outward)
        to_left, to_right = sides(meta, g, mate, far)
        received[s] = (
            lax.ppermute(to_right, "cols", rightward),
            lax.ppermute(to_left, "cols", leftward),
        )
        out = (inner(s, meta, step_size, object_tiles, g, mate, far, out),)
    out = out[0]
    for s in (1, 0):
        for side in range(2):
            out = border(s, side, step_size, received[s][side], out)
    return out


def solution(mesh):
    return jax.shard_map(
        per_device,
        mesh=mesh,
        in_specs=(
            P(None, None, "rows", "cols"),
            P(),
            P(),
            P("rows", "cols", None, None, None),
            P("rows", "cols", None, None),
            P("rows", "cols"),
            P(),
        ),
        out_specs=P(None, None, "rows", "cols"),
        check_vma=False,
    )
```

```python
import math

import jax
import jax.numpy as jnp
from jax import lax
from jax.experimental import pallas as pl
from jax.experimental.pallas import tpu as pltpu
from jax.sharding import PartitionSpec as P

H = 128
W = 512
T = 768
B = 128
HALF = W // 2
LAST = T // H - 1
R0, C0, PR0, PC0, FR0, FC0, LIVE, ODD = range(8)

F32, BF16 = jnp.float32, jnp.bfloat16
WINDOW = jax.ShapeDtypeStruct((2, W, W), F32)
STRIP = jax.ShapeDtypeStruct((2, H, W), F32)
SIDE = jax.ShapeDtypeStruct((2, T, H), F32)


def rows_below(shape, first, limit):
    return lax.broadcasted_iota(jnp.int32, shape, 0) + first < limit


def cols_below(shape, first, limit):
    return lax.broadcasted_iota(jnp.int32, shape, 1) + first < limit


def params(limit_mib):
    return pltpu.CompilerParams(vmem_limit_bytes=limit_mib << 20)


def vmem():
    return pl.BlockSpec(memory_space=pltpu.VMEM)


def smem():
    return pl.BlockSpec(memory_space=pltpu.SMEM)


def prep_kernel(meta, probe, la, lai, rb, rbi, q):
    def table(rows, first_row, row_shift, col_shift):
        p = (lax.broadcasted_iota(jnp.int32, (rows, W), 0) + (first_row - row_shift)) & (W - 1)
        k = (lax.broadcasted_iota(jnp.int32, (rows, W), 1) - col_shift) & (W - 1)
        m = (p * k) & (W - 1)
        quadrant = (m + W // 8) >> 7
        x = (m - quadrant * (W // 4)).astype(F32) * (2.0 * math.pi / W)
        y = x * x
        s = x * (1.0 + y * (-1.0 / 6 + y * (1.0 / 120 + y * (-1.0 / 5040 + y * (1.0 / 362880)))))
        c = 1.0 + y * (-0.5 + y * (1.0 / 24 + y * (-1.0 / 720 + y * (1.0 / 40320 - y * (1.0 / 3628800)))))
        swap = (quadrant & 1) == 1
        cos = jnp.where(swap, s, c)
        sin = jnp.where(swap, c, s)
        cos = jnp.where(((quadrant + 1) & 2) == 2, -cos, cos)
        sin = jnp.where((quadrant & 2) == 2, -sin, sin)
        scaling = 1.0 / math.sqrt(W)
        return (cos * scaling).astype(BF16), (-sin * scaling).astype(BF16)

    r0, c0 = meta[R0], meta[C0]
    for first in range(0, W, B):
        rows = pl.ds(first, B)
        later = pl.ds(W + first, B)
        la[rows, :W], la[rows, W:] = table(B, first, 0, r0)
        lai[rows, :W], lai[rows, W:] = table(B, first, r0, 0)
        rb[rows, :], rb[later, :] = table(B, first, c0, 0)
        rbi[rows, :], rbi[later, :] = table(B, first, 0, c0)
    for part in range(2):
        q[part] = pltpu.roll(pltpu.roll(probe[part], r0 & (W - 1), 0), c0 & (W - 1), 1)


def prepare(meta, probe):
    return pl.pallas_call(
        prep_kernel,
        out_shape=[
            jax.ShapeDtypeStruct((W, 2 * W), BF16),
            jax.ShapeDtypeStruct((W, 2 * W), BF16),
            jax.ShapeDtypeStruct((2 * W, W), BF16),
            jax.ShapeDtypeStruct((2 * W, W), BF16),
            jax.ShapeDtypeStruct((2, W, W), F32),
        ],
        in_specs=[smem(), vmem()],
        out_specs=[vmem()] * 5,
        compiler_params=params(16),
        name="prepare",
    )(meta, probe)


def whole(kernel, name, out_shape, *operands, limit=16, **more):
    return pl.pallas_call(
        kernel,
        out_shape=out_shape,
        in_specs=[smem()] + [vmem()] * (len(operands) - 1),
        out_specs=[vmem()] * len(out_shape),
        compiler_params=params(limit),
        name=name,
        **more,
    )(*operands)


def edges(s, obj):
    return obj[s, :, :, :H], obj[s, :, :, T - H :]


def pack(tile, left, right, c0):
    shape = (tile.shape[0], H)
    middle = (tile.shape[0], W - 2 * H)
    a = jnp.where(cols_below(shape, 0, c0), tile[:, W - H : W], left)
    b = jnp.where(cols_below(middle, H, c0), tile[:, W:], tile[:, : W - 2 * H])
    c = jnp.where(cols_below(shape, W - H, c0), right, tile[:, W - 2 * H : W - H])
    return a, b, c


def put(out, rows, pieces):
    a, b, c = pieces
    out[rows, :H] = a
    out[rows, H : W - H] = b
    out[rows, W - H :] = c


def mate_takes(meta):
    upper = (meta[PR0] < HALF).astype(jnp.int32)
    return upper + meta[ODD] == 1


def far_takes(meta):
    upper = (meta[FR0] < HALF).astype(jnp.int32)
    return upper + meta[ODD] != 1


def pack_edge(out, s, obj, left, right, last, c0):
    rows = pl.ds(pl.multiple_of(last * (T - H), H), H)
    for part in range(2):
        put(out.at[part], slice(None), pack(obj[s, part, rows, :], left[part, rows, :], right[part, rows, :], c0))


def far_kernel(s, meta, obj, left, right, out):
    pack_edge(out, s, obj, left, right, meta[ODD], meta[FC0])


def mate_kernel(s, meta, obj, left, right, passing, out):
    own = mate_takes(meta)

    @pl.when(own)
    def _():
        pack_edge(out, s, obj, left, right, 1 - meta[ODD], meta[PC0])

    @pl.when(jnp.logical_not(own))
    def _():
        out[...] = passing[...]


def local_kernel(s, meta, obj, left, right, out):
    r0, c0 = meta[R0], meta[C0]
    for part in range(2):

        def packed(first):
            rows = pl.ds(first, B)
            return pack(obj[s, part, rows, :], left[part, rows, :], right[part, rows, :], c0)

        put(out.at[part], pl.ds(0, B), packed(W - H))
        for first in range(B, W - B, B):
            low, high = packed(first - H), packed(first + W - H)
            put(
                out.at[part],
                pl.ds(first, B),
                [jnp.where(rows_below(x.shape, first, r0), y, x) for x, y in zip(low, high)],
            )
        put(out.at[part], pl.ds(W - B, B), packed(W - B - H))


def window_rows(meta, local, strip, part, first):
    x = local[part, pl.ds(first, B), :]
    if first == 0:
        x = jnp.where(rows_below(x.shape, first, meta[R0]), x, strip[part])
    if first == W - B:
        x = jnp.where(rows_below(x.shape, first, meta[R0]), strip[part], x)
    return x


def put_left(v4, first, re, im, inverse):
    re, im = re.astype(BF16), im.astype(BF16)
    rows, later = pl.ds(first, B), pl.ds(W + first, B)
    v4[rows, :W] = re
    v4[rows, W:] = im
    v4[later, :W] = im if inverse else -im
    v4[later, W:] = -re if inverse else re


def left_product(table, v4, m4, inverse):
    for first in range(0, W, B):
        rows, later = pl.ds(first, B), pl.ds(W + first, B)
        mid = jnp.dot(table[rows, :], v4[...], preferred_element_type=F32).astype(BF16)
        re, im = mid[:, :W], mid[:, W:]
        m4[rows, :W] = re
        m4[rows, W:] = im if inverse else -im
        m4[later, :W] = im
        m4[later, W:] = -re if inverse else re


def right_product(m4, table, first):
    re = jnp.dot(m4[pl.ds(first, B), :], table[...], preferred_element_type=F32)
    im = jnp.dot(m4[pl.ds(W + first, B), :], table[...], preferred_element_type=F32)
    return re, im


def first_kernel(meta, local, strip, q, kern_re, kern_im, la, lai, rb, rbi, psi, v4, m4):
    for first in range(0, W, B):
        rows = pl.ds(first, B)
        o_re = window_rows(meta, local, strip, 0, first)
        o_im = window_rows(meta, local, strip, 1, first)
        q_re, q_im = q[0, rows, :], q[1, rows, :]
        put_left(v4, first, q_re * o_re - q_im * o_im, q_re * o_im + q_im * o_re, False)
    left_product(la, v4, m4, False)
    for first in range(0, W, B):
        rows = pl.ds(first, B)
        re, im = right_product(m4, rb, first)
        k_re, k_im = kern_re[rows, :], kern_im[rows, :]
        put_left(v4, first, re * k_re - im * k_im, re * k_im + im * k_re, True)
    left_product(lai, v4, m4, True)
    for first in range(0, W, B):
        rows = pl.ds(first, B)
        psi[0, rows, :], psi[1, rows, :] = right_product(m4, rbi, first)


def edge_rows(meta, g, zg):
    keep_first = meta[R0] < HALF
    live = meta[LIVE] > 0

    @pl.when(keep_first)
    def _():
        for part in range(2):
            x = g[part, :H, :]
            hide = rows_below(x.shape, 0, meta[R0])
            zg[part] = jnp.where(jnp.logical_and(live, jnp.logical_not(hide)), x, 0.0)

    @pl.when(jnp.logical_not(keep_first))
    def _():
        for part in range(2):
            x = g[part, W - H :, :]
            show = rows_below(x.shape, W - H, meta[R0])
            zg[part] = jnp.where(jnp.logical_and(live, show), x, 0.0)


def second_kernel(meta, local, strip, psi, amp, la, lai, rb, rbi, g2, back, zg, v4, m4):
    for first in range(0, W, B):
        rows = pl.ds(first, B)
        o_re = window_rows(meta, local, strip, 0, first)
        o_im = window_rows(meta, local, strip, 1, first)
        p_re, p_im = psi[0, rows, :], psi[1, rows, :]
        put_left(v4, first, p_re * o_re - p_im * o_im, p_re * o_im + p_im * o_re, False)
    left_product(la, v4, m4, False)
    for first in range(0, W, B):
        rows = pl.ds(first, B)
        re, im = right_product(m4, rb, first)
        factor = 1.0 - amp[rows, :].astype(F32) / jnp.sqrt(re * re + im * im + 1.0)
        put_left(v4, first, re * factor, im * factor, True)
    left_product(lai, v4, m4, True)
    for first in range(0, W, B):
        rows = pl.ds(first, B)
        re, im = right_product(m4, rbi, first)
        p_re, p_im = psi[0, rows, :], psi[1, rows, :]
        g2[0, rows, :] = p_re * re + p_im * im
        g2[1, rows, :] = p_re * im - p_im * re
        o_re = window_rows(meta, local, strip, 0, first)
        o_im = window_rows(meta, local, strip, 1, first)
        back[0, rows, :] = (o_re * re + o_im * im).astype(BF16)
        back[1, rows, :] = (o_re * im - o_im * re).astype(BF16)
    edge_rows(meta, g2, zg)


def third_kernel(meta, back, q, kern_re, kern_im, la, lai, rb, rbi, g1, zg, v4, m4):
    for first in range(0, W, B):
        rows = pl.ds(first, B)
        put_left(v4, first, back[0, rows, :], back[1, rows, :], False)
    left_product(la, v4, m4, False)
    for first in range(0, W, B):
        rows = pl.ds(first, B)
        re, im = right_product(m4, rb, first)
        k_re, k_im = kern_re[rows, :], kern_im[rows, :]
        put_left(v4, first, re * k_re + im * k_im, im * k_re - re * k_im, True)
    left_product(lai, v4, m4, True)
    for first in range(0, W, B):
        rows = pl.ds(first, B)
        re, im = right_product(m4, rbi, first)
        q_re, q_im = q[0, rows, :], q[1, rows, :]
        g1[0, rows, :] = q_re * re + q_im * im
        g1[1, rows, :] = q_re * im - q_im * re
    edge_rows(meta, g1, zg)


def transforms(kernel, name, out_shape, meta, *operands):
    return pl.pallas_call(
        kernel,
        out_shape=out_shape,
        in_specs=[smem()] + [vmem()] * len(operands),
        out_specs=[vmem()] * len(out_shape),
        scratch_shapes=[pltpu.VMEM((2 * W, 2 * W), BF16), pltpu.VMEM((2 * W, 2 * W), BF16)],
        compiler_params=params(16),
        name=name,
    )(meta, *operands)


def shares(meta, part, mate, far):
    odd = meta[ODD] > 0
    mate = jnp.where(mate_takes(meta), mate[part], 0.0)
    far = jnp.where(far_takes(meta), far[part], 0.0)
    top = jnp.where(odd, mate, far)
    bottom = jnp.where(odd, far, mate)
    c_top = jnp.where(odd, meta[PC0], meta[FC0])
    c_bottom = jnp.where(odd, meta[FC0], meta[PC0])
    return (top, c_top), (bottom, c_bottom)


def left_part(x, c0):
    x = x[:, :H]
    return jnp.where(cols_below(x.shape, 0, c0), 0.0, x)


def right_part(x, c0):
    x = x[:, W - H :]
    return jnp.where(cols_below(x.shape, W - H, c0), x, 0.0)


def inner_parts(x, c0):
    low, high = x[:, H:], x[:, : W - H]
    low = jnp.where(cols_below(low.shape, H, c0), 0.0, low)
    high = jnp.where(cols_below(high.shape, 0, c0), high, 0.0)
    return low, high


def tile_rows(meta, g, part, first):
    live = meta[LIVE] > 0
    if first < W - H:
        x = g[part, pl.ds(first + H, B), :]
        hide = rows_below(x.shape, first + H, meta[R0])
        return jnp.where(jnp.logical_and(live, jnp.logical_not(hide)), x, 0.0)
    x = g[part, pl.ds(first - (W - H), B), :]
    show = rows_below(x.shape, first - (W - H), meta[R0])
    return jnp.where(jnp.logical_and(live, show), x, 0.0)


def sides_kernel(meta, g, mate, far, to_left, to_right):
    for part in range(2):
        top, bottom = shares(meta, part, mate, far)
        for first in range(0, T, B):
            x = tile_rows(meta, g, part, first)
            a, b = left_part(x, meta[C0]), right_part(x, meta[C0])
            if first == 0:
                a, b = a + left_part(*top), b + right_part(*top)
            if first == T - B:
                a, b = a + left_part(*bottom), b + right_part(*bottom)
            to_left[part, pl.ds(first, B), :] = a
            to_right[part, pl.ds(first, B), :] = b


def update_kernel(s, meta, step, obj, g, mate, far, from_left, from_right, *rest):
    out, tile, sems = rest[-3:]
    size = step[s]
    copies = []
    for part in range(2):
        top, bottom = shares(meta, part, mate, far)
        for first in range(0, T, B):
            rows = pl.ds(first, B)
            low, high = inner_parts(tile_rows(meta, g, part, first), meta[C0])
            if first in (0, T - B):
                more = inner_parts(*(top if first == 0 else bottom))
                low, high = low + more[0], high + more[1]
            left = low[:, :H] + from_left[part, rows, :]
            right = high[:, W - 2 * H :] + from_right[part, rows, :]
            tile[part, rows, :H] = obj[s, part, rows, :H] - size * left
            tile[part, rows, H : W - H] = obj[s, part, rows, H : W - H] - size * low[:, H:]
            tile[part, rows, W - H : T - H] = obj[s, part, rows, W - H : T - H] - size * high[:, : W - 2 * H]
            tile[part, rows, T - H :] = obj[s, part, rows, T - H :] - size * right
            copy = pltpu.make_async_copy(tile.at[part, rows, :], out.at[s, part, rows, :], sems.at[part, first // B])
            copy.start()
            copies.append(copy)
    for copy in copies:
        copy.wait()


def update(s, meta, step, obj, g, mate, far, from_left, from_right, before):
    hbm = pl.BlockSpec(memory_space=pl.ANY)
    return pl.pallas_call(
        lambda *refs: update_kernel(s, *refs),
        out_shape=jax.ShapeDtypeStruct(obj.shape, F32),
        in_specs=[smem()] * 2 + [vmem()] * 6 + [hbm] * len(before),
        out_specs=hbm,
        scratch_shapes=[pltpu.VMEM((2, T, T), F32), pltpu.SemaphoreType.DMA((2, T // B))],
        input_output_aliases={8: 0} if before else {},
        compiler_params=params(16),
        name="update",
    )(meta, step, obj, g, mate, far, from_left, from_right, *before)


def per_device(object_tiles, probe, prop_phase, amplitudes, offsets, counts, step_size):
    n_rows, n_cols = lax.axis_size("rows"), lax.axis_size("cols")
    rightward = [(i, i + 1) for i in range(n_cols - 1)]
    leftward = [(i + 1, i) for i in range(n_cols - 1)]
    mates = [(i, i ^ 1) for i in range(n_rows) if i ^ 1 < n_rows]
    fars = [(i, i + 1) for i in range(1, n_rows - 1, 2)]
    fars = fars + [(j, i) for i, j in fars]
    inward = [(i, i - 2) for i in range(2, n_rows, 2)] + [(i, i + 2) for i in range(1, n_rows - 2, 2)]
    outward = [(j, i) for i, j in inward]

    own = offsets.reshape(2)
    odd = lax.axis_index("rows").astype(jnp.int32).reshape(1) & 1
    left, right = [None, None], [None, None]

    def send_edges(s, to_left, to_right):
        left[s] = lax.ppermute(to_right, "cols", rightward)
        right[s] = lax.ppermute(to_left, "cols", leftward)

    send_edges(0, *edges(0, object_tiles))
    beside = [lax.ppermute(own, "rows", mates), lax.ppermute(own, "rows", fars)]
    kernel = (jnp.cos(prop_phase), jnp.sin(prop_phase))
    ready = lax.optimization_barrier(
        (*edges(1, object_tiles), *beside, *prepare(own, probe), *kernel)
    )
    meta = jnp.concatenate([own, *ready[2:4], counts.reshape(1), odd])
    tables, q, kernel = ready[4:8], ready[8], ready[9:]
    send_edges(1, *ready[:2])

    local, strip = [], []
    for s in range(2):
        args = (meta, object_tiles, left[s], right[s])
        bind = lambda kernel, s=s: lambda *refs: kernel(s, *refs)
        (far,) = whole(bind(far_kernel), "far_strip", [STRIP], *args)
        passing = lax.ppermute(far, "rows", inward)
        (mate,) = whole(bind(mate_kernel), "mate_strip", [STRIP], *args, passing)
        strip.append(lax.ppermute(mate, "rows", mates))
        local += whole(bind(local_kernel), "local_window", [WINDOW], *args)

    (psi,) = transforms(first_kernel, "first", [WINDOW], meta, local[0], strip[0], q, *kernel, *tables)
    g2, back, z2 = transforms(
        second_kernel,
        "second",
        [WINDOW, jax.ShapeDtypeStruct((2, W, W), BF16), STRIP],
        meta,
        local[1],
        strip[1],
        psi,
        amplitudes[0, 0, 0],
        *tables,
    )
    g1, z1 = transforms(third_kernel, "third", [WINDOW, STRIP], meta, back, q, *kernel, *tables)

    out = ()
    for s, g, z in ((1, g2, z2), (0, g1, z1)):
        mate = lax.ppermute(z, "rows", mates)
        far = lax.ppermute(mate, "rows", outward)
        to_left, to_right = whole(sides_kernel, "sides", [SIDE] * 2, meta, g, mate, far)
        from_left = lax.ppermute(to_right, "cols", rightward)
        from_right = lax.ppermute(to_left, "cols", leftward)
        out = (update(s, meta, step_size, object_tiles, g, mate, far, from_left, from_right, out),)
    return out[0]


def solution(mesh):
    return jax.shard_map(
        per_device,
        mesh=mesh,
        in_specs=(
            P(None, None, "rows", "cols"),
            P(),
            P(),
            P("rows", "cols", None, None, None),
            P("rows", "cols", None, None),
            P("rows", "cols"),
            P(),
        ),
        out_specs=P(None, None, "rows", "cols"),
        check_vma=False,
    )
```

```python
import math

import jax
import jax.numpy as jnp
from jax import lax
from jax.experimental import pallas as pl
from jax.experimental.pallas import tpu as pltpu
from jax.sharding import PartitionSpec as P

H = 128
W = 512
T = 768
B = 128
HALF = W // 2
LAST = T // H - 1
R0, C0, PR0, PC0, FR0, FC0, LIVE, ODD = range(8)

F32, BF16 = jnp.float32, jnp.bfloat16
WINDOW = jax.ShapeDtypeStruct((2, W, W), F32)
STRIP = jax.ShapeDtypeStruct((2, H, W), F32)
SIDE = jax.ShapeDtypeStruct((2, T, H), F32)


def rows_below(shape, first, limit):
    return lax.broadcasted_iota(jnp.int32, shape, 0) + first < limit


def cols_below(shape, first, limit):
    return lax.broadcasted_iota(jnp.int32, shape, 1) + first < limit


def params(limit_mib):
    return pltpu.CompilerParams(vmem_limit_bytes=limit_mib << 20)


def vmem():
    return pl.BlockSpec(memory_space=pltpu.VMEM)


def smem():
    return pl.BlockSpec(memory_space=pltpu.SMEM)


def table(rows, first_row, row_shift, col_shift):
    p = (lax.broadcasted_iota(jnp.int32, (rows, W), 0) + (first_row - row_shift)) & (W - 1)
    k = (lax.broadcasted_iota(jnp.int32, (rows, W), 1) - col_shift) & (W - 1)
    m = (p * k) & (W - 1)
    quadrant = (m + W // 8) >> 7
    x = (m - quadrant * (W // 4)).astype(F32) * (2.0 * math.pi / W)
    y = x * x
    s = x * (1.0 + y * (-1.0 / 6 + y * (1.0 / 120 + y * (-1.0 / 5040 + y * (1.0 / 362880)))))
    c = 1.0 + y * (-0.5 + y * (1.0 / 24 + y * (-1.0 / 720 + y * (1.0 / 40320 - y * (1.0 / 3628800)))))
    swap = (quadrant & 1) == 1
    cos = jnp.where(swap, s, c)
    sin = jnp.where(swap, c, s)
    cos = jnp.where(((quadrant + 1) & 2) == 2, -cos, cos)
    sin = jnp.where((quadrant & 2) == 2, -sin, sin)
    scaling = 1.0 / math.sqrt(W)
    return (cos * scaling).astype(BF16), (-sin * scaling).astype(BF16)


def forward_kernel(meta, probe, la, rb, q):
    r0, c0 = meta[R0], meta[C0]
    for first in range(0, W, B):
        rows = pl.ds(first, B)
        later = pl.ds(W + first, B)
        la[rows, :W], la[rows, W:] = table(B, first, 0, r0)
        rb[rows, :], rb[later, :] = table(B, first, c0, 0)
    for part in range(2):
        q[part] = pltpu.roll(pltpu.roll(probe[part], r0 & (W - 1), 0), c0 & (W - 1), 1)


def inverse_kernel(meta, lai, rbi):
    r0, c0 = meta[R0], meta[C0]
    for first in range(0, W, B):
        rows = pl.ds(first, B)
        later = pl.ds(W + first, B)
        lai[rows, :W], lai[rows, W:] = table(B, first, r0, 0)
        rbi[rows, :], rbi[later, :] = table(B, first, 0, c0)


LEFT = jax.ShapeDtypeStruct((W, 2 * W), BF16)
RIGHT = jax.ShapeDtypeStruct((2 * W, W), BF16)


def whole(kernel, name, out_shape, *operands, limit=16, **more):
    return pl.pallas_call(
        kernel,
        out_shape=out_shape,
        in_specs=[smem()] + [vmem()] * (len(operands) - 1),
        out_specs=[vmem()] * len(out_shape),
        compiler_params=params(limit),
        name=name,
        **more,
    )(*operands)


def edges(s, obj):
    return obj[s, :, :, :H], obj[s, :, :, T - H :]


def pack(tile, left, right, c0):
    shape = (tile.shape[0], H)
    middle = (tile.shape[0], W - 2 * H)
    a = jnp.where(cols_below(shape, 0, c0), tile[:, W - H : W], left)
    b = jnp.where(cols_below(middle, H, c0), tile[:, W:], tile[:, : W - 2 * H])
    c = jnp.where(cols_below(shape, W - H, c0), right, tile[:, W - 2 * H : W - H])
    return a, b, c


def put(out, rows, pieces):
    a, b, c = pieces
    out[rows, :H] = a
    out[rows, H : W - H] = b
    out[rows, W - H :] = c


def mate_takes(meta):
    upper = (meta[PR0] < HALF).astype(jnp.int32)
    return upper + meta[ODD] == 1


def far_takes(meta):
    upper = (meta[FR0] < HALF).astype(jnp.int32)
    return upper + meta[ODD] != 1


def pack_edge(out, obj, left, right, last, c0):
    rows = pl.ds(pl.multiple_of(last * (T - H), H), H)
    for part in range(2):
        put(out.at[part], slice(None), pack(obj[part], left[part, rows, :], right[part, rows, :], c0))


def far_kernel(meta, obj, left, right, out):
    pack_edge(out, obj, left, right, meta[ODD], meta[FC0])


def mate_kernel(meta, obj, left, right, passing, out):
    own = mate_takes(meta)

    @pl.when(own)
    def _():
        pack_edge(out, obj, left, right, 1 - meta[ODD], meta[PC0])

    @pl.when(jnp.logical_not(own))
    def _():
        out[...] = passing[...]


def local_kernel(meta, obj, left, right, out):
    r0, c0 = meta[R0], meta[C0]
    part = pl.program_id(0)

    def packed(first):
        rows = pl.ds(first, B)
        return pack(obj[rows, :], left[part, rows, :], right[part, rows, :], c0)

    put(out.at[part], pl.ds(0, B), packed(W - H))
    for first in range(B, W - B, B):
        low, high = packed(first - H), packed(first + W - H)
        put(
            out.at[part],
            pl.ds(first, B),
            [jnp.where(rows_below(x.shape, first, r0), y, x) for x, y in zip(low, high)],
        )
    put(out.at[part], pl.ds(W - B, B), packed(W - B - H))


def on_tile(kernel, name, tile, steps, out_shape, meta, obj, *operands):
    return pl.pallas_call(
        kernel,
        out_shape=out_shape,
        grid_spec=pltpu.PrefetchScalarGridSpec(
            num_scalar_prefetch=1,
            grid=(steps,),
            in_specs=[tile] + [vmem()] * len(operands),
            out_specs=vmem(),
        ),
        compiler_params=params(52),
        name=name,
    )(meta, obj, *operands)


def far_strip(s, *args):
    tile = pl.BlockSpec((None, 2, H, T), lambda i, m: (s, 0, m[ODD] * LAST, 0))
    return on_tile(far_kernel, "far_strip", tile, 1, STRIP, *args)


def mate_strip(s, *args):
    tile = pl.BlockSpec((None, 2, H, T), lambda i, m: (s, 0, (1 - m[ODD]) * LAST, 0))
    return on_tile(mate_kernel, "mate_strip", tile, 1, STRIP, *args)


def local_window(s, *args):
    tile = pl.BlockSpec((None, None, T, T), lambda i, m: (s, i, 0, 0))
    return on_tile(local_kernel, "local_window", tile, 2, WINDOW, *args)


def window_rows(meta, local, strip, part, first):
    x = local[part, pl.ds(first, B), :]
    if first == 0:
        x = jnp.where(rows_below(x.shape, first, meta[R0]), x, strip[part])
    if first == W - B:
        x = jnp.where(rows_below(x.shape, first, meta[R0]), strip[part], x)
    return x


def put_left(v4, first, re, im, inverse):
    re, im = re.astype(BF16), im.astype(BF16)
    rows, later = pl.ds(first, B), pl.ds(W + first, B)
    v4[rows, :W] = re
    v4[rows, W:] = im
    v4[later, :W] = im if inverse else -im
    v4[later, W:] = -re if inverse else re


def left_product(table, v4, m4, inverse):
    for first in range(0, W, B):
        rows, later = pl.ds(first, B), pl.ds(W + first, B)
        mid = jnp.dot(table[rows, :], v4[...], preferred_element_type=F32).astype(BF16)
        re, im = mid[:, :W], mid[:, W:]
        m4[rows, :W] = re
        m4[rows, W:] = im if inverse else -im
        m4[later, :W] = im
        m4[later, W:] = -re if inverse else re


def right_product(m4, table, first):
    re = jnp.dot(m4[pl.ds(first, B), :], table[...], preferred_element_type=F32)
    im = jnp.dot(m4[pl.ds(W + first, B), :], table[...], preferred_element_type=F32)
    return re, im


def first_kernel(meta, local, strip, q, kern_re, kern_im, la, lai, rb, rbi, psi, v4, m4):
    for first in range(0, W, B):
        rows = pl.ds(first, B)
        o_re = window_rows(meta, local, strip, 0, first)
        o_im = window_rows(meta, local, strip, 1, first)
        q_re, q_im = q[0, rows, :], q[1, rows, :]
        put_left(v4, first, q_re * o_re - q_im * o_im, q_re * o_im + q_im * o_re, False)
    left_product(la, v4, m4, False)
    for first in range(0, W, B):
        rows = pl.ds(first, B)
        re, im = right_product(m4, rb, first)
        k_re, k_im = kern_re[rows, :], kern_im[rows, :]
        put_left(v4, first, re * k_re - im * k_im, re * k_im + im * k_re, True)
    left_product(lai, v4, m4, True)
    for first in range(0, W, B):
        rows = pl.ds(first, B)
        psi[0, rows, :], psi[1, rows, :] = right_product(m4, rbi, first)


def edge_rows(meta, g, zg):
    keep_first = meta[R0] < HALF
    live = meta[LIVE] > 0

    @pl.when(keep_first)
    def _():
        for part in range(2):
            x = g[part, :H, :]
            hide = rows_below(x.shape, 0, meta[R0])
            zg[part] = jnp.where(jnp.logical_and(live, jnp.logical_not(hide)), x, 0.0)

    @pl.when(jnp.logical_not(keep_first))
    def _():
        for part in range(2):
            x = g[part, W - H :, :]
            show = rows_below(x.shape, W - H, meta[R0])
            zg[part] = jnp.where(jnp.logical_and(live, show), x, 0.0)


def second_kernel(meta, local, strip, psi, amp, la, lai, rb, rbi, g2, back, zg, v4, m4):
    for first in range(0, W, B):
        rows = pl.ds(first, B)
        o_re = window_rows(meta, local, strip, 0, first)
        o_im = window_rows(meta, local, strip, 1, first)
        p_re, p_im = psi[0, rows, :], psi[1, rows, :]
        put_left(v4, first, p_re * o_re - p_im * o_im, p_re * o_im + p_im * o_re, False)
    left_product(la, v4, m4, False)
    for first in range(0, W, B):
        rows = pl.ds(first, B)
        re, im = right_product(m4, rb, first)
        factor = 1.0 - amp[rows, :].astype(F32) / jnp.sqrt(re * re + im * im + 1.0)
        put_left(v4, first, re * factor, im * factor, True)
    left_product(lai, v4, m4, True)
    for first in range(0, W, B):
        rows = pl.ds(first, B)
        re, im = right_product(m4, rbi, first)
        p_re, p_im = psi[0, rows, :], psi[1, rows, :]
        g2[0, rows, :] = p_re * re + p_im * im
        g2[1, rows, :] = p_re * im - p_im * re
        o_re = window_rows(meta, local, strip, 0, first)
        o_im = window_rows(meta, local, strip, 1, first)
        back[0, rows, :] = (o_re * re + o_im * im).astype(BF16)
        back[1, rows, :] = (o_re * im - o_im * re).astype(BF16)
    edge_rows(meta, g2, zg)


def third_kernel(meta, back, q, kern_re, kern_im, la, lai, rb, rbi, g1, zg, v4, m4):
    for first in range(0, W, B):
        rows = pl.ds(first, B)
        put_left(v4, first, back[0, rows, :], back[1, rows, :], False)
    left_product(la, v4, m4, False)
    for first in range(0, W, B):
        rows = pl.ds(first, B)
        re, im = right_product(m4, rb, first)
        k_re, k_im = kern_re[rows, :], kern_im[rows, :]
        put_left(v4, first, re * k_re + im * k_im, im * k_re - re * k_im, True)
    left_product(lai, v4, m4, True)
    for first in range(0, W, B):
        rows = pl.ds(first, B)
        re, im = right_product(m4, rbi, first)
        q_re, q_im = q[0, rows, :], q[1, rows, :]
        g1[0, rows, :] = q_re * re + q_im * im
        g1[1, rows, :] = q_re * im - q_im * re
    edge_rows(meta, g1, zg)


def transforms(kernel, name, out_shape, meta, *operands):
    return pl.pallas_call(
        kernel,
        out_shape=out_shape,
        in_specs=[smem()] + [vmem()] * len(operands),
        out_specs=[vmem()] * len(out_shape),
        scratch_shapes=[pltpu.VMEM((2 * W, 2 * W), BF16), pltpu.VMEM((2 * W, 2 * W), BF16)],
        compiler_params=params(16),
        name=name,
    )(meta, *operands)


def shares(meta, part, mate, far):
    odd = meta[ODD] > 0
    mate = jnp.where(mate_takes(meta), mate[part], 0.0)
    far = jnp.where(far_takes(meta), far[part], 0.0)
    top = jnp.where(odd, mate, far)
    bottom = jnp.where(odd, far, mate)
    c_top = jnp.where(odd, meta[PC0], meta[FC0])
    c_bottom = jnp.where(odd, meta[FC0], meta[PC0])
    return (top, c_top), (bottom, c_bottom)


def left_part(x, c0):
    x = x[:, :H]
    return jnp.where(cols_below(x.shape, 0, c0), 0.0, x)


def right_part(x, c0):
    x = x[:, W - H :]
    return jnp.where(cols_below(x.shape, W - H, c0), x, 0.0)


def inner_parts(x, c0):
    low, high = x[:, H:], x[:, : W - H]
    low = jnp.where(cols_below(low.shape, H, c0), 0.0, low)
    high = jnp.where(cols_below(high.shape, 0, c0), high, 0.0)
    return low, high


def tile_rows(meta, g, part, first):
    live = meta[LIVE] > 0
    if first < W - H:
        x = g[part, pl.ds(first + H, B), :]
        hide = rows_below(x.shape, first + H, meta[R0])
        return jnp.where(jnp.logical_and(live, jnp.logical_not(hide)), x, 0.0)
    x = g[part, pl.ds(first - (W - H), B), :]
    show = rows_below(x.shape, first - (W - H), meta[R0])
    return jnp.where(jnp.logical_and(live, show), x, 0.0)


def sides_kernel(meta, g, mate, far, to_left, to_right):
    for part in range(2):
        top, bottom = shares(meta, part, mate, far)
        for first in range(0, T, B):
            x = tile_rows(meta, g, part, first)
            a, b = left_part(x, meta[C0]), right_part(x, meta[C0])
            if first == 0:
                a, b = a + left_part(*top), b + right_part(*top)
            if first == T - B:
                a, b = a + left_part(*bottom), b + right_part(*bottom)
            to_left[part, pl.ds(first, B), :] = a
            to_right[part, pl.ds(first, B), :] = b


def update_kernel(s, meta, step, obj, g, mate, far, from_left, from_right, *rest):
    out, tile, sems = rest[-3:]
    size = step[s]
    copies = []
    for part in range(2):
        top, bottom = shares(meta, part, mate, far)
        for first in range(0, T, B):
            rows = pl.ds(first, B)
            low, high = inner_parts(tile_rows(meta, g, part, first), meta[C0])
            if first in (0, T - B):
                more = inner_parts(*(top if first == 0 else bottom))
                low, high = low + more[0], high + more[1]
            left = low[:, :H] + from_left[part, rows, :]
            right = high[:, W - 2 * H :] + from_right[part, rows, :]
            tile[part, rows, :H] = obj[s, part, rows, :H] - size * left
            tile[part, rows, H : W - H] = obj[s, part, rows, H : W - H] - size * low[:, H:]
            tile[part, rows, W - H : T - H] = obj[s, part, rows, W - H : T - H] - size * high[:, : W - 2 * H]
            tile[part, rows, T - H :] = obj[s, part, rows, T - H :] - size * right
            copy = pltpu.make_async_copy(tile.at[part, rows, :], out.at[s, part, rows, :], sems.at[part, first // B])
            copy.start()
            copies.append(copy)
    for copy in copies:
        copy.wait()


def update(s, meta, step, obj, g, mate, far, from_left, from_right, before):
    hbm = pl.BlockSpec(memory_space=pl.ANY)
    return pl.pallas_call(
        lambda *refs: update_kernel(s, *refs),
        out_shape=jax.ShapeDtypeStruct(obj.shape, F32),
        in_specs=[smem()] * 2 + [vmem()] * 6 + [hbm] * len(before),
        out_specs=hbm,
        scratch_shapes=[pltpu.VMEM((2, T, T), F32), pltpu.SemaphoreType.DMA((2, T // B))],
        input_output_aliases={8: 0} if before else {},
        compiler_params=params(16),
        name="update",
    )(meta, step, obj, g, mate, far, from_left, from_right, *before)


def per_device(object_tiles, probe, prop_phase, amplitudes, offsets, counts, step_size):
    n_rows, n_cols = lax.axis_size("rows"), lax.axis_size("cols")
    rightward = [(i, i + 1) for i in range(n_cols - 1)]
    leftward = [(i + 1, i) for i in range(n_cols - 1)]
    mates = [(i, i ^ 1) for i in range(n_rows) if i ^ 1 < n_rows]
    fars = [(i, i + 1) for i in range(1, n_rows - 1, 2)]
    fars = fars + [(j, i) for i, j in fars]
    inward = [(i, i - 2) for i in range(2, n_rows, 2)] + [(i, i + 2) for i in range(1, n_rows - 2, 2)]
    outward = [(j, i) for i, j in inward]

    own = offsets.reshape(2)
    odd = lax.axis_index("rows").astype(jnp.int32).reshape(1) & 1
    left, right = [None, None], [None, None]

    def send_edges(s, to_left, to_right):
        left[s] = lax.ppermute(to_right, "cols", rightward)
        right[s] = lax.ppermute(to_left, "cols", leftward)

    beside = [lax.ppermute(own, "rows", mates), lax.ppermute(own, "rows", fars)]
    first, *starts = lax.optimization_barrier((own, *edges(0, object_tiles)))
    send_edges(0, *starts)
    forward = whole(forward_kernel, "forward_tables", [LEFT, RIGHT, WINDOW], first, probe)
    kernel = (jnp.cos(prop_phase), jnp.sin(prop_phase))
    ready = lax.optimization_barrier((object_tiles, *forward, *kernel, *beside))
    obj, la, rb, q = ready[:4]
    kernel, beside = ready[4:6], ready[6:]
    second, *starts = lax.optimization_barrier((own, *edges(1, obj)))
    send_edges(1, *starts)
    lai, rbi = whole(inverse_kernel, "inverse_tables", [LEFT, RIGHT], second)
    meta = jnp.concatenate([own, *beside, counts.reshape(1), odd])
    tables = (la, lai, rb, rbi)
    left[0], right[0], *tables = lax.optimization_barrier((left[0], right[0], *tables))

    local, strip = [], []
    for s in range(2):
        args = (meta, object_tiles, left[s], right[s])
        passing = lax.ppermute(far_strip(s, *args), "rows", inward)
        strip.append(lax.ppermute(mate_strip(s, *args, passing), "rows", mates))
        local.append(local_window(s, *args))

    (psi,) = transforms(first_kernel, "first", [WINDOW], meta, local[0], strip[0], q, *kernel, *tables)
    g2, back, z2 = transforms(
        second_kernel,
        "second",
        [WINDOW, jax.ShapeDtypeStruct((2, W, W), BF16), STRIP],
        meta,
        local[1],
        strip[1],
        psi,
        amplitudes[0, 0, 0],
        *tables,
    )
    g1, z1 = transforms(third_kernel, "third", [WINDOW, STRIP], meta, back, q, *kernel, *tables)

    out = ()
    for s, g, z in ((1, g2, z2), (0, g1, z1)):
        mate = lax.ppermute(z, "rows", mates)
        far = lax.ppermute(mate, "rows", outward)
        to_left, to_right = whole(sides_kernel, "sides", [SIDE] * 2, meta, g, mate, far)
        from_left = lax.ppermute(to_right, "cols", rightward)
        from_right = lax.ppermute(to_left, "cols", leftward)
        out = (update(s, meta, step_size, object_tiles, g, mate, far, from_left, from_right, out),)
    return out[0]


def solution(mesh):
    return jax.shard_map(
        per_device,
        mesh=mesh,
        in_specs=(
            P(None, None, "rows", "cols"),
            P(),
            P(),
            P("rows", "cols", None, None, None),
            P("rows", "cols", None, None),
            P("rows", "cols"),
            P(),
        ),
        out_specs=P(None, None, "rows", "cols"),
        check_vma=False,
    )
```

```python
import math

import jax
import jax.numpy as jnp
from jax import lax
from jax.experimental import pallas as pl
from jax.experimental.pallas import tpu as pltpu
from jax.sharding import PartitionSpec as P

H = 128
W = 512
T = 768
B = 128
HALF = W // 2
LAST = T // H - 1
R0, C0, PR0, PC0, FR0, FC0, LIVE, ODD, CORE = range(9)

F32, BF16 = jnp.float32, jnp.bfloat16
WINDOW = jax.ShapeDtypeStruct((2, W, W), F32)
STRIP = jax.ShapeDtypeStruct((2, H, W), F32)
ENDS = jax.ShapeDtypeStruct((2, 2, 2 * H, H), F32)
MIDDLE = jax.ShapeDtypeStruct((2, 2, T - 2 * H, H), F32)


def rows_below(shape, first, limit):
    return lax.broadcasted_iota(jnp.int32, shape, 0) + first < limit


def cols_below(shape, first, limit):
    return lax.broadcasted_iota(jnp.int32, shape, 1) + first < limit


def params(limit_mib):
    return pltpu.CompilerParams(vmem_limit_bytes=limit_mib << 20)


def vmem():
    return pl.BlockSpec(memory_space=pltpu.VMEM)


def smem():
    return pl.BlockSpec(memory_space=pltpu.SMEM)


def sine_cosine(x, quadrant):
    y = x * x
    s = x * (1.0 + y * (-1.0 / 6 + y * (1.0 / 120 + y * (-1.0 / 5040 + y * (1.0 / 362880)))))
    c = 1.0 + y * (-0.5 + y * (1.0 / 24 + y * (-1.0 / 720 + y * (1.0 / 40320 - y * (1.0 / 3628800)))))
    swap = (quadrant & 1) == 1
    sin = jnp.where(swap, c, s)
    cos = jnp.where(swap, s, c)
    sin = jnp.where((quadrant & 2) == 2, -sin, sin)
    cos = jnp.where(((quadrant + 1) & 2) == 2, -cos, cos)
    return sin, cos


def table(rows, first_row, row_shift, col_shift):
    p = (lax.broadcasted_iota(jnp.int32, (rows, W), 0) + (first_row - row_shift)) & (W - 1)
    k = (lax.broadcasted_iota(jnp.int32, (rows, W), 1) - col_shift) & (W - 1)
    m = (p * k) & (W - 1)
    quadrant = (m + W // 8) >> 7
    x = (m - quadrant * (W // 4)).astype(F32) * (2.0 * math.pi / W)
    sin, cos = sine_cosine(x, quadrant)
    scaling = 1.0 / math.sqrt(W)
    return (cos * scaling).astype(BF16), (-sin * scaling).astype(BF16)


def phase_kernel(meta, phase, obj, cosine, sine):
    parts = (1.5703125, 4.837512969970703e-4, 7.549789948768648e-8)
    for first in range(0, W, B):
        rows = pl.ds(first, B)
        x = phase[rows, :]
        n = jnp.floor(x * (2.0 / math.pi) + 0.5)
        for part in parts:
            x = x - n * part
        sine[rows, :], cosine[rows, :] = sine_cosine(x, n.astype(jnp.int32))


def scalars_kernel(own, mate, far, count, odd, core, meta):
    meta[R0], meta[C0] = own[0], own[1]
    meta[PR0], meta[PC0] = mate[0], mate[1]
    meta[FR0], meta[FC0] = far[0], far[1]
    meta[LIVE], meta[ODD], meta[CORE] = count[0], odd[0], core[0]


def scalars(*operands):
    return pl.pallas_call(
        scalars_kernel,
        out_shape=jax.ShapeDtypeStruct((9,), jnp.int32),
        in_specs=[smem()] * 6,
        out_specs=smem(),
        compiler_params=params(1),
        name="scalars",
    )(*operands)


def forward_kernel(meta, probe, la, rb, q):
    r0, c0 = meta[R0], meta[C0]
    for first in range(0, W, B):
        rows = pl.ds(first, B)
        later = pl.ds(W + first, B)
        la[rows, :W], la[rows, W:] = table(B, first, 0, r0)
        rb[rows, :], rb[later, :] = table(B, first, c0, 0)
    for part in range(2):
        q[part] = pltpu.roll(pltpu.roll(probe[part], r0 & (W - 1), 0), c0 & (W - 1), 1)


def inverse_kernel(meta, lai, rbi):
    r0, c0 = meta[R0], meta[C0]
    for first in range(0, W, B):
        rows = pl.ds(first, B)
        later = pl.ds(W + first, B)
        lai[rows, :W], lai[rows, W:] = table(B, first, r0, 0)
        rbi[rows, :], rbi[later, :] = table(B, first, 0, c0)


PLANE = jax.ShapeDtypeStruct((W, W), F32)
LEFT = jax.ShapeDtypeStruct((W, 2 * W), BF16)
RIGHT = jax.ShapeDtypeStruct((2 * W, W), BF16)


def whole(kernel, name, out_shape, *operands, limit=16, **more):
    return pl.pallas_call(
        kernel,
        out_shape=out_shape,
        in_specs=[smem()] + [vmem()] * (len(operands) - 1),
        out_specs=[vmem()] * len(out_shape),
        compiler_params=params(limit),
        name=name,
        **more,
    )(*operands)


def edges_kernel(pieces, core, obj, near, wide, sem):
    far_side = pl.multiple_of((1 - core[0]) * (T - H), H)
    columns = [pl.ds(far_side, H), pl.ds(pl.multiple_of(T - H - far_side, H), H)]
    copies = []
    for rows, place in pieces:
        for out, cols in zip((near, wide), columns):
            source = obj.at[:, :, pl.ds(rows, place.size), cols]
            copies.append(pltpu.make_async_copy(source, out.at[:, :, place, :], sem.at[len(copies)]))
    for copy in copies:
        copy.start()
    for copy in copies:
        copy.wait()


def edges(shape, pieces, core, obj):
    return pl.pallas_call(
        lambda *refs: edges_kernel(pieces, *refs),
        out_shape=[shape] * 2,
        in_specs=[smem(), pl.BlockSpec(memory_space=pl.ANY)],
        out_specs=[vmem()] * 2,
        scratch_shapes=[pltpu.SemaphoreType.DMA((2 * len(pieces),))],
        compiler_params=params(56),
        name="edges",
    )(core, obj)


def by_side(meta, near, wide):
    first = meta[CORE] == 0
    return jnp.where(first, wide, near), jnp.where(first, near, wide)


def pack(tile, left, right, c0):
    shape = (tile.shape[0], H)
    middle = (tile.shape[0], W - 2 * H)
    a = jnp.where(cols_below(shape, 0, c0), tile[:, W - H : W], left)
    b = jnp.where(cols_below(middle, H, c0), tile[:, W:], tile[:, : W - 2 * H])
    c = jnp.where(cols_below(shape, W - H, c0), right, tile[:, W - 2 * H : W - H])
    return a, b, c


def put(out, rows, pieces):
    a, b, c = pieces
    out[rows, :H] = a
    out[rows, H : W - H] = b
    out[rows, W - H :] = c


def mate_takes(meta):
    upper = (meta[PR0] < HALF).astype(jnp.int32)
    return upper + meta[ODD] == 1


def far_takes(meta):
    upper = (meta[FR0] < HALF).astype(jnp.int32)
    return upper + meta[ODD] != 1


def pack_edge(meta, out, s, obj, near, wide, last, c0):
    rows = pl.ds(pl.multiple_of(last * (T - H), H), H)
    ends = pl.ds(pl.multiple_of(last * H, H), H)
    for part in range(2):
        sides = by_side(meta, near[s, part, ends, :], wide[s, part, ends, :])
        put(out.at[part], slice(None), pack(obj[s, part, rows, :], *sides, c0))


def far_kernel(s, meta, obj, near, wide, out):
    pack_edge(meta, out, s, obj, near, wide, meta[ODD], meta[FC0])


def mate_kernel(s, meta, obj, near, wide, passing, out):
    own = mate_takes(meta)

    @pl.when(own)
    def _():
        pack_edge(meta, out, s, obj, near, wide, 1 - meta[ODD], meta[PC0])

    @pl.when(jnp.logical_not(own))
    def _():
        out[...] = passing[...]


def beside_rows(meta, s, part, first, near, wide, near_ends, wide_ends):
    if first in (0, T - B):
        rows = pl.ds(min(first, H), B)
        return by_side(meta, near_ends[s, part, rows, :], wide_ends[s, part, rows, :])
    rows = pl.ds(first - H, B)
    return by_side(meta, near[s, part, rows, :], wide[s, part, rows, :])


def local_kernel(s, meta, obj, near_ends, wide_ends, near, wide, out):
    r0, c0 = meta[R0], meta[C0]
    for part in range(2):

        def packed(first):
            rows = pl.ds(first, B)
            sides = beside_rows(meta, s, part, first, near, wide, near_ends, wide_ends)
            return pack(obj[s, part, rows, :], *sides, c0)

        put(out.at[part], pl.ds(0, B), packed(W - H))
        for first in range(B, W - B, B):
            low, high = packed(first - H), packed(first + W - H)
            put(
                out.at[part],
                pl.ds(first, B),
                [jnp.where(rows_below(x.shape, first, r0), y, x) for x, y in zip(low, high)],
            )
        put(out.at[part], pl.ds(W - B, B), packed(W - B - H))


def far_strip(s, *args):
    return whole(lambda *refs: far_kernel(s, *refs), "far_strip", [STRIP], *args)[0]


def mate_strip(s, *args):
    return whole(lambda *refs: mate_kernel(s, *refs), "mate_strip", [STRIP], *args)[0]


def local_window(s, *args):
    return whole(lambda *refs: local_kernel(s, *refs), "local_window", [WINDOW], *args)[0]


def window_rows(meta, local, strip, part, first):
    x = local[part, pl.ds(first, B), :]
    if first == 0:
        x = jnp.where(rows_below(x.shape, first, meta[R0]), x, strip[part])
    if first == W - B:
        x = jnp.where(rows_below(x.shape, first, meta[R0]), strip[part], x)
    return x


def put_left(v4, first, re, im, inverse):
    re, im = re.astype(BF16), im.astype(BF16)
    rows, later = pl.ds(first, B), pl.ds(W + first, B)
    v4[rows, :W] = re
    v4[rows, W:] = im
    v4[later, :W] = im if inverse else -im
    v4[later, W:] = -re if inverse else re


def left_product(table, v4, m4, inverse):
    for first in range(0, W, B):
        rows, later = pl.ds(first, B), pl.ds(W + first, B)
        mid = jnp.dot(table[rows, :], v4[...], preferred_element_type=F32).astype(BF16)
        re, im = mid[:, :W], mid[:, W:]
        m4[rows, :W] = re
        m4[rows, W:] = im if inverse else -im
        m4[later, :W] = im
        m4[later, W:] = -re if inverse else re


def right_product(m4, table, first):
    re = jnp.dot(m4[pl.ds(first, B), :], table[...], preferred_element_type=F32)
    im = jnp.dot(m4[pl.ds(W + first, B), :], table[...], preferred_element_type=F32)
    return re, im


def first_kernel(meta, local, strip, q, kern_re, kern_im, la, lai, rb, rbi, psi, v4, m4):
    for first in range(0, W, B):
        rows = pl.ds(first, B)
        o_re = window_rows(meta, local, strip, 0, first)
        o_im = window_rows(meta, local, strip, 1, first)
        q_re, q_im = q[0, rows, :], q[1, rows, :]
        put_left(v4, first, q_re * o_re - q_im * o_im, q_re * o_im + q_im * o_re, False)
    left_product(la, v4, m4, False)
    for first in range(0, W, B):
        rows = pl.ds(first, B)
        re, im = right_product(m4, rb, first)
        k_re, k_im = kern_re[rows, :], kern_im[rows, :]
        put_left(v4, first, re * k_re - im * k_im, re * k_im + im * k_re, True)
    left_product(lai, v4, m4, True)
    for first in range(0, W, B):
        rows = pl.ds(first, B)
        psi[0, rows, :], psi[1, rows, :] = right_product(m4, rbi, first)


def edge_rows(meta, g, zg):
    keep_first = meta[R0] < HALF
    live = meta[LIVE] > 0

    @pl.when(keep_first)
    def _():
        for part in range(2):
            x = g[part, :H, :]
            hide = rows_below(x.shape, 0, meta[R0])
            zg[part] = jnp.where(jnp.logical_and(live, jnp.logical_not(hide)), x, 0.0)

    @pl.when(jnp.logical_not(keep_first))
    def _():
        for part in range(2):
            x = g[part, W - H :, :]
            show = rows_below(x.shape, W - H, meta[R0])
            zg[part] = jnp.where(jnp.logical_and(live, show), x, 0.0)


def second_kernel(meta, local, strip, psi, amp, la, lai, rb, rbi, g2, back, zg, v4, m4):
    for first in range(0, W, B):
        rows = pl.ds(first, B)
        o_re = window_rows(meta, local, strip, 0, first)
        o_im = window_rows(meta, local, strip, 1, first)
        p_re, p_im = psi[0, rows, :], psi[1, rows, :]
        put_left(v4, first, p_re * o_re - p_im * o_im, p_re * o_im + p_im * o_re, False)
    left_product(la, v4, m4, False)
    for first in range(0, W, B):
        rows = pl.ds(first, B)
        re, im = right_product(m4, rb, first)
        factor = 1.0 - amp[rows, :].astype(F32) / jnp.sqrt(re * re + im * im + 1.0)
        put_left(v4, first, re * factor, im * factor, True)
    left_product(lai, v4, m4, True)
    for first in range(0, W, B):
        rows = pl.ds(first, B)
        re, im = right_product(m4, rbi, first)
        p_re, p_im = psi[0, rows, :], psi[1, rows, :]
        g2[0, rows, :] = p_re * re + p_im * im
        g2[1, rows, :] = p_re * im - p_im * re
        o_re = window_rows(meta, local, strip, 0, first)
        o_im = window_rows(meta, local, strip, 1, first)
        back[0, rows, :] = (o_re * re + o_im * im).astype(BF16)
        back[1, rows, :] = (o_re * im - o_im * re).astype(BF16)
    edge_rows(meta, g2, zg)


def third_kernel(meta, back, q, kern_re, kern_im, la, lai, rb, rbi, g1, zg, v4, m4):
    for first in range(0, W, B):
        rows = pl.ds(first, B)
        put_left(v4, first, back[0, rows, :], back[1, rows, :], False)
    left_product(la, v4, m4, False)
    for first in range(0, W, B):
        rows = pl.ds(first, B)
        re, im = right_product(m4, rb, first)
        k_re, k_im = kern_re[rows, :], kern_im[rows, :]
        put_left(v4, first, re * k_re + im * k_im, im * k_re - re * k_im, True)
    left_product(lai, v4, m4, True)
    for first in range(0, W, B):
        rows = pl.ds(first, B)
        re, im = right_product(m4, rbi, first)
        q_re, q_im = q[0, rows, :], q[1, rows, :]
        g1[0, rows, :] = q_re * re + q_im * im
        g1[1, rows, :] = q_re * im - q_im * re
    edge_rows(meta, g1, zg)


def transforms(kernel, name, out_shape, meta, *operands):
    return pl.pallas_call(
        kernel,
        out_shape=out_shape,
        in_specs=[smem()] + [vmem()] * len(operands),
        out_specs=[vmem()] * len(out_shape),
        scratch_shapes=[pltpu.VMEM((2 * W, 2 * W), BF16), pltpu.VMEM((2 * W, 2 * W), BF16)],
        compiler_params=params(16),
        name=name,
    )(meta, *operands)


def shares(meta, part, mate, far):
    odd = meta[ODD] > 0
    mate = jnp.where(mate_takes(meta), mate[part], 0.0)
    far = jnp.where(far_takes(meta), far[part], 0.0)
    top = jnp.where(odd, mate, far)
    bottom = jnp.where(odd, far, mate)
    c_top = jnp.where(odd, meta[PC0], meta[FC0])
    c_bottom = jnp.where(odd, meta[FC0], meta[PC0])
    return (top, c_top), (bottom, c_bottom)


def left_part(x, c0):
    x = x[:, :H]
    return jnp.where(cols_below(x.shape, 0, c0), 0.0, x)


def right_part(x, c0):
    x = x[:, W - H :]
    return jnp.where(cols_below(x.shape, W - H, c0), x, 0.0)


def inner_parts(x, c0):
    low, high = x[:, H:], x[:, : W - H]
    low = jnp.where(cols_below(low.shape, H, c0), 0.0, low)
    high = jnp.where(cols_below(high.shape, 0, c0), high, 0.0)
    return low, high


def tile_rows(meta, g, part, first):
    live = meta[LIVE] > 0
    if first < W - H:
        x = g[part, pl.ds(first + H, B), :]
        hide = rows_below(x.shape, first + H, meta[R0])
        return jnp.where(jnp.logical_and(live, jnp.logical_not(hide)), x, 0.0)
    x = g[part, pl.ds(first - (W - H), B), :]
    show = rows_below(x.shape, first - (W - H), meta[R0])
    return jnp.where(jnp.logical_and(live, show), x, 0.0)


def middle_kernel(meta, g1, g2, near, wide):
    for s, g in enumerate((g1, g2)):
        for part in range(2):
            for first in range(B, T - B, B):
                x = tile_rows(meta, g, part, first)
                x = by_side(meta, left_part(x, meta[C0]), right_part(x, meta[C0]))
                rows = pl.ds(first - H, B)
                near[s, part, rows, :], wide[s, part, rows, :] = x


def corner_kernel(meta, g, mate, far, near, wide):
    for part in range(2):
        for first, (strip, c0) in zip((0, T - H), shares(meta, part, mate, far)):
            x = tile_rows(meta, g, part, first)
            a = left_part(x, meta[C0]) + left_part(strip, c0)
            b = right_part(x, meta[C0]) + right_part(strip, c0)
            rows = pl.ds(min(first, H), B)
            near[part, rows, :], wide[part, rows, :] = by_side(meta, a, b)


def own_rows(meta, g, part, first, mate, far):
    low, high = inner_parts(tile_rows(meta, g, part, first), meta[C0])
    if first in (0, T - B):
        top, bottom = shares(meta, part, mate, far)
        more = inner_parts(*(top if first == 0 else bottom))
        low, high = low + more[0], high + more[1]
    return low, high


def inner_kernel(s, meta, step, obj, g, mate, far, *rest):
    out, tile, sems = rest[-3:]
    size = step[s]
    copies = []
    for part in range(2):
        for first in range(0, T, B):
            rows = pl.ds(first, B)
            low, high = own_rows(meta, g, part, first, mate, far)
            tile[part, rows, : W - 2 * H] = obj[s, part, rows, H : W - H] - size * low[:, H:]
            tile[part, rows, W - 2 * H :] = obj[s, part, rows, W - H : T - H] - size * high[:, : W - 2 * H]
            target = out.at[s, part, rows, pl.ds(H, T - 2 * H)]
            copies.append(pltpu.make_async_copy(tile.at[part, rows, :], target, sems.at[part, first // B]))
            copies[-1].start()
    for copy in copies:
        copy.wait()


def border_kernel(s, meta, step, obj, g, mate, far, near, wide, near_ends, wide_ends, before, out, tile, sems):
    size = step[s]
    copies = []
    for part in range(2):
        for first in range(0, T, B):
            rows = pl.ds(first, B)
            low, high = own_rows(meta, g, part, first, mate, far)
            if first in (0, T - B):
                ends = pl.ds(min(first, H), B)
                received = by_side(meta, near_ends[part, ends, :], wide_ends[part, ends, :])
            else:
                received = beside_rows(meta, s, part, first, near, wide, None, None)
            for side, x in enumerate((low[:, :H], high[:, W - 2 * H :])):
                cols = pl.ds(side * (T - H), H)
                tile[side, part, rows, :] = obj[s, part, rows, cols] - size * (x + received[side])
                target = out.at[s, part, rows, cols]
                sem = sems.at[part, side * (T // B) + first // B]
                copies.append(pltpu.make_async_copy(tile.at[side, part, rows, :], target, sem))
                copies[-1].start()
    for copy in copies:
        copy.wait()


def update(kernel, name, tile, sems, before, meta, step, obj, *operands):
    hbm = pl.BlockSpec(memory_space=pl.ANY)
    return pl.pallas_call(
        kernel,
        out_shape=jax.ShapeDtypeStruct(obj.shape, F32),
        in_specs=[smem()] * 2 + [vmem()] * (1 + len(operands)) + [hbm] * len(before),
        out_specs=hbm,
        scratch_shapes=[pltpu.VMEM(tile, F32), pltpu.SemaphoreType.DMA(sems)],
        input_output_aliases={3 + len(operands): 0} if before else {},
        compiler_params=params(16),
        name=name,
    )(meta, step, obj, *operands, *before)


def inner(s, before, *operands):
    kernel = lambda *refs: inner_kernel(s, *refs)
    return (update(kernel, "inner", (2, T, T - 2 * H), (2, T // B), before, *operands),)


def border(s, before, *operands):
    kernel = lambda *refs: border_kernel(s, *refs)
    return (update(kernel, "border", (2, 2, T, H), (2, 2 * (T // B)), before, *operands),)


def per_device(object_tiles, probe, prop_phase, amplitudes, offsets, counts, step_size):
    n_rows, n_cols = lax.axis_size("rows"), lax.axis_size("cols")
    at_chip = [(i, i ^ 1) for i in range(n_cols) if i ^ 1 < n_cols]
    past_chip = [(i, i + 1) for i in range(1, n_cols - 1, 2)]
    past_chip = past_chip + [(j, i) for i, j in past_chip]
    mates = [(i, i ^ 1) for i in range(n_rows) if i ^ 1 < n_rows]
    fars = [(i, i + 1) for i in range(1, n_rows - 1, 2)]
    fars = fars + [(j, i) for i, j in fars]
    inward = [(i, i - 2) for i in range(2, n_rows, 2)] + [(i, i + 2) for i in range(1, n_rows - 2, 2)]
    outward = [(j, i) for i, j in inward]

    own = offsets.reshape(2)
    parity = lambda axis: lax.axis_index(axis).astype(jnp.int32).reshape(1) & 1
    odd, core = parity("rows"), parity("cols")
    after = lambda *values: lax.optimization_barrier(values)

    beside = [lax.ppermute(own, "rows", mates), lax.ppermute(own, "rows", fars)]
    far, passing, strip, local = [[None, None] for _ in range(4)]

    def beside_cols(near, wide):
        wide = lax.ppermute(wide, "cols", past_chip)
        return lax.ppermute(near, "cols", at_chip), wide

    pieces = [(0, pl.ds(0, H)), (T - H, pl.ds(H, H))]
    first, obj, count, odd, *sent = after(
        own, object_tiles, counts.reshape(1), odd, *edges(ENDS, pieces, core, object_tiles)
    )
    ends = beside_cols(*sent)
    first, *sent = after(first, *edges(MIDDLE, [(H, pl.ds(0, T - 2 * H))], core, obj))
    middle = beside_cols(*sent)
    kernel = whole(phase_kernel, "phase", [PLANE, PLANE], first, prop_phase, object_tiles)
    first, *kernel = after(first, *kernel)
    meta = scalars(first, *beside, count, odd, core)

    for s in range(2):
        far[s] = far_strip(s, meta, object_tiles, *ends)
        passing[s] = lax.ppermute(far[s], "rows", inward)
    third, _ = after(meta, far[1])
    lai, rbi = whole(inverse_kernel, "inverse_tables", [LEFT, RIGHT], third)
    la, rb, q = whole(forward_kernel, "forward_tables", [LEFT, RIGHT, WINDOW], third, probe)
    passing[0], la, rb, q, lai, rbi = after(passing[0], la, rb, q, lai, rbi)
    strip[0] = lax.ppermute(mate_strip(0, meta, object_tiles, *ends, passing[0]), "rows", mates)
    local[0] = local_window(0, meta, object_tiles, *ends, *middle)
    local[1] = local_window(1, meta, object_tiles, *ends, *middle)
    strip[1] = lax.ppermute(mate_strip(1, meta, object_tiles, *ends, passing[1]), "rows", mates)
    tables = (la, lai, rb, rbi)

    (psi,) = transforms(first_kernel, "first", [WINDOW], meta, local[0], strip[0], q, *kernel, *tables)
    g2, back, z2 = transforms(
        second_kernel,
        "second",
        [WINDOW, jax.ShapeDtypeStruct((2, W, W), BF16), STRIP],
        meta,
        local[1],
        strip[1],
        psi,
        amplitudes[0, 0, 0],
        *tables,
    )
    g1, z1 = transforms(third_kernel, "third", [WINDOW, STRIP], meta, back, q, *kernel, *tables)

    mate, far, ends = [None, None], [None, None], [None, None]
    mate[1] = lax.ppermute(z2, "rows", mates)
    mate[0] = lax.ppermute(z1, "rows", mates)
    far[1] = lax.ppermute(mate[1], "rows", outward)
    _, *sent = after(mate[1], *whole(middle_kernel, "middle", [MIDDLE] * 2, meta, g1, g2))
    middle = beside_cols(*sent)
    far[0] = lax.ppermute(mate[0], "rows", outward)
    grads = (g1, g2)
    out = ()
    for s in (1, 0):
        shape = jax.ShapeDtypeStruct(ENDS.shape[1:], F32)
        sent = whole(corner_kernel, "corner", [shape] * 2, meta, grads[s], mate[s], far[s])
        ends[s] = beside_cols(*sent)
    for s in (1, 0):
        out = inner(s, out, meta, step_size, object_tiles, grads[s], mate[s], far[s])
    for s in (1, 0):
        out = border(s, out, meta, step_size, object_tiles, grads[s], mate[s], far[s], *middle, *ends[s])
    return out[0]


def solution(mesh):
    return jax.shard_map(
        per_device,
        mesh=mesh,
        in_specs=(
            P(None, None, "rows", "cols"),
            P(),
            P(),
            P("rows", "cols", None, None, None),
            P("rows", "cols", None, None),
            P("rows", "cols"),
            P(),
        ),
        out_specs=P(None, None, "rows", "cols"),
        check_vma=False,
    )
```

```python
import math

import jax
import jax.numpy as jnp
from jax import lax
from jax.experimental import pallas as pl
from jax.experimental.pallas import tpu as pltpu
from jax.sharding import PartitionSpec as P

H = 128
W = 512
T = 768
B = 128
HALF = W // 2
LAST = T // H - 1
R0, C0, PR0, PC0, FR0, FC0, LIVE, ODD, CORE = range(9)

F32, BF16 = jnp.float32, jnp.bfloat16
WINDOW = jax.ShapeDtypeStruct((2, W, W), F32)
STRIP = jax.ShapeDtypeStruct((2, H, W), F32)
ENDS = jax.ShapeDtypeStruct((2, 2, 2 * H, H), F32)
MIDDLE = jax.ShapeDtypeStruct((2, 2, T - 2 * H, H), F32)


def rows_below(shape, first, limit):
    return lax.broadcasted_iota(jnp.int32, shape, 0) + first < limit


def cols_below(shape, first, limit):
    return lax.broadcasted_iota(jnp.int32, shape, 1) + first < limit


def params(limit_mib):
    return pltpu.CompilerParams(vmem_limit_bytes=limit_mib << 20)


def vmem():
    return pl.BlockSpec(memory_space=pltpu.VMEM)


def smem():
    return pl.BlockSpec(memory_space=pltpu.SMEM)


def sine_cosine(x, quadrant):
    y = x * x
    s = x * (1.0 + y * (-1.0 / 6 + y * (1.0 / 120 + y * (-1.0 / 5040 + y * (1.0 / 362880)))))
    c = 1.0 + y * (-0.5 + y * (1.0 / 24 + y * (-1.0 / 720 + y * (1.0 / 40320 - y * (1.0 / 3628800)))))
    swap = (quadrant & 1) == 1
    sin = jnp.where(swap, c, s)
    cos = jnp.where(swap, s, c)
    sin = jnp.where((quadrant & 2) == 2, -sin, sin)
    cos = jnp.where(((quadrant + 1) & 2) == 2, -cos, cos)
    return sin, cos


def table(rows, first_row, row_shift, col_shift):
    p = (lax.broadcasted_iota(jnp.int32, (rows, W), 0) + (first_row - row_shift)) & (W - 1)
    k = (lax.broadcasted_iota(jnp.int32, (rows, W), 1) - col_shift) & (W - 1)
    m = (p * k) & (W - 1)
    quadrant = (m + W // 8) >> 7
    x = (m - quadrant * (W // 4)).astype(F32) * (2.0 * math.pi / W)
    sin, cos = sine_cosine(x, quadrant)
    scaling = 1.0 / math.sqrt(W)
    return (cos * scaling).astype(BF16), (-sin * scaling).astype(BF16)


def phase_kernel(meta, phase, obj, cosine, sine):
    parts = (1.5703125, 4.837512969970703e-4, 7.549789948768648e-8)
    for first in range(0, W, B):
        rows = pl.ds(first, B)
        x = phase[rows, :]
        n = jnp.floor(x * (2.0 / math.pi) + 0.5)
        for part in parts:
            x = x - n * part
        sine[rows, :], cosine[rows, :] = sine_cosine(x, n.astype(jnp.int32))


def scalars_kernel(own, mate, far, count, odd, core, meta):
    meta[R0], meta[C0] = own[0], own[1]
    meta[PR0], meta[PC0] = mate[0], mate[1]
    meta[FR0], meta[FC0] = far[0], far[1]
    meta[LIVE], meta[ODD], meta[CORE] = count[0], odd[0], core[0]


def scalars(*operands):
    return pl.pallas_call(
        scalars_kernel,
        out_shape=jax.ShapeDtypeStruct((9,), jnp.int32),
        in_specs=[smem()] * 6,
        out_specs=smem(),
        compiler_params=params(1),
        name="scalars",
    )(*operands)


def forward_kernel(meta, probe, la, rb, q):
    r0, c0 = meta[R0], meta[C0]
    for first in range(0, W, B):
        rows = pl.ds(first, B)
        later = pl.ds(W + first, B)
        la[rows, :W], la[rows, W:] = table(B, first, 0, r0)
        rb[rows, :], rb[later, :] = table(B, first, c0, 0)
    for part in range(2):
        q[part] = pltpu.roll(pltpu.roll(probe[part], r0 & (W - 1), 0), c0 & (W - 1), 1)


def inverse_kernel(meta, lai, rbi):
    r0, c0 = meta[R0], meta[C0]
    for first in range(0, W, B):
        rows = pl.ds(first, B)
        later = pl.ds(W + first, B)
        lai[rows, :W], lai[rows, W:] = table(B, first, r0, 0)
        rbi[rows, :], rbi[later, :] = table(B, first, 0, c0)


PLANE = jax.ShapeDtypeStruct((W, W), F32)
LEFT = jax.ShapeDtypeStruct((W, 2 * W), BF16)
RIGHT = jax.ShapeDtypeStruct((2 * W, W), BF16)


def whole(kernel, name, out_shape, *operands, limit=16, **more):
    return pl.pallas_call(
        kernel,
        out_shape=out_shape,
        in_specs=[smem()] + [vmem()] * (len(operands) - 1),
        out_specs=[vmem()] * len(out_shape),
        compiler_params=params(limit),
        name=name,
        **more,
    )(*operands)


def edges_kernel(pieces, core, obj, near, wide, sem):
    far_side = pl.multiple_of((1 - core[0]) * (T - H), H)
    columns = [pl.ds(far_side, H), pl.ds(pl.multiple_of(T - H - far_side, H), H)]
    copies = []
    for rows, place in pieces:
        for out, cols in zip((near, wide), columns):
            source = obj.at[:, :, pl.ds(rows, place.size), cols]
            copies.append(pltpu.make_async_copy(source, out.at[:, :, place, :], sem.at[len(copies)]))
    for copy in copies:
        copy.start()
    for copy in copies:
        copy.wait()


def edges(shape, pieces, core, obj):
    return pl.pallas_call(
        lambda *refs: edges_kernel(pieces, *refs),
        out_shape=[shape] * 2,
        in_specs=[smem(), pl.BlockSpec(memory_space=pl.ANY)],
        out_specs=[vmem()] * 2,
        scratch_shapes=[pltpu.SemaphoreType.DMA((2 * len(pieces),))],
        compiler_params=params(56),
        name="edges",
    )(core, obj)


def by_side(meta, near, wide):
    first = meta[CORE] == 0
    return jnp.where(first, wide, near), jnp.where(first, near, wide)


def pack(tile, left, right, c0):
    shape = (tile.shape[0], H)
    middle = (tile.shape[0], W - 2 * H)
    a = jnp.where(cols_below(shape, 0, c0), tile[:, W - H : W], left)
    b = jnp.where(cols_below(middle, H, c0), tile[:, W:], tile[:, : W - 2 * H])
    c = jnp.where(cols_below(shape, W - H, c0), right, tile[:, W - 2 * H : W - H])
    return a, b, c


def put(out, rows, pieces):
    a, b, c = pieces
    out[rows, :H] = a
    out[rows, H : W - H] = b
    out[rows, W - H :] = c


def mate_takes(meta):
    upper = (meta[PR0] < HALF).astype(jnp.int32)
    return upper + meta[ODD] == 1


def far_takes(meta):
    upper = (meta[FR0] < HALF).astype(jnp.int32)
    return upper + meta[ODD] != 1


def pack_edge(meta, out, s, obj, near, wide, last, c0):
    rows = pl.ds(pl.multiple_of(last * (T - H), H), H)
    ends = pl.ds(pl.multiple_of(last * H, H), H)
    for part in range(2):
        sides = by_side(meta, near[s, part, ends, :], wide[s, part, ends, :])
        put(out.at[part], slice(None), pack(obj[s, part, rows, :], *sides, c0))


def far_kernel(s, meta, obj, near, wide, out):
    pack_edge(meta, out, s, obj, near, wide, meta[ODD], meta[FC0])


def mate_kernel(s, meta, obj, near, wide, passing, out):
    own = mate_takes(meta)

    @pl.when(own)
    def _():
        pack_edge(meta, out, s, obj, near, wide, 1 - meta[ODD], meta[PC0])

    @pl.when(jnp.logical_not(own))
    def _():
        out[...] = passing[...]


def beside_rows(meta, s, part, first, near, wide, near_ends, wide_ends):
    if first in (0, T - B):
        rows = pl.ds(min(first, H), B)
        return by_side(meta, near_ends[s, part, rows, :], wide_ends[s, part, rows, :])
    rows = pl.ds(first - H, B)
    return by_side(meta, near[s, part, rows, :], wide[s, part, rows, :])


def local_kernel(s, meta, obj, near_ends, wide_ends, near, wide, out):
    r0, c0 = meta[R0], meta[C0]
    for part in range(2):

        def packed(first):
            rows = pl.ds(first, B)
            sides = beside_rows(meta, s, part, first, near, wide, near_ends, wide_ends)
            return pack(obj[s, part, rows, :], *sides, c0)

        put(out.at[part], pl.ds(0, B), packed(W - H))
        for first in range(B, W - B, B):
            low, high = packed(first - H), packed(first + W - H)
            put(
                out.at[part],
                pl.ds(first, B),
                [jnp.where(rows_below(x.shape, first, r0), y, x) for x, y in zip(low, high)],
            )
        put(out.at[part], pl.ds(W - B, B), packed(W - B - H))


def far_strip(s, *args):
    return whole(lambda *refs: far_kernel(s, *refs), "far_strip", [STRIP], *args)[0]


def mate_strip(s, *args):
    return whole(lambda *refs: mate_kernel(s, *refs), "mate_strip", [STRIP], *args)[0]


def local_window(s, *args):
    return whole(lambda *refs: local_kernel(s, *refs), "local_window", [WINDOW], *args)[0]


def window_rows(meta, local, strip, part, first):
    x = local[part, pl.ds(first, B), :]
    if first == 0:
        x = jnp.where(rows_below(x.shape, first, meta[R0]), x, strip[part])
    if first == W - B:
        x = jnp.where(rows_below(x.shape, first, meta[R0]), strip[part], x)
    return x


def put_left(v4, first, re, im, inverse):
    re, im = re.astype(BF16), im.astype(BF16)
    rows, later = pl.ds(first, B), pl.ds(W + first, B)
    v4[rows, :W] = re
    v4[rows, W:] = im
    v4[later, :W] = im if inverse else -im
    v4[later, W:] = -re if inverse else re


def left_product(table, v4, m4, inverse):
    for first in range(0, W, B):
        rows, later = pl.ds(first, B), pl.ds(W + first, B)
        mid = jnp.dot(table[rows, :], v4[...], preferred_element_type=F32).astype(BF16)
        re, im = mid[:, :W], mid[:, W:]
        m4[rows, :W] = re
        m4[rows, W:] = im if inverse else -im
        m4[later, :W] = im
        m4[later, W:] = -re if inverse else re


def right_product(m4, table, first):
    re = jnp.dot(m4[pl.ds(first, B), :], table[...], preferred_element_type=F32)
    im = jnp.dot(m4[pl.ds(W + first, B), :], table[...], preferred_element_type=F32)
    return re, im


def first_kernel(meta, local, strip, q, kern_re, kern_im, la, lai, rb, rbi, psi, v4, m4):
    for first in range(0, W, B):
        rows = pl.ds(first, B)
        o_re = window_rows(meta, local, strip, 0, first)
        o_im = window_rows(meta, local, strip, 1, first)
        q_re, q_im = q[0, rows, :], q[1, rows, :]
        put_left(v4, first, q_re * o_re - q_im * o_im, q_re * o_im + q_im * o_re, False)
    left_product(la, v4, m4, False)
    for first in range(0, W, B):
        rows = pl.ds(first, B)
        re, im = right_product(m4, rb, first)
        k_re, k_im = kern_re[rows, :], kern_im[rows, :]
        put_left(v4, first, re * k_re - im * k_im, re * k_im + im * k_re, True)
    left_product(lai, v4, m4, True)
    for first in range(0, W, B):
        rows = pl.ds(first, B)
        psi[0, rows, :], psi[1, rows, :] = right_product(m4, rbi, first)


def edge_rows(meta, g, zg):
    keep_first = meta[R0] < HALF
    live = meta[LIVE] > 0

    @pl.when(keep_first)
    def _():
        for part in range(2):
            x = g[part, :H, :]
            hide = rows_below(x.shape, 0, meta[R0])
            zg[part] = jnp.where(jnp.logical_and(live, jnp.logical_not(hide)), x, 0.0)

    @pl.when(jnp.logical_not(keep_first))
    def _():
        for part in range(2):
            x = g[part, W - H :, :]
            show = rows_below(x.shape, W - H, meta[R0])
            zg[part] = jnp.where(jnp.logical_and(live, show), x, 0.0)


def second_kernel(meta, local, strip, psi, amp, la, lai, rb, rbi, g2, back, zg, v4, m4):
    for first in range(0, W, B):
        rows = pl.ds(first, B)
        o_re = window_rows(meta, local, strip, 0, first)
        o_im = window_rows(meta, local, strip, 1, first)
        p_re, p_im = psi[0, rows, :], psi[1, rows, :]
        put_left(v4, first, p_re * o_re - p_im * o_im, p_re * o_im + p_im * o_re, False)
    left_product(la, v4, m4, False)
    for first in range(0, W, B):
        rows = pl.ds(first, B)
        re, im = right_product(m4, rb, first)
        factor = 1.0 - amp[rows, :].astype(F32) / jnp.sqrt(re * re + im * im + 1.0)
        put_left(v4, first, re * factor, im * factor, True)
    left_product(lai, v4, m4, True)
    for first in range(0, W, B):
        rows = pl.ds(first, B)
        re, im = right_product(m4, rbi, first)
        p_re, p_im = psi[0, rows, :], psi[1, rows, :]
        g2[0, rows, :] = p_re * re + p_im * im
        g2[1, rows, :] = p_re * im - p_im * re
        o_re = window_rows(meta, local, strip, 0, first)
        o_im = window_rows(meta, local, strip, 1, first)
        back[0, rows, :] = (o_re * re + o_im * im).astype(BF16)
        back[1, rows, :] = (o_re * im - o_im * re).astype(BF16)
    edge_rows(meta, g2, zg)


def third_kernel(meta, back, q, kern_re, kern_im, la, lai, rb, rbi, g1, zg, v4, m4):
    for first in range(0, W, B):
        rows = pl.ds(first, B)
        put_left(v4, first, back[0, rows, :], back[1, rows, :], False)
    left_product(la, v4, m4, False)
    for first in range(0, W, B):
        rows = pl.ds(first, B)
        re, im = right_product(m4, rb, first)
        k_re, k_im = kern_re[rows, :], kern_im[rows, :]
        put_left(v4, first, re * k_re + im * k_im, im * k_re - re * k_im, True)
    left_product(lai, v4, m4, True)
    for first in range(0, W, B):
        rows = pl.ds(first, B)
        re, im = right_product(m4, rbi, first)
        q_re, q_im = q[0, rows, :], q[1, rows, :]
        g1[0, rows, :] = q_re * re + q_im * im
        g1[1, rows, :] = q_re * im - q_im * re
    edge_rows(meta, g1, zg)


def transforms(kernel, name, out_shape, meta, *operands):
    return pl.pallas_call(
        kernel,
        out_shape=out_shape,
        in_specs=[smem()] + [vmem()] * len(operands),
        out_specs=[vmem()] * len(out_shape),
        scratch_shapes=[pltpu.VMEM((2 * W, 2 * W), BF16), pltpu.VMEM((2 * W, 2 * W), BF16)],
        compiler_params=params(16),
        name=name,
    )(meta, *operands)


def shares(meta, part, mate, far):
    odd = meta[ODD] > 0
    mate = jnp.where(mate_takes(meta), mate[part], 0.0)
    far = jnp.where(far_takes(meta), far[part], 0.0)
    top = jnp.where(odd, mate, far)
    bottom = jnp.where(odd, far, mate)
    c_top = jnp.where(odd, meta[PC0], meta[FC0])
    c_bottom = jnp.where(odd, meta[FC0], meta[PC0])
    return (top, c_top), (bottom, c_bottom)


def left_part(x, c0):
    x = x[:, :H]
    return jnp.where(cols_below(x.shape, 0, c0), 0.0, x)


def right_part(x, c0):
    x = x[:, W - H :]
    return jnp.where(cols_below(x.shape, W - H, c0), x, 0.0)


def inner_parts(x, c0):
    low, high = x[:, H:], x[:, : W - H]
    low = jnp.where(cols_below(low.shape, H, c0), 0.0, low)
    high = jnp.where(cols_below(high.shape, 0, c0), high, 0.0)
    return low, high


def tile_rows(meta, g, part, first):
    live = meta[LIVE] > 0
    if first < W - H:
        x = g[part, pl.ds(first + H, B), :]
        hide = rows_below(x.shape, first + H, meta[R0])
        return jnp.where(jnp.logical_and(live, jnp.logical_not(hide)), x, 0.0)
    x = g[part, pl.ds(first - (W - H), B), :]
    show = rows_below(x.shape, first - (W - H), meta[R0])
    return jnp.where(jnp.logical_and(live, show), x, 0.0)


def middle_kernel(meta, g1, g2, near, wide):
    for s, g in enumerate((g1, g2)):
        for part in range(2):
            for first in range(B, T - B, B):
                x = tile_rows(meta, g, part, first)
                x = by_side(meta, left_part(x, meta[C0]), right_part(x, meta[C0]))
                rows = pl.ds(first - H, B)
                near[s, part, rows, :], wide[s, part, rows, :] = x


def corner_kernel(meta, g, mate, far, near, wide):
    for part in range(2):
        for first, (strip, c0) in zip((0, T - H), shares(meta, part, mate, far)):
            x = tile_rows(meta, g, part, first)
            a = left_part(x, meta[C0]) + left_part(strip, c0)
            b = right_part(x, meta[C0]) + right_part(strip, c0)
            rows = pl.ds(min(first, H), B)
            near[part, rows, :], wide[part, rows, :] = by_side(meta, a, b)


def own_rows(meta, g, part, first, mate, far):
    low, high = inner_parts(tile_rows(meta, g, part, first), meta[C0])
    if first in (0, T - B):
        top, bottom = shares(meta, part, mate, far)
        more = inner_parts(*(top if first == 0 else bottom))
        low, high = low + more[0], high + more[1]
    return low, high


def inner_kernel(s, meta, step, obj, g, mate, far, *rest):
    out, tile, sems = rest[-3:]
    size = step[s]
    copies = []
    for part in range(2):
        for first in range(0, T, B):
            rows = pl.ds(first, B)
            low, high = own_rows(meta, g, part, first, mate, far)
            tile[part, rows, : W - 2 * H] = obj[s, part, rows, H : W - H] - size * low[:, H:]
            tile[part, rows, W - 2 * H :] = obj[s, part, rows, W - H : T - H] - size * high[:, : W - 2 * H]
            target = out.at[s, part, rows, pl.ds(H, T - 2 * H)]
            copies.append(pltpu.make_async_copy(tile.at[part, rows, :], target, sems.at[part, first // B]))
            copies[-1].start()
    for copy in copies:
        copy.wait()


def border_kernel(s, meta, step, obj, g, mate, far, near, wide, near_ends, wide_ends, before, out, tile, sems):
    size = step[s]
    copies = []
    for part in range(2):
        for first in range(0, T, B):
            rows = pl.ds(first, B)
            low, high = own_rows(meta, g, part, first, mate, far)
            if first in (0, T - B):
                ends = pl.ds(min(first, H), B)
                received = by_side(meta, near_ends[part, ends, :], wide_ends[part, ends, :])
            else:
                received = beside_rows(meta, s, part, first, near, wide, None, None)
            for side, x in enumerate((low[:, :H], high[:, W - 2 * H :])):
                cols = pl.ds(side * (T - H), H)
                tile[side, part, rows, :] = obj[s, part, rows, cols] - size * (x + received[side])
                target = out.at[s, part, rows, cols]
                sem = sems.at[part, side * (T // B) + first // B]
                copies.append(pltpu.make_async_copy(tile.at[side, part, rows, :], target, sem))
                copies[-1].start()
    for copy in copies:
        copy.wait()


def update(kernel, name, tile, sems, before, meta, step, obj, *operands):
    hbm = pl.BlockSpec(memory_space=pl.ANY)
    return pl.pallas_call(
        kernel,
        out_shape=jax.ShapeDtypeStruct(obj.shape, F32),
        in_specs=[smem()] * 2 + [vmem()] * (1 + len(operands)) + [hbm] * len(before),
        out_specs=hbm,
        scratch_shapes=[pltpu.VMEM(tile, F32), pltpu.SemaphoreType.DMA(sems)],
        input_output_aliases={3 + len(operands): 0} if before else {},
        compiler_params=params(16),
        name=name,
    )(meta, step, obj, *operands, *before)


def inner(s, before, *operands):
    kernel = lambda *refs: inner_kernel(s, *refs)
    return (update(kernel, "inner", (2, T, T - 2 * H), (2, T // B), before, *operands),)


def border(s, before, *operands):
    kernel = lambda *refs: border_kernel(s, *refs)
    return (update(kernel, "border", (2, 2, T, H), (2, 2 * (T // B)), before, *operands),)


def per_device(object_tiles, probe, prop_phase, amplitudes, offsets, counts, step_size):
    n_rows, n_cols = lax.axis_size("rows"), lax.axis_size("cols")
    at_chip = [(i, i ^ 1) for i in range(n_cols) if i ^ 1 < n_cols]
    past_chip = [(i, i + 1) for i in range(1, n_cols - 1, 2)]
    past_chip = past_chip + [(j, i) for i, j in past_chip]
    mates = [(i, i ^ 1) for i in range(n_rows) if i ^ 1 < n_rows]
    fars = [(i, i + 1) for i in range(1, n_rows - 1, 2)]
    fars = fars + [(j, i) for i, j in fars]
    inward = [(i, i - 2) for i in range(2, n_rows, 2)] + [(i, i + 2) for i in range(1, n_rows - 2, 2)]
    outward = [(j, i) for i, j in inward]

    own = offsets.reshape(2)
    parity = lambda axis: lax.axis_index(axis).astype(jnp.int32).reshape(1) & 1
    odd, core = parity("rows"), parity("cols")
    after = lambda *values: lax.optimization_barrier(values)

    beside = [lax.ppermute(own, "rows", mates), lax.ppermute(own, "rows", fars)]
    far, passing, strip, local = [[None, None] for _ in range(4)]

    def beside_cols(near, wide):
        wide = lax.ppermute(wide, "cols", past_chip)
        return lax.ppermute(near, "cols", at_chip), wide

    pieces = [(0, pl.ds(0, H)), (T - H, pl.ds(H, H))]
    first, obj, count, odd, *sent = after(
        own, object_tiles, counts.reshape(1), odd, *edges(ENDS, pieces, core, object_tiles)
    )
    ends = beside_cols(*sent)
    first, *sent = after(first, *edges(MIDDLE, [(H, pl.ds(0, T - 2 * H))], core, obj))
    first, *rest = after(first, *sent, *beside)
    beside = rest[2:]
    middle = beside_cols(*rest[:2])
    kernel = whole(phase_kernel, "phase", [PLANE, PLANE], first, prop_phase, object_tiles)
    first, *kernel = after(first, *kernel)
    meta = scalars(first, *beside, count, odd, core)

    for s in range(2):
        far[s] = far_strip(s, meta, object_tiles, *ends)
        passing[s] = lax.ppermute(far[s], "rows", inward)
    third, _ = after(meta, far[1])
    lai, rbi = whole(inverse_kernel, "inverse_tables", [LEFT, RIGHT], third)
    la, rb, q = whole(forward_kernel, "forward_tables", [LEFT, RIGHT, WINDOW], third, probe)
    passing[0], la, rb, q, lai, rbi, *middle = after(passing[0], la, rb, q, lai, rbi, *middle)
    strip[0] = lax.ppermute(mate_strip(0, meta, object_tiles, *ends, passing[0]), "rows", mates)
    local[0] = local_window(0, meta, object_tiles, *ends, *middle)
    local[1] = local_window(1, meta, object_tiles, *ends, *middle)
    strip[1] = lax.ppermute(mate_strip(1, meta, object_tiles, *ends, passing[1]), "rows", mates)
    tables = (la, lai, rb, rbi)

    (psi,) = transforms(first_kernel, "first", [WINDOW], meta, local[0], strip[0], q, *kernel, *tables)
    g2, back, z2 = transforms(
        second_kernel,
        "second",
        [WINDOW, jax.ShapeDtypeStruct((2, W, W), BF16), STRIP],
        meta,
        local[1],
        strip[1],
        psi,
        amplitudes[0, 0, 0],
        *tables,
    )
    g1, z1 = transforms(third_kernel, "third", [WINDOW, STRIP], meta, back, q, *kernel, *tables)

    mate, far, ends = [None, None], [None, None], [None, None]
    mate[1] = lax.ppermute(z2, "rows", mates)
    mate[0] = lax.ppermute(z1, "rows", mates)
    far[1] = lax.ppermute(mate[1], "rows", outward)
    _, *sent = after(mate[1], *whole(middle_kernel, "middle", [MIDDLE] * 2, meta, g1, g2))
    middle = beside_cols(*sent)
    far[0] = lax.ppermute(mate[0], "rows", outward)
    grads = (g1, g2)
    out = ()
    for s in (1, 0):
        shape = jax.ShapeDtypeStruct(ENDS.shape[1:], F32)
        sent = whole(corner_kernel, "corner", [shape] * 2, meta, grads[s], mate[s], far[s])
        ends[s] = beside_cols(*sent)
    for s in (1, 0):
        out = inner(s, out, meta, step_size, object_tiles, grads[s], mate[s], far[s])
    for s in (1, 0):
        out = border(s, out, meta, step_size, object_tiles, grads[s], mate[s], far[s], *middle, *ends[s])
    return out[0]


def solution(mesh):
    return jax.shard_map(
        per_device,
        mesh=mesh,
        in_specs=(
            P(None, None, "rows", "cols"),
            P(),
            P(),
            P("rows", "cols", None, None, None),
            P("rows", "cols", None, None),
            P("rows", "cols"),
            P(),
        ),
        out_specs=P(None, None, "rows", "cols"),
        check_vma=False,
    )
```

```python
import math

import jax
import jax.numpy as jnp
from jax import lax
from jax.experimental import pallas as pl
from jax.experimental.pallas import tpu as pltpu
from jax.sharding import PartitionSpec as P

H = 128
W = 512
T = 768
B = 128
HALF = W // 2
LAST = T // H - 1
R0, C0, PR0, PC0, FR0, FC0, LIVE, ODD, CORE = range(9)

F32, BF16 = jnp.float32, jnp.bfloat16
WINDOW = jax.ShapeDtypeStruct((2, W, W), F32)
STRIP = jax.ShapeDtypeStruct((2, H, W), F32)
ENDS = jax.ShapeDtypeStruct((2, 2, 2 * H, H), F32)
MIDDLE = jax.ShapeDtypeStruct((2, 2, T - 2 * H, H), F32)


def rows_below(shape, first, limit):
    return lax.broadcasted_iota(jnp.int32, shape, 0) + first < limit


def cols_below(shape, first, limit):
    return lax.broadcasted_iota(jnp.int32, shape, 1) + first < limit


def params(limit_mib):
    return pltpu.CompilerParams(vmem_limit_bytes=limit_mib << 20)


def vmem():
    return pl.BlockSpec(memory_space=pltpu.VMEM)


def smem():
    return pl.BlockSpec(memory_space=pltpu.SMEM)


def sine_cosine(x, quadrant):
    y = x * x
    s = x * (1.0 + y * (-1.0 / 6 + y * (1.0 / 120 + y * (-1.0 / 5040 + y * (1.0 / 362880)))))
    c = 1.0 + y * (-0.5 + y * (1.0 / 24 + y * (-1.0 / 720 + y * (1.0 / 40320 - y * (1.0 / 3628800)))))
    swap = (quadrant & 1) == 1
    sin = jnp.where(swap, c, s)
    cos = jnp.where(swap, s, c)
    sin = jnp.where((quadrant & 2) == 2, -sin, sin)
    cos = jnp.where(((quadrant + 1) & 2) == 2, -cos, cos)
    return sin, cos


def table(rows, first_row, row_shift, col_shift):
    p = (lax.broadcasted_iota(jnp.int32, (rows, W), 0) + (first_row - row_shift)) & (W - 1)
    k = (lax.broadcasted_iota(jnp.int32, (rows, W), 1) - col_shift) & (W - 1)
    m = (p * k) & (W - 1)
    quadrant = (m + W // 8) >> 7
    x = (m - quadrant * (W // 4)).astype(F32) * (2.0 * math.pi / W)
    sin, cos = sine_cosine(x, quadrant)
    scaling = 1.0 / math.sqrt(W)
    return (cos * scaling).astype(BF16), (-sin * scaling).astype(BF16)


def phase_kernel(meta, phase, obj, cosine, sine):
    parts = (1.5703125, 4.837512969970703e-4, 7.549789948768648e-8)
    for first in range(0, W, B):
        rows = pl.ds(first, B)
        x = phase[rows, :]
        n = jnp.floor(x * (2.0 / math.pi) + 0.5)
        for part in parts:
            x = x - n * part
        sine[rows, :], cosine[rows, :] = sine_cosine(x, n.astype(jnp.int32))


def scalars_kernel(own, mate, far, count, odd, core, meta):
    meta[R0], meta[C0] = own[0], own[1]
    meta[PR0], meta[PC0] = mate[0], mate[1]
    meta[FR0], meta[FC0] = far[0], far[1]
    meta[LIVE], meta[ODD], meta[CORE] = count[0], odd[0], core[0]


def scalars(*operands):
    return pl.pallas_call(
        scalars_kernel,
        out_shape=jax.ShapeDtypeStruct((9,), jnp.int32),
        in_specs=[smem()] * 6,
        out_specs=smem(),
        compiler_params=params(1),
        name="scalars",
    )(*operands)


def forward_kernel(meta, probe, la, rb, q):
    r0, c0 = meta[R0], meta[C0]
    for first in range(0, W, B):
        rows = pl.ds(first, B)
        later = pl.ds(W + first, B)
        la[rows, :W], la[rows, W:] = table(B, first, 0, r0)
        rb[rows, :], rb[later, :] = table(B, first, c0, 0)
    for part in range(2):
        q[part] = pltpu.roll(pltpu.roll(probe[part], r0 & (W - 1), 0), c0 & (W - 1), 1)


def inverse_kernel(meta, lai, rbi):
    r0, c0 = meta[R0], meta[C0]
    for first in range(0, W, B):
        rows = pl.ds(first, B)
        later = pl.ds(W + first, B)
        lai[rows, :W], lai[rows, W:] = table(B, first, r0, 0)
        rbi[rows, :], rbi[later, :] = table(B, first, 0, c0)


PLANE = jax.ShapeDtypeStruct((W, W), F32)
LEFT = jax.ShapeDtypeStruct((W, 2 * W), BF16)
RIGHT = jax.ShapeDtypeStruct((2 * W, W), BF16)


def whole(kernel, name, out_shape, *operands, limit=16, **more):
    return pl.pallas_call(
        kernel,
        out_shape=out_shape,
        in_specs=[smem()] + [vmem()] * (len(operands) - 1),
        out_specs=[vmem()] * len(out_shape),
        compiler_params=params(limit),
        name=name,
        **more,
    )(*operands)


def edges_kernel(pieces, core, obj, near, wide, sem):
    far_side = pl.multiple_of((1 - core[0]) * (T - H), H)
    columns = [pl.ds(far_side, H), pl.ds(pl.multiple_of(T - H - far_side, H), H)]
    copies = []
    for rows, place in pieces:
        for out, cols in zip((near, wide), columns):
            source = obj.at[:, :, pl.ds(rows, place.size), cols]
            copies.append(pltpu.make_async_copy(source, out.at[:, :, place, :], sem.at[len(copies)]))
    for copy in copies:
        copy.start()
    for copy in copies:
        copy.wait()


def edges(shape, pieces, core, obj):
    return pl.pallas_call(
        lambda *refs: edges_kernel(pieces, *refs),
        out_shape=[shape] * 2,
        in_specs=[smem(), pl.BlockSpec(memory_space=pl.ANY)],
        out_specs=[vmem()] * 2,
        scratch_shapes=[pltpu.SemaphoreType.DMA((2 * len(pieces),))],
        compiler_params=params(56),
        name="edges",
    )(core, obj)


def by_side(meta, near, wide):
    first = meta[CORE] == 0
    return jnp.where(first, wide, near), jnp.where(first, near, wide)


def pack(tile, left, right, c0):
    shape = (tile.shape[0], H)
    middle = (tile.shape[0], W - 2 * H)
    a = jnp.where(cols_below(shape, 0, c0), tile[:, W - H : W], left)
    b = jnp.where(cols_below(middle, H, c0), tile[:, W:], tile[:, : W - 2 * H])
    c = jnp.where(cols_below(shape, W - H, c0), right, tile[:, W - 2 * H : W - H])
    return a, b, c


def put(out, rows, pieces):
    a, b, c = pieces
    out[rows, :H] = a
    out[rows, H : W - H] = b
    out[rows, W - H :] = c


def mate_takes(meta):
    upper = (meta[PR0] < HALF).astype(jnp.int32)
    return upper + meta[ODD] == 1


def far_takes(meta):
    upper = (meta[FR0] < HALF).astype(jnp.int32)
    return upper + meta[ODD] != 1


def pack_edge(meta, out, s, obj, near, wide, last, c0):
    rows = pl.ds(pl.multiple_of(last * (T - H), H), H)
    ends = pl.ds(pl.multiple_of(last * H, H), H)
    for part in range(2):
        sides = by_side(meta, near[s, part, ends, :], wide[s, part, ends, :])
        put(out.at[part], slice(None), pack(obj[s, part, rows, :], *sides, c0))


def far_kernel(s, meta, obj, near, wide, out):
    pack_edge(meta, out, s, obj, near, wide, meta[ODD], meta[FC0])


def mate_kernel(s, meta, obj, near, wide, passing, out):
    own = mate_takes(meta)

    @pl.when(own)
    def _():
        pack_edge(meta, out, s, obj, near, wide, 1 - meta[ODD], meta[PC0])

    @pl.when(jnp.logical_not(own))
    def _():
        out[...] = passing[...]


def beside_rows(meta, s, part, first, near, wide, near_ends, wide_ends):
    if first in (0, T - B):
        rows = pl.ds(min(first, H), B)
        return by_side(meta, near_ends[s, part, rows, :], wide_ends[s, part, rows, :])
    rows = pl.ds(first - H, B)
    return by_side(meta, near[s, part, rows, :], wide[s, part, rows, :])


def local_kernel(s, meta, obj, near_ends, wide_ends, near, wide, out):
    r0, c0 = meta[R0], meta[C0]
    for part in range(2):

        def packed(first):
            rows = pl.ds(first, B)
            sides = beside_rows(meta, s, part, first, near, wide, near_ends, wide_ends)
            return pack(obj[s, part, rows, :], *sides, c0)

        put(out.at[part], pl.ds(0, B), packed(W - H))
        for first in range(B, W - B, B):
            low, high = packed(first - H), packed(first + W - H)
            put(
                out.at[part],
                pl.ds(first, B),
                [jnp.where(rows_below(x.shape, first, r0), y, x) for x, y in zip(low, high)],
            )
        put(out.at[part], pl.ds(W - B, B), packed(W - B - H))


def far_strip(s, *args):
    return whole(lambda *refs: far_kernel(s, *refs), "far_strip", [STRIP], *args)[0]


def mate_strip(s, *args):
    return whole(lambda *refs: mate_kernel(s, *refs), "mate_strip", [STRIP], *args)[0]


def local_window(s, *args):
    return whole(lambda *refs: local_kernel(s, *refs), "local_window", [WINDOW], *args)[0]


def window_rows(meta, local, strip, part, first):
    x = local[part, pl.ds(first, B), :]
    if first == 0:
        x = jnp.where(rows_below(x.shape, first, meta[R0]), x, strip[part])
    if first == W - B:
        x = jnp.where(rows_below(x.shape, first, meta[R0]), strip[part], x)
    return x


def put_left(v4, first, re, im, inverse):
    re, im = re.astype(BF16), im.astype(BF16)
    rows, later = pl.ds(first, B), pl.ds(W + first, B)
    v4[rows, :W] = re
    v4[rows, W:] = im
    v4[later, :W] = im if inverse else -im
    v4[later, W:] = -re if inverse else re


def left_product(table, v4, m4, inverse):
    for first in range(0, W, W):
        rows, later = pl.ds(first, W), pl.ds(W + first, W)
        mid = jnp.dot(table[rows, :], v4[...], preferred_element_type=F32).astype(BF16)
        re, im = mid[:, :W], mid[:, W:]
        m4[rows, :W] = re
        m4[rows, W:] = im if inverse else -im
        m4[later, :W] = im
        m4[later, W:] = -re if inverse else re


def right_product(m4, table, first):
    re = jnp.dot(m4[pl.ds(first, B), :], table[...], preferred_element_type=F32)
    im = jnp.dot(m4[pl.ds(W + first, B), :], table[...], preferred_element_type=F32)
    return re, im


def first_kernel(meta, local, strip, q, kern_re, kern_im, la, lai, rb, rbi, psi, v4, m4):
    for first in range(0, W, B):
        rows = pl.ds(first, B)
        o_re = window_rows(meta, local, strip, 0, first)
        o_im = window_rows(meta, local, strip, 1, first)
        q_re, q_im = q[0, rows, :], q[1, rows, :]
        put_left(v4, first, q_re * o_re - q_im * o_im, q_re * o_im + q_im * o_re, False)
    left_product(la, v4, m4, False)
    for first in range(0, W, B):
        rows = pl.ds(first, B)
        re, im = right_product(m4, rb, first)
        k_re, k_im = kern_re[rows, :], kern_im[rows, :]
        put_left(v4, first, re * k_re - im * k_im, re * k_im + im * k_re, True)
    left_product(lai, v4, m4, True)
    for first in range(0, W, B):
        rows = pl.ds(first, B)
        psi[0, rows, :], psi[1, rows, :] = right_product(m4, rbi, first)


def edge_rows(meta, g, zg):
    keep_first = meta[R0] < HALF
    live = meta[LIVE] > 0

    @pl.when(keep_first)
    def _():
        for part in range(2):
            x = g[part, :H, :]
            hide = rows_below(x.shape, 0, meta[R0])
            zg[part] = jnp.where(jnp.logical_and(live, jnp.logical_not(hide)), x, 0.0)

    @pl.when(jnp.logical_not(keep_first))
    def _():
        for part in range(2):
            x = g[part, W - H :, :]
            show = rows_below(x.shape, W - H, meta[R0])
            zg[part] = jnp.where(jnp.logical_and(live, show), x, 0.0)


def second_kernel(meta, local, strip, psi, amp, la, lai, rb, rbi, g2, back, zg, v4, m4):
    for first in range(0, W, B):
        rows = pl.ds(first, B)
        o_re = window_rows(meta, local, strip, 0, first)
        o_im = window_rows(meta, local, strip, 1, first)
        p_re, p_im = psi[0, rows, :], psi[1, rows, :]
        put_left(v4, first, p_re * o_re - p_im * o_im, p_re * o_im + p_im * o_re, False)
    left_product(la, v4, m4, False)
    for first in range(0, W, B):
        rows = pl.ds(first, B)
        re, im = right_product(m4, rb, first)
        factor = 1.0 - amp[rows, :].astype(F32) / jnp.sqrt(re * re + im * im + 1.0)
        put_left(v4, first, re * factor, im * factor, True)
    left_product(lai, v4, m4, True)
    for first in range(0, W, B):
        rows = pl.ds(first, B)
        re, im = right_product(m4, rbi, first)
        p_re, p_im = psi[0, rows, :], psi[1, rows, :]
        g2[0, rows, :] = p_re * re + p_im * im
        g2[1, rows, :] = p_re * im - p_im * re
        o_re = window_rows(meta, local, strip, 0, first)
        o_im = window_rows(meta, local, strip, 1, first)
        back[0, rows, :] = (o_re * re + o_im * im).astype(BF16)
        back[1, rows, :] = (o_re * im - o_im * re).astype(BF16)
    edge_rows(meta, g2, zg)


def third_kernel(meta, back, q, kern_re, kern_im, la, lai, rb, rbi, g1, zg, v4, m4):
    for first in range(0, W, B):
        rows = pl.ds(first, B)
        put_left(v4, first, back[0, rows, :], back[1, rows, :], False)
    left_product(la, v4, m4, False)
    for first in range(0, W, B):
        rows = pl.ds(first, B)
        re, im = right_product(m4, rb, first)
        k_re, k_im = kern_re[rows, :], kern_im[rows, :]
        put_left(v4, first, re * k_re + im * k_im, im * k_re - re * k_im, True)
    left_product(lai, v4, m4, True)
    for first in range(0, W, B):
        rows = pl.ds(first, B)
        re, im = right_product(m4, rbi, first)
        q_re, q_im = q[0, rows, :], q[1, rows, :]
        g1[0, rows, :] = q_re * re + q_im * im
        g1[1, rows, :] = q_re * im - q_im * re
    edge_rows(meta, g1, zg)


def transforms(kernel, name, out_shape, meta, *operands):
    return pl.pallas_call(
        kernel,
        out_shape=out_shape,
        in_specs=[smem()] + [vmem()] * len(operands),
        out_specs=[vmem()] * len(out_shape),
        scratch_shapes=[pltpu.VMEM((2 * W, 2 * W), BF16), pltpu.VMEM((2 * W, 2 * W), BF16)],
        compiler_params=params(16),
        name=name,
    )(meta, *operands)


def shares(meta, part, mate, far):
    odd = meta[ODD] > 0
    mate = jnp.where(mate_takes(meta), mate[part], 0.0)
    far = jnp.where(far_takes(meta), far[part], 0.0)
    top = jnp.where(odd, mate, far)
    bottom = jnp.where(odd, far, mate)
    c_top = jnp.where(odd, meta[PC0], meta[FC0])
    c_bottom = jnp.where(odd, meta[FC0], meta[PC0])
    return (top, c_top), (bottom, c_bottom)


def left_part(x, c0):
    x = x[:, :H]
    return jnp.where(cols_below(x.shape, 0, c0), 0.0, x)


def right_part(x, c0):
    x = x[:, W - H :]
    return jnp.where(cols_below(x.shape, W - H, c0), x, 0.0)


def inner_parts(x, c0):
    low, high = x[:, H:], x[:, : W - H]
    low = jnp.where(cols_below(low.shape, H, c0), 0.0, low)
    high = jnp.where(cols_below(high.shape, 0, c0), high, 0.0)
    return low, high


def tile_rows(meta, g, part, first):
    live = meta[LIVE] > 0
    if first < W - H:
        x = g[part, pl.ds(first + H, B), :]
        hide = rows_below(x.shape, first + H, meta[R0])
        return jnp.where(jnp.logical_and(live, jnp.logical_not(hide)), x, 0.0)
    x = g[part, pl.ds(first - (W - H), B), :]
    show = rows_below(x.shape, first - (W - H), meta[R0])
    return jnp.where(jnp.logical_and(live, show), x, 0.0)


def middle_kernel(meta, g1, g2, near, wide):
    for s, g in enumerate((g1, g2)):
        for part in range(2):
            for first in range(B, T - B, B):
                x = tile_rows(meta, g, part, first)
                x = by_side(meta, left_part(x, meta[C0]), right_part(x, meta[C0]))
                rows = pl.ds(first - H, B)
                near[s, part, rows, :], wide[s, part, rows, :] = x


def corner_kernel(meta, g, mate, far, near, wide):
    for part in range(2):
        for first, (strip, c0) in zip((0, T - H), shares(meta, part, mate, far)):
            x = tile_rows(meta, g, part, first)
            a = left_part(x, meta[C0]) + left_part(strip, c0)
            b = right_part(x, meta[C0]) + right_part(strip, c0)
            rows = pl.ds(min(first, H), B)
            near[part, rows, :], wide[part, rows, :] = by_side(meta, a, b)


def own_rows(meta, g, part, first, mate, far):
    low, high = inner_parts(tile_rows(meta, g, part, first), meta[C0])
    if first in (0, T - B):
        top, bottom = shares(meta, part, mate, far)
        more = inner_parts(*(top if first == 0 else bottom))
        low, high = low + more[0], high + more[1]
    return low, high


def inner_kernel(s, meta, step, obj, g, mate, far, *rest):
    out, tile, sems = rest[-3:]
    size = step[s]
    copies = []
    for part in range(2):
        for first in range(0, T, B):
            rows = pl.ds(first, B)
            low, high = own_rows(meta, g, part, first, mate, far)
            tile[part, rows, : W - 2 * H] = obj[s, part, rows, H : W - H] - size * low[:, H:]
            tile[part, rows, W - 2 * H :] = obj[s, part, rows, W - H : T - H] - size * high[:, : W - 2 * H]
            target = out.at[s, part, rows, pl.ds(H, T - 2 * H)]
            copies.append(pltpu.make_async_copy(tile.at[part, rows, :], target, sems.at[part, first // B]))
            copies[-1].start()
    for copy in copies:
        copy.wait()


def border_kernel(s, meta, step, obj, g, mate, far, near, wide, near_ends, wide_ends, before, out, tile, sems):
    size = step[s]
    copies = []
    for part in range(2):
        for first in range(0, T, B):
            rows = pl.ds(first, B)
            low, high = own_rows(meta, g, part, first, mate, far)
            if first in (0, T - B):
                ends = pl.ds(min(first, H), B)
                received = by_side(meta, near_ends[part, ends, :], wide_ends[part, ends, :])
            else:
                received = beside_rows(meta, s, part, first, near, wide, None, None)
            for side, x in enumerate((low[:, :H], high[:, W - 2 * H :])):
                cols = pl.ds(side * (T - H), H)
                tile[side, part, rows, :] = obj[s, part, rows, cols] - size * (x + received[side])
        for side in range(2):
            target = out.at[s, part, :, pl.ds(side * (T - H), H)]
            copies.append(pltpu.make_async_copy(tile.at[side, part], target, sems.at[part, side]))
            copies[-1].start()
    for copy in copies:
        copy.wait()


def update(kernel, name, tile, sems, before, meta, step, obj, *operands):
    hbm = pl.BlockSpec(memory_space=pl.ANY)
    return pl.pallas_call(
        kernel,
        out_shape=jax.ShapeDtypeStruct(obj.shape, F32),
        in_specs=[smem()] * 2 + [vmem()] * (1 + len(operands)) + [hbm] * len(before),
        out_specs=hbm,
        scratch_shapes=[pltpu.VMEM(tile, F32), pltpu.SemaphoreType.DMA(sems)],
        input_output_aliases={3 + len(operands): 0} if before else {},
        compiler_params=params(16),
        name=name,
    )(meta, step, obj, *operands, *before)


def inner(s, before, *operands):
    kernel = lambda *refs: inner_kernel(s, *refs)
    return (update(kernel, "inner", (2, T, T - 2 * H), (2, T // B), before, *operands),)


def border(s, before, *operands):
    kernel = lambda *refs: border_kernel(s, *refs)
    return (update(kernel, "border", (2, 2, T, H), (2, 2), before, *operands),)


def per_device(object_tiles, probe, prop_phase, amplitudes, offsets, counts, step_size):
    n_rows, n_cols = lax.axis_size("rows"), lax.axis_size("cols")
    at_chip = [(i, i ^ 1) for i in range(n_cols) if i ^ 1 < n_cols]
    past_chip = [(i, i + 1) for i in range(1, n_cols - 1, 2)]
    past_chip = past_chip + [(j, i) for i, j in past_chip]
    mates = [(i, i ^ 1) for i in range(n_rows) if i ^ 1 < n_rows]
    fars = [(i, i + 1) for i in range(1, n_rows - 1, 2)]
    fars = fars + [(j, i) for i, j in fars]
    inward = [(i, i - 2) for i in range(2, n_rows, 2)] + [(i, i + 2) for i in range(1, n_rows - 2, 2)]
    outward = [(j, i) for i, j in inward]

    own = offsets.reshape(2)
    parity = lambda axis: lax.axis_index(axis).astype(jnp.int32).reshape(1) & 1
    odd, core = parity("rows"), parity("cols")
    after = lambda *values: lax.optimization_barrier(values)

    far, passing, strip, local = [[None, None] for _ in range(4)]

    def beside_cols(near, wide):
        wide = lax.ppermute(wide, "cols", past_chip)
        return lax.ppermute(near, "cols", at_chip), wide

    pieces = [(0, pl.ds(0, H)), (T - H, pl.ds(H, H))]
    first, obj, count, odd, *sent = after(
        own, object_tiles, counts.reshape(1), odd, *edges(ENDS, pieces, core, object_tiles)
    )
    beside = [lax.ppermute(first, "rows", mates), lax.ppermute(first, "rows", fars)]
    ends = beside_cols(*sent)
    first, *sent = after(first, *edges(MIDDLE, [(H, pl.ds(0, T - 2 * H))], core, obj))
    middle_wide = lax.ppermute(sent[1], "cols", past_chip)
    kernel = whole(phase_kernel, "phase", [PLANE, PLANE], first, prop_phase, object_tiles)
    first, *kernel = after(first, *kernel)
    meta = scalars(first, *beside, count, odd, core)
    middle_near, _ = after(sent[0], meta)
    middle = lax.ppermute(middle_near, "cols", at_chip), middle_wide

    for s in range(2):
        far[s] = far_strip(s, meta, object_tiles, *ends)
        passing[s] = lax.ppermute(far[s], "rows", inward)
    third, _ = after(meta, far[1])
    lai, rbi = whole(inverse_kernel, "inverse_tables", [LEFT, RIGHT], third)
    la, rb, q = whole(forward_kernel, "forward_tables", [LEFT, RIGHT, WINDOW], third, probe)
    passing[0], la, rb, q, lai, rbi, *middle = after(passing[0], la, rb, q, lai, rbi, *middle)
    strip[0] = lax.ppermute(mate_strip(0, meta, object_tiles, *ends, passing[0]), "rows", mates)
    local[0] = local_window(0, meta, object_tiles, *ends, *middle)
    local[1] = local_window(1, meta, object_tiles, *ends, *middle)
    strip[1] = lax.ppermute(mate_strip(1, meta, object_tiles, *ends, passing[1]), "rows", mates)
    tables = (la, lai, rb, rbi)

    (psi,) = transforms(first_kernel, "first", [WINDOW], meta, local[0], strip[0], q, *kernel, *tables)
    g2, back, z2 = transforms(
        second_kernel,
        "second",
        [WINDOW, jax.ShapeDtypeStruct((2, W, W), BF16), STRIP],
        meta,
        local[1],
        strip[1],
        psi,
        amplitudes[0, 0, 0],
        *tables,
    )
    g1, z1 = transforms(third_kernel, "third", [WINDOW, STRIP], meta, back, q, *kernel, *tables)

    mate, far, ends = [None, None], [None, None], [None, None]
    mate[1] = lax.ppermute(z2, "rows", mates)
    mate[0] = lax.ppermute(z1, "rows", mates)
    far[1] = lax.ppermute(mate[1], "rows", outward)
    _, *sent = after(mate[1], *whole(middle_kernel, "middle", [MIDDLE] * 2, meta, g1, g2))
    middle = beside_cols(*sent)
    far[0] = lax.ppermute(mate[0], "rows", outward)
    grads = (g1, g2)
    out = ()
    for s in (1, 0):
        shape = jax.ShapeDtypeStruct(ENDS.shape[1:], F32)
        sent = whole(corner_kernel, "corner", [shape] * 2, meta, grads[s], mate[s], far[s])
        ends[s] = beside_cols(*sent)
    for s in (1, 0):
        out = inner(s, out, meta, step_size, object_tiles, grads[s], mate[s], far[s])
    for s in (1, 0):
        out = border(s, out, meta, step_size, object_tiles, grads[s], mate[s], far[s], *middle, *ends[s])
    return out[0]


def solution(mesh):
    return jax.shard_map(
        per_device,
        mesh=mesh,
        in_specs=(
            P(None, None, "rows", "cols"),
            P(),
            P(),
            P("rows", "cols", None, None, None),
            P("rows", "cols", None, None),
            P("rows", "cols"),
            P(),
        ),
        out_specs=P(None, None, "rows", "cols"),
        check_vma=False,
    )
```

```python
import math

import jax
import jax.numpy as jnp
from jax import lax
from jax.experimental import pallas as pl
from jax.experimental.pallas import tpu as pltpu
from jax.sharding import PartitionSpec as P

H = 128
W = 512
T = 768
B = 128
HALF = W // 2
LAST = T // H - 1
R0, C0, PR0, PC0, FR0, FC0, LIVE, ODD, CORE = range(9)

F32, BF16 = jnp.float32, jnp.bfloat16
WINDOW = jax.ShapeDtypeStruct((2, W, W), F32)
STRIP = jax.ShapeDtypeStruct((2, H, W), F32)
ENDS = jax.ShapeDtypeStruct((2, 2, 2 * H, H), F32)
MIDDLE = jax.ShapeDtypeStruct((2, 2, T - 2 * H, H), F32)


def rows_below(shape, first, limit):
    return lax.broadcasted_iota(jnp.int32, shape, 0) + first < limit


def cols_below(shape, first, limit):
    return lax.broadcasted_iota(jnp.int32, shape, 1) + first < limit


def params(limit_mib):
    return pltpu.CompilerParams(vmem_limit_bytes=limit_mib << 20)


def vmem():
    return pl.BlockSpec(memory_space=pltpu.VMEM)


def smem():
    return pl.BlockSpec(memory_space=pltpu.SMEM)


def sine_cosine(x, quadrant):
    y = x * x
    s = x * (1.0 + y * (-1.0 / 6 + y * (1.0 / 120 + y * (-1.0 / 5040 + y * (1.0 / 362880)))))
    c = 1.0 + y * (-0.5 + y * (1.0 / 24 + y * (-1.0 / 720 + y * (1.0 / 40320 - y * (1.0 / 3628800)))))
    swap = (quadrant & 1) == 1
    sin = jnp.where(swap, c, s)
    cos = jnp.where(swap, s, c)
    sin = jnp.where((quadrant & 2) == 2, -sin, sin)
    cos = jnp.where(((quadrant + 1) & 2) == 2, -cos, cos)
    return sin, cos


def table(rows, first_row, row_shift, col_shift):
    p = (lax.broadcasted_iota(jnp.int32, (rows, W), 0) + (first_row - row_shift)) & (W - 1)
    k = (lax.broadcasted_iota(jnp.int32, (rows, W), 1) - col_shift) & (W - 1)
    m = (p * k) & (W - 1)
    quadrant = (m + W // 8) >> 7
    x = (m - quadrant * (W // 4)).astype(F32) * (2.0 * math.pi / W)
    sin, cos = sine_cosine(x, quadrant)
    scaling = 1.0 / math.sqrt(W)
    return (cos * scaling).astype(BF16), (-sin * scaling).astype(BF16)


def phase_kernel(meta, phase, obj, cosine, sine):
    parts = (1.5703125, 4.837512969970703e-4, 7.549789948768648e-8)
    for first in range(0, W, B):
        rows = pl.ds(first, B)
        x = phase[rows, :]
        n = jnp.floor(x * (2.0 / math.pi) + 0.5)
        for part in parts:
            x = x - n * part
        sine[rows, :], cosine[rows, :] = sine_cosine(x, n.astype(jnp.int32))


def scalars_kernel(own, mate, far, count, odd, core, meta):
    meta[R0], meta[C0] = own[0], own[1]
    meta[PR0], meta[PC0] = mate[0], mate[1]
    meta[FR0], meta[FC0] = far[0], far[1]
    meta[LIVE], meta[ODD], meta[CORE] = count[0], odd[0], core[0]


def scalars(*operands):
    return pl.pallas_call(
        scalars_kernel,
        out_shape=jax.ShapeDtypeStruct((9,), jnp.int32),
        in_specs=[smem()] * 6,
        out_specs=smem(),
        compiler_params=params(1),
        name="scalars",
    )(*operands)


def forward_kernel(meta, probe, la, rb, q):
    r0, c0 = meta[R0], meta[C0]
    for first in range(0, W, B):
        rows = pl.ds(first, B)
        later = pl.ds(W + first, B)
        la[rows, :W], la[rows, W:] = table(B, first, 0, r0)
        rb[rows, :], rb[later, :] = table(B, first, c0, 0)
    for part in range(2):
        q[part] = pltpu.roll(pltpu.roll(probe[part], r0 & (W - 1), 0), c0 & (W - 1), 1)


def inverse_kernel(meta, lai, rbi):
    r0, c0 = meta[R0], meta[C0]
    for first in range(0, W, B):
        rows = pl.ds(first, B)
        later = pl.ds(W + first, B)
        lai[rows, :W], lai[rows, W:] = table(B, first, r0, 0)
        rbi[rows, :], rbi[later, :] = table(B, first, 0, c0)


PLANE = jax.ShapeDtypeStruct((W, W), F32)
LEFT = jax.ShapeDtypeStruct((W, 2 * W), BF16)
RIGHT = jax.ShapeDtypeStruct((2 * W, W), BF16)


def whole(kernel, name, out_shape, *operands, limit=16, **more):
    return pl.pallas_call(
        kernel,
        out_shape=out_shape,
        in_specs=[smem()] + [vmem()] * (len(operands) - 1),
        out_specs=[vmem()] * len(out_shape),
        compiler_params=params(limit),
        name=name,
        **more,
    )(*operands)


def edges_kernel(pieces, core, obj, near, wide, sem):
    far_side = pl.multiple_of((1 - core[0]) * (T - H), H)
    columns = [pl.ds(far_side, H), pl.ds(pl.multiple_of(T - H - far_side, H), H)]
    copies = []
    for rows, place in pieces:
        for out, cols in zip((near, wide), columns):
            source = obj.at[:, :, pl.ds(rows, place.size), cols]
            copies.append(pltpu.make_async_copy(source, out.at[:, :, place, :], sem.at[len(copies)]))
    for copy in copies:
        copy.start()
    for copy in copies:
        copy.wait()


def edges(shape, pieces, core, obj):
    return pl.pallas_call(
        lambda *refs: edges_kernel(pieces, *refs),
        out_shape=[shape] * 2,
        in_specs=[smem(), pl.BlockSpec(memory_space=pl.ANY)],
        out_specs=[vmem()] * 2,
        scratch_shapes=[pltpu.SemaphoreType.DMA((2 * len(pieces),))],
        compiler_params=params(56),
        name="edges",
    )(core, obj)


def by_side(meta, near, wide):
    first = meta[CORE] == 0
    return jnp.where(first, wide, near), jnp.where(first, near, wide)


def pack(tile, left, right, c0):
    shape = (tile.shape[0], H)
    middle = (tile.shape[0], W - 2 * H)
    a = jnp.where(cols_below(shape, 0, c0), tile[:, W - H : W], left)
    b = jnp.where(cols_below(middle, H, c0), tile[:, W:], tile[:, : W - 2 * H])
    c = jnp.where(cols_below(shape, W - H, c0), right, tile[:, W - 2 * H : W - H])
    return a, b, c


def put(out, rows, pieces):
    a, b, c = pieces
    out[rows, :H] = a
    out[rows, H : W - H] = b
    out[rows, W - H :] = c


def mate_takes(meta):
    upper = (meta[PR0] < HALF).astype(jnp.int32)
    return upper + meta[ODD] == 1


def far_takes(meta):
    upper = (meta[FR0] < HALF).astype(jnp.int32)
    return upper + meta[ODD] != 1


def pack_edge(meta, out, s, obj, near, wide, last, c0):
    rows = pl.ds(pl.multiple_of(last * (T - H), H), H)
    ends = pl.ds(pl.multiple_of(last * H, H), H)
    for part in range(2):
        sides = by_side(meta, near[s, part, ends, :], wide[s, part, ends, :])
        put(out.at[part], slice(None), pack(obj[s, part, rows, :], *sides, c0))


def far_kernel(s, meta, obj, near, wide, out):
    pack_edge(meta, out, s, obj, near, wide, meta[ODD], meta[FC0])


def mate_kernel(s, meta, obj, near, wide, passing, out):
    own = mate_takes(meta)

    @pl.when(own)
    def _():
        pack_edge(meta, out, s, obj, near, wide, 1 - meta[ODD], meta[PC0])

    @pl.when(jnp.logical_not(own))
    def _():
        out[...] = passing[...]


def beside_rows(meta, s, part, first, near, wide, near_ends, wide_ends):
    if first in (0, T - B):
        rows = pl.ds(min(first, H), B)
        return by_side(meta, near_ends[s, part, rows, :], wide_ends[s, part, rows, :])
    rows = pl.ds(first - H, B)
    return by_side(meta, near[s, part, rows, :], wide[s, part, rows, :])


def local_kernel(s, meta, obj, near_ends, wide_ends, near, wide, out):
    r0, c0 = meta[R0], meta[C0]
    for part in range(2):

        def packed(first):
            rows = pl.ds(first, B)
            sides = beside_rows(meta, s, part, first, near, wide, near_ends, wide_ends)
            return pack(obj[s, part, rows, :], *sides, c0)

        put(out.at[part], pl.ds(0, B), packed(W - H))
        for first in range(B, W - B, B):
            low, high = packed(first - H), packed(first + W - H)
            put(
                out.at[part],
                pl.ds(first, B),
                [jnp.where(rows_below(x.shape, first, r0), y, x) for x, y in zip(low, high)],
            )
        put(out.at[part], pl.ds(W - B, B), packed(W - B - H))


def far_strip(s, *args):
    return whole(lambda *refs: far_kernel(s, *refs), "far_strip", [STRIP], *args)[0]


def mate_strip(s, *args):
    return whole(lambda *refs: mate_kernel(s, *refs), "mate_strip", [STRIP], *args)[0]


def local_window(s, *args):
    return whole(lambda *refs: local_kernel(s, *refs), "local_window", [WINDOW], *args)[0]


def window_rows(meta, local, strip, part, first):
    x = local[part, pl.ds(first, B), :]
    if first == 0:
        x = jnp.where(rows_below(x.shape, first, meta[R0]), x, strip[part])
    if first == W - B:
        x = jnp.where(rows_below(x.shape, first, meta[R0]), strip[part], x)
    return x


def put_left(v4, first, re, im, inverse):
    re, im = re.astype(BF16), im.astype(BF16)
    rows, later = pl.ds(first, B), pl.ds(W + first, B)
    v4[rows, :W] = re
    v4[rows, W:] = im
    v4[later, :W] = im if inverse else -im
    v4[later, W:] = -re if inverse else re


def left_product(table, v4, m4, inverse):
    for first in range(0, W, W):
        rows, later = pl.ds(first, W), pl.ds(W + first, W)
        mid = jnp.dot(table[rows, :], v4[...], preferred_element_type=F32).astype(BF16)
        re, im = mid[:, :W], mid[:, W:]
        m4[rows, :W] = re
        m4[rows, W:] = im if inverse else -im
        m4[later, :W] = im
        m4[later, W:] = -re if inverse else re


def right_product(m4, table, first):
    re = jnp.dot(m4[pl.ds(first, B), :], table[...], preferred_element_type=F32)
    im = jnp.dot(m4[pl.ds(W + first, B), :], table[...], preferred_element_type=F32)
    return re, im


def first_kernel(meta, local, strip, q, kern_re, kern_im, la, lai, rb, rbi, psi, v4, m4):
    for first in range(0, W, B):
        rows = pl.ds(first, B)
        o_re = window_rows(meta, local, strip, 0, first)
        o_im = window_rows(meta, local, strip, 1, first)
        q_re, q_im = q[0, rows, :], q[1, rows, :]
        put_left(v4, first, q_re * o_re - q_im * o_im, q_re * o_im + q_im * o_re, False)
    left_product(la, v4, m4, False)
    for first in range(0, W, B):
        rows = pl.ds(first, B)
        re, im = right_product(m4, rb, first)
        k_re, k_im = kern_re[rows, :], kern_im[rows, :]
        put_left(v4, first, re * k_re - im * k_im, re * k_im + im * k_re, True)
    left_product(lai, v4, m4, True)
    for first in range(0, W, B):
        rows = pl.ds(first, B)
        psi[0, rows, :], psi[1, rows, :] = right_product(m4, rbi, first)


def edge_rows(meta, g, zg):
    keep_first = meta[R0] < HALF
    live = meta[LIVE] > 0

    @pl.when(keep_first)
    def _():
        for part in range(2):
            x = g[part, :H, :]
            hide = rows_below(x.shape, 0, meta[R0])
            zg[part] = jnp.where(jnp.logical_and(live, jnp.logical_not(hide)), x, 0.0)

    @pl.when(jnp.logical_not(keep_first))
    def _():
        for part in range(2):
            x = g[part, W - H :, :]
            show = rows_below(x.shape, W - H, meta[R0])
            zg[part] = jnp.where(jnp.logical_and(live, show), x, 0.0)


def second_kernel(meta, local, strip, psi, amp, la, lai, rb, rbi, m4, zg, v4):
    for first in range(0, W, B):
        rows = pl.ds(first, B)
        o_re = window_rows(meta, local, strip, 0, first)
        o_im = window_rows(meta, local, strip, 1, first)
        p_re, p_im = psi[0, rows, :], psi[1, rows, :]
        put_left(v4, first, p_re * o_re - p_im * o_im, p_re * o_im + p_im * o_re, False)
    left_product(la, v4, m4, False)
    for first in range(0, W, B):
        rows = pl.ds(first, B)
        re, im = right_product(m4, rb, first)
        factor = 1.0 - amp[rows, :].astype(F32) / jnp.sqrt(re * re + im * im + 1.0)
        put_left(v4, first, re * factor, im * factor, True)
    left_product(lai, v4, m4, True)
    upper = meta[R0] < HALF
    first = pl.multiple_of(jnp.where(upper, 0, W - B), B)
    rows = pl.ds(first, B)
    re, im = right_product(m4, rbi, first)
    p_re, p_im = psi[0, rows, :], psi[1, rows, :]
    below = rows_below(re.shape, first, meta[R0]).astype(jnp.int32)
    leaves = jnp.logical_and(below + upper.astype(jnp.int32) == 1, meta[LIVE] > 0)
    zg[0] = jnp.where(leaves, p_re * re + p_im * im, 0.0)
    zg[1] = jnp.where(leaves, p_re * im - p_im * re, 0.0)


def third_kernel(meta, mid, local, strip, psi, q, kern_re, kern_im, la, lai, rb, rbi, g2, g1, zg, v4, m4):
    for first in range(0, W, B):
        rows = pl.ds(first, B)
        re, im = right_product(mid, rbi, first)
        p_re, p_im = psi[0, rows, :], psi[1, rows, :]
        g2[0, rows, :] = p_re * re + p_im * im
        g2[1, rows, :] = p_re * im - p_im * re
        o_re = window_rows(meta, local, strip, 0, first)
        o_im = window_rows(meta, local, strip, 1, first)
        put_left(v4, first, o_re * re + o_im * im, o_re * im - o_im * re, False)
    left_product(la, v4, m4, False)
    for first in range(0, W, B):
        rows = pl.ds(first, B)
        re, im = right_product(m4, rb, first)
        k_re, k_im = kern_re[rows, :], kern_im[rows, :]
        put_left(v4, first, re * k_re + im * k_im, im * k_re - re * k_im, True)
    left_product(lai, v4, m4, True)
    for first in range(0, W, B):
        rows = pl.ds(first, B)
        re, im = right_product(m4, rbi, first)
        q_re, q_im = q[0, rows, :], q[1, rows, :]
        g1[0, rows, :] = q_re * re + q_im * im
        g1[1, rows, :] = q_re * im - q_im * re
    edge_rows(meta, g1, zg)


def transforms(kernel, name, out_shape, meta, *operands, scratch=2):
    return pl.pallas_call(
        kernel,
        out_shape=out_shape,
        in_specs=[smem()] + [vmem()] * len(operands),
        out_specs=[vmem()] * len(out_shape),
        scratch_shapes=[pltpu.VMEM((2 * W, 2 * W), BF16)] * scratch,
        compiler_params=params(16),
        name=name,
    )(meta, *operands)


def shares(meta, part, mate, far):
    odd = meta[ODD] > 0
    mate = jnp.where(mate_takes(meta), mate[part], 0.0)
    far = jnp.where(far_takes(meta), far[part], 0.0)
    top = jnp.where(odd, mate, far)
    bottom = jnp.where(odd, far, mate)
    c_top = jnp.where(odd, meta[PC0], meta[FC0])
    c_bottom = jnp.where(odd, meta[FC0], meta[PC0])
    return (top, c_top), (bottom, c_bottom)


def left_part(x, c0):
    x = x[:, :H]
    return jnp.where(cols_below(x.shape, 0, c0), 0.0, x)


def right_part(x, c0):
    x = x[:, W - H :]
    return jnp.where(cols_below(x.shape, W - H, c0), x, 0.0)


def inner_parts(x, c0):
    low, high = x[:, H:], x[:, : W - H]
    low = jnp.where(cols_below(low.shape, H, c0), 0.0, low)
    high = jnp.where(cols_below(high.shape, 0, c0), high, 0.0)
    return low, high


def tile_rows(meta, g, part, first):
    live = meta[LIVE] > 0
    if first < W - H:
        x = g[part, pl.ds(first + H, B), :]
        hide = rows_below(x.shape, first + H, meta[R0])
        return jnp.where(jnp.logical_and(live, jnp.logical_not(hide)), x, 0.0)
    x = g[part, pl.ds(first - (W - H), B), :]
    show = rows_below(x.shape, first - (W - H), meta[R0])
    return jnp.where(jnp.logical_and(live, show), x, 0.0)


def middle_kernel(meta, g1, g2, near, wide):
    for s, g in enumerate((g1, g2)):
        for part in range(2):
            for first in range(B, T - B, B):
                x = tile_rows(meta, g, part, first)
                x = by_side(meta, left_part(x, meta[C0]), right_part(x, meta[C0]))
                rows = pl.ds(first - H, B)
                near[s, part, rows, :], wide[s, part, rows, :] = x


def corner_kernel(meta, g, mate, far, near, wide):
    for part in range(2):
        for first, (strip, c0) in zip((0, T - H), shares(meta, part, mate, far)):
            x = tile_rows(meta, g, part, first)
            a = left_part(x, meta[C0]) + left_part(strip, c0)
            b = right_part(x, meta[C0]) + right_part(strip, c0)
            rows = pl.ds(min(first, H), B)
            near[part, rows, :], wide[part, rows, :] = by_side(meta, a, b)


def own_rows(meta, g, part, first, mate, far):
    low, high = inner_parts(tile_rows(meta, g, part, first), meta[C0])
    if first in (0, T - B):
        top, bottom = shares(meta, part, mate, far)
        more = inner_parts(*(top if first == 0 else bottom))
        low, high = low + more[0], high + more[1]
    return low, high


def inner_kernel(s, meta, step, obj, g, mate, far, *rest):
    out, tile, sems = rest[-3:]
    size = step[s]
    copies = []
    for part in range(2):
        for first in range(0, T, B):
            rows = pl.ds(first, B)
            low, high = own_rows(meta, g, part, first, mate, far)
            tile[part, rows, : W - 2 * H] = obj[s, part, rows, H : W - H] - size * low[:, H:]
            tile[part, rows, W - 2 * H :] = obj[s, part, rows, W - H : T - H] - size * high[:, : W - 2 * H]
            target = out.at[s, part, rows, pl.ds(H, T - 2 * H)]
            copies.append(pltpu.make_async_copy(tile.at[part, rows, :], target, sems.at[part, first // B]))
            copies[-1].start()
    for copy in copies:
        copy.wait()


def border_kernel(s, meta, step, obj, g, mate, far, near, wide, near_ends, wide_ends, before, out, tile, sems):
    size = step[s]
    copies = []
    for part in range(2):
        for first in range(0, T, B):
            rows = pl.ds(first, B)
            low, high = own_rows(meta, g, part, first, mate, far)
            if first in (0, T - B):
                ends = pl.ds(min(first, H), B)
                received = by_side(meta, near_ends[part, ends, :], wide_ends[part, ends, :])
            else:
                received = beside_rows(meta, s, part, first, near, wide, None, None)
            for side, x in enumerate((low[:, :H], high[:, W - 2 * H :])):
                cols = pl.ds(side * (T - H), H)
                tile[side, part, rows, :] = obj[s, part, rows, cols] - size * (x + received[side])
        for side in range(2):
            target = out.at[s, part, :, pl.ds(side * (T - H), H)]
            copies.append(pltpu.make_async_copy(tile.at[side, part], target, sems.at[part, side]))
            copies[-1].start()
    for copy in copies:
        copy.wait()


def update(kernel, name, tile, sems, before, meta, step, obj, *operands):
    hbm = pl.BlockSpec(memory_space=pl.ANY)
    return pl.pallas_call(
        kernel,
        out_shape=jax.ShapeDtypeStruct(obj.shape, F32),
        in_specs=[smem()] * 2 + [vmem()] * (1 + len(operands)) + [hbm] * len(before),
        out_specs=hbm,
        scratch_shapes=[pltpu.VMEM(tile, F32), pltpu.SemaphoreType.DMA(sems)],
        input_output_aliases={3 + len(operands): 0} if before else {},
        compiler_params=params(16),
        name=name,
    )(meta, step, obj, *operands, *before)


def inner(s, before, *operands):
    kernel = lambda *refs: inner_kernel(s, *refs)
    return (update(kernel, "inner", (2, T, T - 2 * H), (2, T // B), before, *operands),)


def border(s, before, *operands):
    kernel = lambda *refs: border_kernel(s, *refs)
    return (update(kernel, "border", (2, 2, T, H), (2, 2), before, *operands),)


def per_device(object_tiles, probe, prop_phase, amplitudes, offsets, counts, step_size):
    n_rows, n_cols = lax.axis_size("rows"), lax.axis_size("cols")
    at_chip = [(i, i ^ 1) for i in range(n_cols) if i ^ 1 < n_cols]
    past_chip = [(i, i + 1) for i in range(1, n_cols - 1, 2)]
    past_chip = past_chip + [(j, i) for i, j in past_chip]
    mates = [(i, i ^ 1) for i in range(n_rows) if i ^ 1 < n_rows]
    fars = [(i, i + 1) for i in range(1, n_rows - 1, 2)]
    fars = fars + [(j, i) for i, j in fars]
    inward = [(i, i - 2) for i in range(2, n_rows, 2)] + [(i, i + 2) for i in range(1, n_rows - 2, 2)]
    outward = [(j, i) for i, j in inward]

    own = offsets.reshape(2)
    parity = lambda axis: lax.axis_index(axis).astype(jnp.int32).reshape(1) & 1
    odd, core = parity("rows"), parity("cols")
    after = lambda *values: lax.optimization_barrier(values)

    far, passing, strip, local = [[None, None] for _ in range(4)]

    def beside_cols(near, wide):
        wide = lax.ppermute(wide, "cols", past_chip)
        return lax.ppermute(near, "cols", at_chip), wide

    pieces = [(0, pl.ds(0, H)), (T - H, pl.ds(H, H))]
    first, obj, count, odd, *sent = after(
        own, object_tiles, counts.reshape(1), odd, *edges(ENDS, pieces, core, object_tiles)
    )
    beside = [lax.ppermute(first, "rows", mates), lax.ppermute(first, "rows", fars)]
    ends = beside_cols(*sent)
    first, *sent = after(first, *edges(MIDDLE, [(H, pl.ds(0, T - 2 * H))], core, obj))
    middle_wide = lax.ppermute(sent[1], "cols", past_chip)
    kernel = whole(phase_kernel, "phase", [PLANE, PLANE], first, prop_phase, object_tiles)
    first, *kernel = after(first, *kernel)
    meta = scalars(first, *beside, count, odd, core)
    middle_near, _ = after(sent[0], meta)
    middle = lax.ppermute(middle_near, "cols", at_chip), middle_wide

    for s in range(2):
        far[s] = far_strip(s, meta, object_tiles, *ends)
        passing[s] = lax.ppermute(far[s], "rows", inward)
    third, _ = after(meta, far[1])
    lai, rbi = whole(inverse_kernel, "inverse_tables", [LEFT, RIGHT], third)
    la, rb, q = whole(forward_kernel, "forward_tables", [LEFT, RIGHT, WINDOW], third, probe)
    passing[0], la, rb, q, lai, rbi, *middle = after(passing[0], la, rb, q, lai, rbi, *middle)
    strip[0] = lax.ppermute(mate_strip(0, meta, object_tiles, *ends, passing[0]), "rows", mates)
    local[0] = local_window(0, meta, object_tiles, *ends, *middle)
    local[1] = local_window(1, meta, object_tiles, *ends, *middle)
    strip[1] = lax.ppermute(mate_strip(1, meta, object_tiles, *ends, passing[1]), "rows", mates)
    tables = (la, lai, rb, rbi)

    (psi,) = transforms(first_kernel, "first", [WINDOW], meta, local[0], strip[0], q, *kernel, *tables)
    mid, z2 = transforms(
        second_kernel,
        "second",
        [jax.ShapeDtypeStruct((2 * W, 2 * W), BF16), STRIP],
        meta,
        local[1],
        strip[1],
        psi,
        amplitudes[0, 0, 0],
        *tables,
        scratch=1,
    )
    g2, g1, z1 = transforms(
        third_kernel, "third", [WINDOW, WINDOW, STRIP], meta, mid, local[1], strip[1], psi, q, *kernel, *tables
    )

    mate, far, ends = [None, None], [None, None], [None, None]
    mate[1] = lax.ppermute(z2, "rows", mates)
    mate[0] = lax.ppermute(z1, "rows", mates)
    far[1] = lax.ppermute(mate[1], "rows", outward)
    _, *sent = after(mate[1], *whole(middle_kernel, "middle", [MIDDLE] * 2, meta, g1, g2))
    middle = beside_cols(*sent)
    far[0] = lax.ppermute(mate[0], "rows", outward)
    grads = (g1, g2)
    out = ()
    for s in (1, 0):
        shape = jax.ShapeDtypeStruct(ENDS.shape[1:], F32)
        sent = whole(corner_kernel, "corner", [shape] * 2, meta, grads[s], mate[s], far[s])
        ends[s] = beside_cols(*sent)
    for s in (1, 0):
        out = inner(s, out, meta, step_size, object_tiles, grads[s], mate[s], far[s])
    for s in (1, 0):
        out = border(s, out, meta, step_size, object_tiles, grads[s], mate[s], far[s], *middle, *ends[s])
    return out[0]


def solution(mesh):
    return jax.shard_map(
        per_device,
        mesh=mesh,
        in_specs=(
            P(None, None, "rows", "cols"),
            P(),
            P(),
            P("rows", "cols", None, None, None),
            P("rows", "cols", None, None),
            P("rows", "cols"),
            P(),
        ),
        out_specs=P(None, None, "rows", "cols"),
        check_vma=False,
    )
```

```python
import math

import jax
import jax.numpy as jnp
from jax import lax
from jax.experimental import pallas as pl
from jax.experimental.pallas import tpu as pltpu
from jax.sharding import PartitionSpec as P

H = 128
W = 512
T = 768
B = 128
HALF = W // 2
LAST = T // H - 1
R0, C0, PR0, PC0, FR0, FC0, LIVE, ODD, CORE = range(9)

F32, BF16 = jnp.float32, jnp.bfloat16
WINDOW = jax.ShapeDtypeStruct((2, W, W), F32)
STRIP = jax.ShapeDtypeStruct((2, H, W), F32)
ENDS = jax.ShapeDtypeStruct((2, 2, 2 * H, H), F32)
MIDDLE = jax.ShapeDtypeStruct((2, 2, T - 2 * H, H), F32)


def rows_below(shape, first, limit):
    return lax.broadcasted_iota(jnp.int32, shape, 0) + first < limit


def cols_below(shape, first, limit):
    return lax.broadcasted_iota(jnp.int32, shape, 1) + first < limit


def params(limit_mib):
    return pltpu.CompilerParams(vmem_limit_bytes=limit_mib << 20)


def vmem():
    return pl.BlockSpec(memory_space=pltpu.VMEM)


def smem():
    return pl.BlockSpec(memory_space=pltpu.SMEM)


def sine_cosine(x, quadrant):
    y = x * x
    s = x * (1.0 + y * (-1.0 / 6 + y * (1.0 / 120 + y * (-1.0 / 5040 + y * (1.0 / 362880)))))
    c = 1.0 + y * (-0.5 + y * (1.0 / 24 + y * (-1.0 / 720 + y * (1.0 / 40320 - y * (1.0 / 3628800)))))
    swap = (quadrant & 1) == 1
    sin = jnp.where(swap, c, s)
    cos = jnp.where(swap, s, c)
    sin = jnp.where((quadrant & 2) == 2, -sin, sin)
    cos = jnp.where(((quadrant + 1) & 2) == 2, -cos, cos)
    return sin, cos


def table(rows, first_row, row_shift, col_shift):
    p = (lax.broadcasted_iota(jnp.int32, (rows, W), 0) + (first_row - row_shift)) & (W - 1)
    k = (lax.broadcasted_iota(jnp.int32, (rows, W), 1) - col_shift) & (W - 1)
    m = (p * k) & (W - 1)
    quadrant = (m + W // 8) >> 7
    x = (m - quadrant * (W // 4)).astype(F32) * (2.0 * math.pi / W)
    sin, cos = sine_cosine(x, quadrant)
    scaling = 1.0 / math.sqrt(W)
    return (cos * scaling).astype(BF16), (-sin * scaling).astype(BF16)


def phase_kernel(meta, phase, obj, cosine, sine):
    parts = (1.5703125, 4.837512969970703e-4, 7.549789948768648e-8)
    for first in range(0, W, B):
        rows = pl.ds(first, B)
        x = phase[rows, :]
        n = jnp.floor(x * (2.0 / math.pi) + 0.5)
        for part in parts:
            x = x - n * part
        sine[rows, :], cosine[rows, :] = sine_cosine(x, n.astype(jnp.int32))


def scalars_kernel(own, mate, far, count, odd, core, meta):
    meta[R0], meta[C0] = own[0], own[1]
    meta[PR0], meta[PC0] = mate[0], mate[1]
    meta[FR0], meta[FC0] = far[0], far[1]
    meta[LIVE], meta[ODD], meta[CORE] = count[0], odd[0], core[0]


def scalars(*operands):
    return pl.pallas_call(
        scalars_kernel,
        out_shape=jax.ShapeDtypeStruct((9,), jnp.int32),
        in_specs=[smem()] * 6,
        out_specs=smem(),
        compiler_params=params(1),
        name="scalars",
    )(*operands)


def forward_kernel(meta, probe, la, rb, q):
    r0, c0 = meta[R0], meta[C0]
    for first in range(0, W, B):
        rows = pl.ds(first, B)
        later = pl.ds(W + first, B)
        la[rows, :W], la[rows, W:] = table(B, first, 0, r0)
        rb[rows, :], rb[later, :] = table(B, first, c0, 0)
    for part in range(2):
        q[part] = pltpu.roll(pltpu.roll(probe[part], r0 & (W - 1), 0), c0 & (W - 1), 1)


def inverse_kernel(meta, lai, rbi):
    r0, c0 = meta[R0], meta[C0]
    for first in range(0, W, B):
        rows = pl.ds(first, B)
        later = pl.ds(W + first, B)
        lai[rows, :W], lai[rows, W:] = table(B, first, r0, 0)
        rbi[rows, :], rbi[later, :] = table(B, first, 0, c0)


PLANE = jax.ShapeDtypeStruct((W, W), F32)
LEFT = jax.ShapeDtypeStruct((W, 2 * W), BF16)
RIGHT = jax.ShapeDtypeStruct((2 * W, W), BF16)


def whole(kernel, name, out_shape, *operands, limit=16, **more):
    return pl.pallas_call(
        kernel,
        out_shape=out_shape,
        in_specs=[smem()] + [vmem()] * (len(operands) - 1),
        out_specs=[vmem()] * len(out_shape),
        compiler_params=params(limit),
        name=name,
        **more,
    )(*operands)


def edges_kernel(pieces, core, obj, near, wide, sem):
    far_side = pl.multiple_of((1 - core[0]) * (T - H), H)
    columns = [pl.ds(far_side, H), pl.ds(pl.multiple_of(T - H - far_side, H), H)]
    copies = []
    for rows, place in pieces:
        for out, cols in zip((near, wide), columns):
            source = obj.at[:, :, pl.ds(rows, place.size), cols]
            copies.append(pltpu.make_async_copy(source, out.at[:, :, place, :], sem.at[len(copies)]))
    for copy in copies:
        copy.start()
    for copy in copies:
        copy.wait()


def edges(shape, pieces, core, obj):
    return pl.pallas_call(
        lambda *refs: edges_kernel(pieces, *refs),
        out_shape=[shape] * 2,
        in_specs=[smem(), pl.BlockSpec(memory_space=pl.ANY)],
        out_specs=[vmem()] * 2,
        scratch_shapes=[pltpu.SemaphoreType.DMA((2 * len(pieces),))],
        compiler_params=params(56),
        name="edges",
    )(core, obj)


def by_side(meta, near, wide):
    first = meta[CORE] == 0
    return jnp.where(first, wide, near), jnp.where(first, near, wide)


def pack(tile, left, right, c0):
    shape = (tile.shape[0], H)
    middle = (tile.shape[0], W - 2 * H)
    a = jnp.where(cols_below(shape, 0, c0), tile[:, W - H : W], left)
    b = jnp.where(cols_below(middle, H, c0), tile[:, W:], tile[:, : W - 2 * H])
    c = jnp.where(cols_below(shape, W - H, c0), right, tile[:, W - 2 * H : W - H])
    return a, b, c


def put(out, rows, pieces):
    a, b, c = pieces
    out[rows, :H] = a
    out[rows, H : W - H] = b
    out[rows, W - H :] = c


def mate_takes(meta):
    upper = (meta[PR0] < HALF).astype(jnp.int32)
    return upper + meta[ODD] == 1


def far_takes(meta):
    upper = (meta[FR0] < HALF).astype(jnp.int32)
    return upper + meta[ODD] != 1


def pack_edge(meta, out, s, obj, near, wide, last, c0):
    rows = pl.ds(pl.multiple_of(last * (T - H), H), H)
    ends = pl.ds(pl.multiple_of(last * H, H), H)
    for part in range(2):
        sides = by_side(meta, near[s, part, ends, :], wide[s, part, ends, :])
        put(out.at[part], slice(None), pack(obj[s, part, rows, :], *sides, c0))


def far_kernel(s, meta, obj, near, wide, out):
    pack_edge(meta, out, s, obj, near, wide, meta[ODD], meta[FC0])


def mate_kernel(s, meta, obj, near, wide, passing, out):
    own = mate_takes(meta)

    @pl.when(own)
    def _():
        pack_edge(meta, out, s, obj, near, wide, 1 - meta[ODD], meta[PC0])

    @pl.when(jnp.logical_not(own))
    def _():
        out[...] = passing[...]


def beside_rows(meta, s, part, first, near, wide, near_ends, wide_ends):
    if first in (0, T - B):
        rows = pl.ds(min(first, H), B)
        return by_side(meta, near_ends[s, part, rows, :], wide_ends[s, part, rows, :])
    rows = pl.ds(first - H, B)
    return by_side(meta, near[s, part, rows, :], wide[s, part, rows, :])


def local_kernel(s, meta, obj, near_ends, wide_ends, near, wide, out):
    r0, c0 = meta[R0], meta[C0]
    for part in range(2):

        def packed(first):
            rows = pl.ds(first, B)
            sides = beside_rows(meta, s, part, first, near, wide, near_ends, wide_ends)
            return pack(obj[s, part, rows, :], *sides, c0)

        put(out.at[part], pl.ds(0, B), packed(W - H))
        for first in range(B, W - B, B):
            low, high = packed(first - H), packed(first + W - H)
            put(
                out.at[part],
                pl.ds(first, B),
                [jnp.where(rows_below(x.shape, first, r0), y, x) for x, y in zip(low, high)],
            )
        put(out.at[part], pl.ds(W - B, B), packed(W - B - H))


def far_strip(s, *args):
    return whole(lambda *refs: far_kernel(s, *refs), "far_strip", [STRIP], *args)[0]


def mate_strip(s, *args):
    return whole(lambda *refs: mate_kernel(s, *refs), "mate_strip", [STRIP], *args)[0]


def local_window(s, *args):
    return whole(lambda *refs: local_kernel(s, *refs), "local_window", [WINDOW], *args)[0]


def window_rows(meta, local, strip, part, first):
    x = local[part, pl.ds(first, B), :]
    if first == 0:
        x = jnp.where(rows_below(x.shape, first, meta[R0]), x, strip[part])
    if first == W - B:
        x = jnp.where(rows_below(x.shape, first, meta[R0]), strip[part], x)
    return x


def put_left(v4, first, re, im, inverse):
    re, im = re.astype(BF16), im.astype(BF16)
    rows, later = pl.ds(first, B), pl.ds(W + first, B)
    v4[rows, :W] = re
    v4[rows, W:] = im
    v4[later, :W] = im if inverse else -im
    v4[later, W:] = -re if inverse else re


def left_product(table, v4, m4, inverse):
    for first in range(0, W, W):
        rows, later = pl.ds(first, W), pl.ds(W + first, W)
        mid = jnp.dot(table[rows, :], v4[...], preferred_element_type=F32).astype(BF16)
        re, im = mid[:, :W], mid[:, W:]
        m4[rows, :W] = re
        m4[rows, W:] = im if inverse else -im
        m4[later, :W] = im
        m4[later, W:] = -re if inverse else re


def right_product(m4, table, first):
    re = jnp.dot(m4[pl.ds(first, B), :], table[...], preferred_element_type=F32)
    im = jnp.dot(m4[pl.ds(W + first, B), :], table[...], preferred_element_type=F32)
    return re, im


def first_kernel(meta, local, strip, q, kern_re, kern_im, la, lai, rb, rbi, psi, v4, m4):
    for first in range(0, W, B):
        rows = pl.ds(first, B)
        o_re = window_rows(meta, local, strip, 0, first)
        o_im = window_rows(meta, local, strip, 1, first)
        q_re, q_im = q[0, rows, :], q[1, rows, :]
        put_left(v4, first, q_re * o_re - q_im * o_im, q_re * o_im + q_im * o_re, False)
    left_product(la, v4, m4, False)
    for first in range(0, W, B):
        rows = pl.ds(first, B)
        re, im = right_product(m4, rb, first)
        k_re, k_im = kern_re[rows, :], kern_im[rows, :]
        put_left(v4, first, re * k_re - im * k_im, re * k_im + im * k_re, True)
    left_product(lai, v4, m4, True)
    for first in range(0, W, B):
        rows = pl.ds(first, B)
        psi[0, rows, :], psi[1, rows, :] = right_product(m4, rbi, first)


def edge_rows(meta, g, zg):
    keep_first = meta[R0] < HALF
    live = meta[LIVE] > 0

    @pl.when(keep_first)
    def _():
        for part in range(2):
            x = g[part, :H, :]
            hide = rows_below(x.shape, 0, meta[R0])
            zg[part] = jnp.where(jnp.logical_and(live, jnp.logical_not(hide)), x, 0.0)

    @pl.when(jnp.logical_not(keep_first))
    def _():
        for part in range(2):
            x = g[part, W - H :, :]
            show = rows_below(x.shape, W - H, meta[R0])
            zg[part] = jnp.where(jnp.logical_and(live, show), x, 0.0)


def second_kernel(meta, local, strip, psi, amp, la, lai, rb, rbi, m4, zg, v4):
    for first in range(0, W, B):
        rows = pl.ds(first, B)
        o_re = window_rows(meta, local, strip, 0, first)
        o_im = window_rows(meta, local, strip, 1, first)
        p_re, p_im = psi[0, rows, :], psi[1, rows, :]
        put_left(v4, first, p_re * o_re - p_im * o_im, p_re * o_im + p_im * o_re, False)
    left_product(la, v4, m4, False)
    for first in range(0, W, B):
        rows = pl.ds(first, B)
        re, im = right_product(m4, rb, first)
        factor = 1.0 - amp[rows, :].astype(F32) / jnp.sqrt(re * re + im * im + 1.0)
        put_left(v4, first, re * factor, im * factor, True)
    left_product(lai, v4, m4, True)
    upper = meta[R0] < HALF
    first = pl.multiple_of(jnp.where(upper, 0, W - B), B)
    rows = pl.ds(first, B)
    re, im = right_product(m4, rbi, first)
    p_re, p_im = psi[0, rows, :], psi[1, rows, :]
    below = rows_below(re.shape, first, meta[R0]).astype(jnp.int32)
    leaves = jnp.logical_and(below + upper.astype(jnp.int32) == 1, meta[LIVE] > 0)
    zg[0] = jnp.where(leaves, p_re * re + p_im * im, 0.0)
    zg[1] = jnp.where(leaves, p_re * im - p_im * re, 0.0)


def third_kernel(meta, mid, local, strip, psi, q, kern_re, kern_im, la, lai, rb, rbi, g2, g1, zg, v4, m4):
    for first in range(0, W, B):
        rows = pl.ds(first, B)
        re, im = right_product(mid, rbi, first)
        p_re, p_im = psi[0, rows, :], psi[1, rows, :]
        g2[0, rows, :] = p_re * re + p_im * im
        g2[1, rows, :] = p_re * im - p_im * re
        o_re = window_rows(meta, local, strip, 0, first)
        o_im = window_rows(meta, local, strip, 1, first)
        put_left(v4, first, o_re * re + o_im * im, o_re * im - o_im * re, False)
    left_product(la, v4, m4, False)
    for first in range(0, W, B):
        rows = pl.ds(first, B)
        re, im = right_product(m4, rb, first)
        k_re, k_im = kern_re[rows, :], kern_im[rows, :]
        put_left(v4, first, re * k_re + im * k_im, im * k_re - re * k_im, True)
    left_product(lai, v4, m4, True)
    for first in range(0, W, B):
        rows = pl.ds(first, B)
        re, im = right_product(m4, rbi, first)
        q_re, q_im = q[0, rows, :], q[1, rows, :]
        g1[0, rows, :] = q_re * re + q_im * im
        g1[1, rows, :] = q_re * im - q_im * re
    edge_rows(meta, g1, zg)


def transforms(kernel, name, out_shape, meta, *operands, scratch=2):
    return pl.pallas_call(
        kernel,
        out_shape=out_shape,
        in_specs=[smem()] + [vmem()] * len(operands),
        out_specs=[vmem()] * len(out_shape),
        scratch_shapes=[pltpu.VMEM((2 * W, 2 * W), BF16)] * scratch,
        compiler_params=params(16),
        name=name,
    )(meta, *operands)


def shares(meta, part, mate, far):
    odd = meta[ODD] > 0
    mate = jnp.where(mate_takes(meta), mate[part], 0.0)
    far = jnp.where(far_takes(meta), far[part], 0.0)
    top = jnp.where(odd, mate, far)
    bottom = jnp.where(odd, far, mate)
    c_top = jnp.where(odd, meta[PC0], meta[FC0])
    c_bottom = jnp.where(odd, meta[FC0], meta[PC0])
    return (top, c_top), (bottom, c_bottom)


def left_part(x, c0):
    x = x[:, :H]
    return jnp.where(cols_below(x.shape, 0, c0), 0.0, x)


def right_part(x, c0):
    x = x[:, W - H :]
    return jnp.where(cols_below(x.shape, W - H, c0), x, 0.0)


def inner_parts(x, c0):
    low, high = x[:, H:], x[:, : W - H]
    low = jnp.where(cols_below(low.shape, H, c0), 0.0, low)
    high = jnp.where(cols_below(high.shape, 0, c0), high, 0.0)
    return low, high


def tile_rows(meta, g, part, first):
    live = meta[LIVE] > 0
    if first < W - H:
        x = g[part, pl.ds(first + H, B), :]
        hide = rows_below(x.shape, first + H, meta[R0])
        return jnp.where(jnp.logical_and(live, jnp.logical_not(hide)), x, 0.0)
    x = g[part, pl.ds(first - (W - H), B), :]
    show = rows_below(x.shape, first - (W - H), meta[R0])
    return jnp.where(jnp.logical_and(live, show), x, 0.0)


def middle_kernel(meta, g1, g2, near, wide):
    for s, g in enumerate((g1, g2)):
        for part in range(2):
            for first in range(B, T - B, B):
                x = tile_rows(meta, g, part, first)
                x = by_side(meta, left_part(x, meta[C0]), right_part(x, meta[C0]))
                rows = pl.ds(first - H, B)
                near[s, part, rows, :], wide[s, part, rows, :] = x


def corner_kernel(meta, g, mate, far, near, wide):
    for part in range(2):
        for first, (strip, c0) in zip((0, T - H), shares(meta, part, mate, far)):
            x = tile_rows(meta, g, part, first)
            a = left_part(x, meta[C0]) + left_part(strip, c0)
            b = right_part(x, meta[C0]) + right_part(strip, c0)
            rows = pl.ds(min(first, H), B)
            near[part, rows, :], wide[part, rows, :] = by_side(meta, a, b)


def own_rows(meta, g, part, first, mate, far):
    low, high = inner_parts(tile_rows(meta, g, part, first), meta[C0])
    if first in (0, T - B):
        top, bottom = shares(meta, part, mate, far)
        more = inner_parts(*(top if first == 0 else bottom))
        low, high = low + more[0], high + more[1]
    return low, high


def inner_kernel(s, meta, step, obj, g, mate, far, *rest):
    out, tile, sems = rest[-3:]
    size = step[s]
    copies = []
    for part in range(2):
        for first in range(0, T, B):
            rows = pl.ds(first, B)
            low, high = own_rows(meta, g, part, first, mate, far)
            tile[part, rows, : W - 2 * H] = obj[s, part, rows, H : W - H] - size * low[:, H:]
            tile[part, rows, W - 2 * H :] = obj[s, part, rows, W - H : T - H] - size * high[:, : W - 2 * H]
            target = out.at[s, part, rows, pl.ds(H, T - 2 * H)]
            copies.append(pltpu.make_async_copy(tile.at[part, rows, :], target, sems.at[part, first // B]))
            copies[-1].start()
    for copy in copies:
        copy.wait()


def border_kernel(s, meta, step, obj, g, mate, far, near, wide, near_ends, wide_ends, before, out, tile, sems):
    size = step[s]
    copies = []
    for part in range(2):
        for first in range(0, T, B):
            rows = pl.ds(first, B)
            low, high = own_rows(meta, g, part, first, mate, far)
            if first in (0, T - B):
                ends = pl.ds(min(first, H), B)
                received = by_side(meta, near_ends[part, ends, :], wide_ends[part, ends, :])
            else:
                received = beside_rows(meta, s, part, first, near, wide, None, None)
            for side, x in enumerate((low[:, :H], high[:, W - 2 * H :])):
                cols = pl.ds(side * (T - H), H)
                tile[side, part, rows, :] = obj[s, part, rows, cols] - size * (x + received[side])
        for side in range(2):
            target = out.at[s, part, :, pl.ds(side * (T - H), H)]
            copies.append(pltpu.make_async_copy(tile.at[side, part], target, sems.at[part, side]))
            copies[-1].start()
    for copy in copies:
        copy.wait()


def update(kernel, name, tile, sems, before, meta, step, obj, *operands):
    hbm = pl.BlockSpec(memory_space=pl.ANY)
    return pl.pallas_call(
        kernel,
        out_shape=jax.ShapeDtypeStruct(obj.shape, F32),
        in_specs=[smem()] * 2 + [vmem()] * (1 + len(operands)) + [hbm] * len(before),
        out_specs=hbm,
        scratch_shapes=[pltpu.VMEM(tile, F32), pltpu.SemaphoreType.DMA(sems)],
        input_output_aliases={3 + len(operands): 0} if before else {},
        compiler_params=params(16),
        name=name,
    )(meta, step, obj, *operands, *before)


def inner(s, before, *operands):
    kernel = lambda *refs: inner_kernel(s, *refs)
    return (update(kernel, "inner", (2, T, T - 2 * H), (2, T // B), before, *operands),)


def border(s, before, *operands):
    kernel = lambda *refs: border_kernel(s, *refs)
    return (update(kernel, "border", (2, 2, T, H), (2, 2), before, *operands),)


def per_device(object_tiles, probe, prop_phase, amplitudes, offsets, counts, step_size):
    n_rows, n_cols = lax.axis_size("rows"), lax.axis_size("cols")
    at_chip = [(i, i ^ 1) for i in range(n_cols) if i ^ 1 < n_cols]
    past_chip = [(i, i + 1) for i in range(1, n_cols - 1, 2)]
    past_chip = past_chip + [(j, i) for i, j in past_chip]
    mates = [(i, i ^ 1) for i in range(n_rows) if i ^ 1 < n_rows]
    fars = [(i, i + 1) for i in range(1, n_rows - 1, 2)]
    fars = fars + [(j, i) for i, j in fars]
    inward = [(i, i - 2) for i in range(2, n_rows, 2)] + [(i, i + 2) for i in range(1, n_rows - 2, 2)]
    outward = [(j, i) for i, j in inward]

    own = offsets.reshape(2)
    parity = lambda axis: lax.axis_index(axis).astype(jnp.int32).reshape(1) & 1
    odd, core = parity("rows"), parity("cols")
    after = lambda *values: lax.optimization_barrier(values)

    far, passing, strip, local = [[None, None] for _ in range(4)]

    def beside_cols(near, wide):
        wide = lax.ppermute(wide, "cols", past_chip)
        return lax.ppermute(near, "cols", at_chip), wide

    pieces = [(0, pl.ds(0, H)), (T - H, pl.ds(H, H))]
    first, obj, count, odd, *sent = after(
        own, object_tiles, counts.reshape(1), odd, *edges(ENDS, pieces, core, object_tiles)
    )
    beside = [lax.ppermute(first, "rows", mates), lax.ppermute(first, "rows", fars)]
    ends = beside_cols(*sent)
    first, *sent = after(first, *edges(MIDDLE, [(H, pl.ds(0, T - 2 * H))], core, obj))
    middle_wide = lax.ppermute(sent[1], "cols", past_chip)
    kernel = whole(phase_kernel, "phase", [PLANE, PLANE], first, prop_phase, object_tiles)
    first, *kernel = after(first, *kernel)
    meta = scalars(first, *beside, count, odd, core)
    middle_near, _ = after(sent[0], meta)
    middle = lax.ppermute(middle_near, "cols", at_chip), middle_wide

    la, rb, q = whole(forward_kernel, "forward_tables", [LEFT, RIGHT, WINDOW], meta, probe)
    *ends, la, rb, q = after(*ends, la, rb, q)

    for s in range(2):
        far[s] = far_strip(s, meta, object_tiles, *ends)
        passing[s] = lax.ppermute(far[s], "rows", inward)
    third, _ = after(meta, far[1])
    lai, rbi = whole(inverse_kernel, "inverse_tables", [LEFT, RIGHT], third)
    passing[0], la, rb, q, lai, rbi, *middle = after(passing[0], la, rb, q, lai, rbi, *middle)
    strip[0] = lax.ppermute(mate_strip(0, meta, object_tiles, *ends, passing[0]), "rows", mates)
    local[0] = local_window(0, meta, object_tiles, *ends, *middle)
    local[1] = local_window(1, meta, object_tiles, *ends, *middle)
    strip[1] = lax.ppermute(mate_strip(1, meta, object_tiles, *ends, passing[1]), "rows", mates)
    tables = (la, lai, rb, rbi)

    (psi,) = transforms(first_kernel, "first", [WINDOW], meta, local[0], strip[0], q, *kernel, *tables)
    mid, z2 = transforms(
        second_kernel,
        "second",
        [jax.ShapeDtypeStruct((2 * W, 2 * W), BF16), STRIP],
        meta,
        local[1],
        strip[1],
        psi,
        amplitudes[0, 0, 0],
        *tables,
        scratch=1,
    )
    g2, g1, z1 = transforms(
        third_kernel, "third", [WINDOW, WINDOW, STRIP], meta, mid, local[1], strip[1], psi, q, *kernel, *tables
    )

    mate, far, ends = [None, None], [None, None], [None, None]
    mate[1] = lax.ppermute(z2, "rows", mates)
    mate[0] = lax.ppermute(z1, "rows", mates)
    far[1] = lax.ppermute(mate[1], "rows", outward)
    _, *sent = after(mate[1], *whole(middle_kernel, "middle", [MIDDLE] * 2, meta, g1, g2))
    middle = beside_cols(*sent)
    far[0] = lax.ppermute(mate[0], "rows", outward)
    grads = (g1, g2)
    out = ()
    for s in (1, 0):
        shape = jax.ShapeDtypeStruct(ENDS.shape[1:], F32)
        sent = whole(corner_kernel, "corner", [shape] * 2, meta, grads[s], mate[s], far[s])
        ends[s] = beside_cols(*sent)
    for s in (1, 0):
        out = inner(s, out, meta, step_size, object_tiles, grads[s], mate[s], far[s])
    for s in (1, 0):
        out = border(s, out, meta, step_size, object_tiles, grads[s], mate[s], far[s], *middle, *ends[s])
    return out[0]


def solution(mesh):
    return jax.shard_map(
        per_device,
        mesh=mesh,
        in_specs=(
            P(None, None, "rows", "cols"),
            P(),
            P(),
            P("rows", "cols", None, None, None),
            P("rows", "cols", None, None),
            P("rows", "cols"),
            P(),
        ),
        out_specs=P(None, None, "rows", "cols"),
        check_vma=False,
    )
```
